32 devices in a mesh: dp: 4 (over y, x), fsdp: 8 (over z, core).
Axes of the slice: x: 2, y: 2, z: 4, core: 2. Of those that a mesh axis runs over, the one named last changes fastest.
Arguments:
- scenes_in: bfloat16 [32, 256, 1024], P(('dp', 'fsdp')), may hold values from -6 to 6
- scene_lengths: int32 [32], P(('dp', 'fsdp')), may hold values from 128 to 256, as said below
- cotangent: bfloat16 [32, 256, 1024], P(('dp', 'fsdp')), may hold values from -6 to 6
- qkv_weight: bfloat16 [1024, 3072], P('fsdp'), may hold values from -0.1875 to 0.1875
- out_weight: bfloat16 [1024, 1024], P('fsdp'), may hold values from -0.75 to 0.75
- up_weight: bfloat16 [1024, 4096], P('fsdp'), may hold values from -0.1875 to 0.1875
- down_weight: bfloat16 [4096, 1024], P('fsdp'), may hold values from -0.125 to 0.125
- gain_one: bfloat16 [1024], P('fsdp'), may hold values from 0.5 to 1.5
- bias_one: bfloat16 [1024], P('fsdp'), may hold values from -2 to 2
- gain_two: bfloat16 [1024], P('fsdp'), may hold values from 0.5 to 1.5
- bias_two: bfloat16 [1024], P('fsdp'), may hold values from -2 to 2
Outputs:
- layer_out: bfloat16 [32, 256, 1024], P(('dp', 'fsdp'))
- input_grad: bfloat16 [32, 256, 1024], P(('dp', 'fsdp'))
- qkv_grad: float32 [1024, 3072], P('fsdp')
- out_grad: float32 [1024, 1024], P('fsdp')
- up_grad: float32 [1024, 4096], P('fsdp')
- down_grad: float32 [4096, 1024], P('fsdp')
- gain_one_grad: float32 [1024], P('fsdp')
- bias_one_grad: float32 [1024], P('fsdp')
- gain_two_grad: float32 [1024], P('fsdp')
- bias_two_grad: float32 [1024], P('fsdp')
The draws below stay inside these ranges and needn't reach their ends.
Inputs may be any that keep to these rules, and one draw needn't show every extreme that they name: `scene_lengths`: each length is a multiple of 128; some scene has exactly 256 tokens.
All inputs are finite; a program needn't handle non-finite values.
Results may differ from the reference program's by a relative error of at most 0.017.
Values may be sent and summed in bfloat16 or wider, within the bound.
A program may use at most 192 MiB of HBM per device.

```python
import math
import jax
import jax.numpy as jnp
from jax import lax

D = 1024
HEADS = 16
HEAD_DIM = 64
FF = 4096
SEQ = 256
UNIT = 128
SCENES = 32


def draw_scene_lengths(key, part):
    unit_count = SEQ // UNIT
    first_key = jax.random.fold_in(key, 11)
    second_key = jax.random.fold_in(key, 12)
    counts_drawn = jax.random.randint(first_key, (SCENES,), 1, unit_count + 1)
    longest = jax.random.randint(second_key, (), 0, SCENES)
    counts_drawn = counts_drawn.at[longest].set(unit_count)
    return (counts_drawn * UNIT).astype(jnp.int32)


def level_of(rng, extent, pieces, least, largest):
    factor_of, own = 1.0, jax.random.fold_in(rng, 6)
    for dim, blocks in pieces:
        heights = jnp.exp(jax.random.uniform(jax.random.fold_in(own, dim), (blocks,), jnp.float32, least / len(pieces), largest / len(pieces)))
        factor_of = factor_of * jnp.repeat(heights, extent[dim] // blocks).reshape([-1 if axis == dim else 1 for axis in range(len(extent))])
    return factor_of


def centred(own_key, shape, width, limit, split=(), kind=jnp.bfloat16):
    gain = level_of(own_key, shape, split, -0.22, 0.18) if split else 1.0
    entries = jax.random.normal(own_key, shape, jnp.float32) * width * gain
    return jnp.minimum(jnp.maximum(entries, -limit), limit).astype(kind)


def setup_inputs(seed: int = 0) -> dict:
    key_list = jax.random.split(jax.random.key(seed), 12)
    scenes_in = centred(key_list[0], (SCENES, SEQ, D), 1.0, 6.0, ((0, 32),))
    scene_lengths = draw_scene_lengths(jax.random.fold_in(key_list[11], 71), 0)
    cotangent = centred(key_list[2], (SCENES, SEQ, D), 1.0, 6.0, ((0, 32),))
    qkv_weight = centred(key_list[3], (D, 3 * D), D ** -0.5, 0.1875, ((0, 8),))
    out_weight = centred(key_list[4], (D, D), (D // 16) ** -0.5, 0.75, ((0, 8),))
    up_weight = centred(key_list[5], (D, FF), D ** -0.5, 0.1875, ((0, 8),))
    down_weight = centred(key_list[6], (FF, D), (FF // 2) ** -0.5, 0.125, ((0, 8),))
    gain_one = jnp.clip(1.0 + 0.1 * jax.random.normal(key_list[7], (D,), jnp.float32), 0.5, 1.5).astype(jnp.bfloat16)
    bias_one = centred(key_list[8], (D,), 0.3, 2.0, ((0, 8),))
    gain_two = jnp.clip(1.0 + 0.1 * jax.random.normal(key_list[9], (D,), jnp.float32), 0.5, 1.5).astype(jnp.bfloat16)
    bias_two = centred(key_list[10], (D,), 0.3, 2.0, ((0, 8),))
    return dict(scenes_in=scenes_in, scene_lengths=scene_lengths, cotangent=cotangent, qkv_weight=qkv_weight, out_weight=out_weight, up_weight=up_weight, down_weight=down_weight, gain_one=gain_one, bias_one=bias_one, gain_two=gain_two, bias_two=bias_two)


@jax.custom_vjp
def low(v):
    return lax.optimization_barrier(v.astype(jnp.bfloat16)).astype(jnp.float32)

@jax.custom_vjp
def low_back(v):
    return v

def low_keep(v):
    return (low(v), None)

def low_pass(kept, grad):
    return (grad,)

def back_keep(v):
    return (v, None)

def back_low(kept, grad):
    return (low(grad),)
low.defvjp(low_keep, low_pass)
low_back.defvjp(back_keep, back_low)
epsilon = 1e-05

def normalize(values_in):
    row_mean = lax.optimization_barrier(jnp.mean(values_in, axis=-1, keepdims=True))
    centered = values_in - row_mean
    variance = lax.optimization_barrier(jnp.mean(centered * centered, axis=-1, keepdims=True))
    return centered * lax.rsqrt(variance + epsilon)

def matmul_high(left, right):
    return jnp.matmul(left, right, precision=lax.Precision.HIGHEST)

def layer(inputs, valid_rows, valid_keys, qkv_weight, out_weight, up_weight, down_weight, gain_one, bias_one, gain_two, bias_two):
    group_size = inputs.shape[0]
    seq_len = inputs.shape[1]
    hidden_one = low(normalize(inputs) * gain_one + bias_one)
    qkv_all = low(low_back(matmul_high(hidden_one, qkv_weight)))
    split_view = qkv_all.reshape(group_size, seq_len, 3, HEADS, HEAD_DIM)
    queries = split_view[:, :, 0]
    keys_all = split_view[:, :, 1]
    values_all = split_view[:, :, 2]
    scale_factor = 1.0 / math.sqrt(HEAD_DIM)
    scores = low_back(jnp.einsum('gqhd,gkhd->ghqk', queries, keys_all, precision=lax.Precision.HIGHEST) * scale_factor)
    masked = jnp.where(valid_keys[:, None, None, :], scores, -1e+30)
    probs = jax.nn.softmax(masked, axis=-1)
    probs_low = low(probs)
    attended = jnp.einsum('ghqk,gkhd->gqhd', probs_low, values_all, precision=lax.Precision.HIGHEST)
    attn_flat = low(low_back(attended.reshape(group_size, seq_len, D)))
    resid_one = inputs + low_back(matmul_high(attn_flat, out_weight))
    hidden_two = low(normalize(resid_one) * gain_two + bias_two)
    hidden_pre = low_back(matmul_high(hidden_two, up_weight))
    activated = low(jax.nn.gelu(hidden_pre, approximate=False))
    result = resid_one + low_back(matmul_high(activated, down_weight))
    return result * valid_rows[..., None]

def reference(scenes_in, scene_lengths, cotangent, qkv_weight, out_weight, up_weight, down_weight, gain_one, bias_one, gain_two, bias_two):
    group_size = math.gcd(SCENES, max(1, 4096 // SEQ))
    group_count = SCENES // group_size
    weights = tuple((matrix.astype(jnp.float32) for matrix in (qkv_weight, out_weight, up_weight, down_weight, gain_one, bias_one, gain_two, bias_two)))
    positions = jnp.arange(SEQ, dtype=jnp.int32)

    def one_group(totals, slab_in):
        inputs, lengths_here, cot_here = slab_in
        valid_keys = positions[None, :] < lengths_here[:, None]
        valid_rows = valid_keys.astype(jnp.float32)

        def forward(inputs_float, *params):
            return layer(inputs_float, valid_rows, valid_keys, *params)
        output, pullback = jax.vjp(forward, inputs.astype(jnp.float32), *weights)
        gradients = pullback(cot_here.astype(jnp.float32))
        totals = tuple((total + grad_part for total, grad_part in zip(totals, gradients[1:])))
        return (totals, (output.astype(jnp.bfloat16), gradients[0].astype(jnp.bfloat16)))
    initial = tuple((jnp.zeros(matrix.shape, jnp.float32) for matrix in weights))
    slabs = (scenes_in.reshape(group_count, group_size, SEQ, D), scene_lengths.reshape(group_count, group_size), cotangent.reshape(group_count, group_size, SEQ, D))
    totals, (outputs, input_grads) = lax.scan(one_group, initial, slabs)
    return (outputs.reshape(SCENES, SEQ, D), input_grads.reshape(SCENES, SEQ, D), totals[0], totals[1], totals[2], totals[3], totals[4], totals[5], totals[6], totals[7])
```

```python
import functools
import math

import jax
import jax.numpy as jnp
from jax import lax
from jax.experimental import pallas as pl
from jax.experimental.pallas import tpu as pltpu
from jax.sharding import PartitionSpec as P

D = 1024
HEADS = 16
HEAD_DIM = 64


epsilon = 1e-05


def norm_rows(values_in):
    row_mean = jnp.mean(values_in, axis=-1, keepdims=True)
    centered = values_in - row_mean
    variance = jnp.mean(centered * centered, axis=-1, keepdims=True)
    inverse = lax.rsqrt(variance + epsilon)
    return (centered * inverse, inverse)


def norm_back(grad_normed, normed, inverse):
    first_mean = jnp.mean(grad_normed, axis=-1, keepdims=True)
    second_mean = jnp.mean(grad_normed * normed, axis=-1, keepdims=True)
    return inverse * (grad_normed - first_mean - normed * second_mean)


def inner_rows(left, right):
    return lax.dot_general(
        left, right, (((0,), (0,)), ((), ())), preferred_element_type=jnp.float32
    )


def outer_cols(left, right):
    return lax.dot_general(
        left, right, (((1,), (1,)), ((), ())), preferred_element_type=jnp.float32
    )


def forward_pass(inputs, key_valid, params):
    qkv_weight, out_weight, up_weight, down_weight, gain_one, bias_one, gain_two, bias_two = params
    seq_len = inputs.shape[0]
    normed_one, inverse_one = norm_rows(inputs)
    hidden_one = (normed_one * gain_one.astype(jnp.float32) + bias_one.astype(jnp.float32)).astype(
        jnp.bfloat16
    )
    qkv_low = jnp.dot(hidden_one, qkv_weight, preferred_element_type=jnp.float32).astype(
        jnp.bfloat16
    )
    split_view = qkv_low.reshape(seq_len, 3, HEADS, HEAD_DIM)
    queries = split_view[:, 0]
    keys_all = split_view[:, 1]
    values_all = split_view[:, 2]
    scale_factor = 1.0 / math.sqrt(HEAD_DIM)
    scores = (
        jnp.einsum("qhd,khd->hqk", queries, keys_all, preferred_element_type=jnp.float32)
        * scale_factor
    )
    masked = jnp.where(key_valid[None, None, :], scores, -1e30)
    highest = jnp.max(masked, axis=-1, keepdims=True)
    expont = jnp.exp(masked - highest)
    probs = expont / jnp.sum(expont, axis=-1, keepdims=True)
    probs_low = probs.astype(jnp.bfloat16)
    attended = jnp.einsum("hqk,khd->qhd", probs_low, values_all, preferred_element_type=jnp.float32)
    attn_low = attended.reshape(seq_len, D).astype(jnp.bfloat16)
    resid_one = inputs + jnp.dot(attn_low, out_weight, preferred_element_type=jnp.float32)
    normed_two, inverse_two = norm_rows(resid_one)
    hidden_two = (normed_two * gain_two.astype(jnp.float32) + bias_two.astype(jnp.float32)).astype(
        jnp.bfloat16
    )
    hidden_pre = jnp.dot(hidden_two, up_weight, preferred_element_type=jnp.float32)
    activated = jax.nn.gelu(hidden_pre, approximate=False).astype(jnp.bfloat16)
    result = resid_one + jnp.dot(activated, down_weight, preferred_element_type=jnp.float32)
    return (
        result,
        normed_one,
        inverse_one,
        hidden_one,
        queries,
        keys_all,
        values_all,
        probs,
        probs_low,
        attn_low,
        normed_two,
        inverse_two,
        hidden_two,
        hidden_pre,
        activated,
    )


def mlp_back(grad_out, saved, params):
    up_weight, down_weight, gain_two = (params[2], params[3], params[6])
    normed_two, inverse_two, hidden_two, hidden_pre, activated = (
        saved[10],
        saved[11],
        saved[12],
        saved[13],
        saved[14],
    )
    grad_low = grad_out.astype(jnp.bfloat16)
    down_grad = inner_rows(activated, grad_low)
    grad_act = outer_cols(grad_low, down_weight)
    cumul = 0.5 * (1.0 + lax.erf(hidden_pre * (1.0 / math.sqrt(2.0))))
    density = jnp.exp(-0.5 * hidden_pre * hidden_pre) * (1.0 / math.sqrt(2.0 * math.pi))
    grad_pre = (grad_act * (cumul + hidden_pre * density)).astype(jnp.bfloat16)
    up_grad = inner_rows(hidden_two, grad_pre)
    grad_hidden = outer_cols(grad_pre, up_weight)
    gain_two_grad = jnp.sum(grad_hidden * normed_two, axis=0)
    bias_two_grad = jnp.sum(grad_hidden, axis=0)
    grad_resid = grad_out + norm_back(
        grad_hidden * gain_two.astype(jnp.float32), normed_two, inverse_two
    )
    return (grad_resid, up_grad, down_grad, gain_two_grad, bias_two_grad)


def attn_back(grad_resid, saved, params):
    qkv_weight, out_weight, gain_one = (params[0], params[1], params[4])
    normed_one, inverse_one, hidden_one = (saved[1], saved[2], saved[3])
    queries, keys_all, values_all, probs, probs_low, attn_low = (
        saved[4],
        saved[5],
        saved[6],
        saved[7],
        saved[8],
        saved[9],
    )
    seq_len = grad_resid.shape[0]
    scale_factor = 1.0 / math.sqrt(HEAD_DIM)
    resid_low = grad_resid.astype(jnp.bfloat16)
    out_grad = inner_rows(attn_low, resid_low)
    grad_attn = (
        outer_cols(resid_low, out_weight).astype(jnp.bfloat16).reshape(seq_len, HEADS, HEAD_DIM)
    )
    grad_probs = jnp.einsum(
        "qhd,khd->hqk", grad_attn, values_all, preferred_element_type=jnp.float32
    )
    row_dot = jnp.sum(probs * grad_probs, axis=-1, keepdims=True)
    grad_scores = (probs * (grad_probs - row_dot)).astype(jnp.bfloat16)
    grad_values = jnp.einsum(
        "hqk,qhd->khd", probs_low, grad_attn, preferred_element_type=jnp.float32
    )
    grad_queries = (
        jnp.einsum("hqk,khd->qhd", grad_scores, keys_all, preferred_element_type=jnp.float32)
        * scale_factor
    )
    grad_keys = (
        jnp.einsum("hqk,qhd->khd", grad_scores, queries, preferred_element_type=jnp.float32)
        * scale_factor
    )
    grad_qkv = (
        jnp.stack([grad_queries, grad_keys, grad_values], axis=1)
        .reshape(seq_len, 3 * D)
        .astype(jnp.bfloat16)
    )
    qkv_grad = inner_rows(hidden_one, grad_qkv)
    grad_hidden = outer_cols(grad_qkv, qkv_weight)
    gain_one_grad = jnp.sum(grad_hidden * normed_one, axis=0)
    bias_one_grad = jnp.sum(grad_hidden, axis=0)
    input_grad = grad_resid + norm_back(
        grad_hidden * gain_one.astype(jnp.float32), normed_one, inverse_one
    )
    return (input_grad, qkv_grad, out_grad, gain_one_grad, bias_one_grad)


MESH_ID = pl.DeviceIdType.MESH


def aligned(index, size):
    return pl.ds(pl.multiple_of(index * size, size), size)


def greet(dp_index, fsdp_index, fsdp_size):
    barrier = pltpu.get_barrier_semaphore()
    peers = [(dp_index ^ 1, fsdp_index), (dp_index ^ 2, fsdp_index), (dp_index ^ 3, fsdp_index)]
    peers += [(dp_index, lax.rem(fsdp_index + k, fsdp_size)) for k in range(1, fsdp_size)]
    for peer in peers:
        pl.semaphore_signal(barrier, inc=1, device_id=peer, device_id_type=MESH_ID)
    pl.semaphore_wait(barrier, len(peers))


def send(src, dst, send_sem, recv_sem, device):
    return pltpu.make_async_remote_copy(
        src_ref=src,
        dst_ref=dst,
        send_sem=send_sem,
        recv_sem=recv_sem,
        device_id=device,
        device_id_type=MESH_ID,
    )


def gather_kernel(fsdp_size, pieces, *refs):
    shards = refs[:pieces]
    small = refs[pieces]
    fulls = refs[pieces + 1 : 2 * pieces + 1]
    small_full = refs[2 * pieces + 1]
    own_sem, zs, zr, xs, xr, ys, yr, ds, dr, es, er, cs, cr, ss, sr = refs[2 * pieces + 2 :]
    column = fsdp_size // 2
    d = lax.axis_index("dp")
    f = lax.axis_index("fsdp")
    core = lax.rem(f, 2)
    place = lax.div(f, 2)
    x_peer, y_peer, c_peer = (d ^ 1, f), (d ^ 2, f), (d, f ^ 1)
    greet(d, f, fsdp_size)

    def block(piece, place_from, quarter, half=None):
        rows = shards[piece].shape[0]
        wide = shards[piece].shape[1] // 4
        row_part = aligned(place_from * 2 + core, rows)
        if half is None:
            return fulls[piece].at[row_part, aligned(quarter, wide)]
        return fulls[piece].at[row_part, aligned(quarter * 2 + half, wide // 2)]

    pending = []

    def go(copy):
        copy.start()
        pending.append(copy)

    def to_partner(piece, view):
        send(view, view, cs.at[piece], cr.at[piece], c_peer).start()

    small_rows = small.shape[0]
    for k in range(1, fsdp_size):
        go(
            send(
                small,
                small_full.at[aligned(f, small_rows)],
                ss.at[k - 1],
                sr.at[k - 1],
                (d, lax.rem(f + k, fsdp_size)),
            )
        )
    local = []
    for piece in range(pieces):
        rows = shards[piece].shape[0]
        wide = shards[piece].shape[1] // 4
        for k in range(1, column):
            go(
                send(
                    shards[piece].at[:, aligned(d, wide)],
                    block(piece, place, d),
                    zs.at[piece, k - 1],
                    zr.at[piece, k - 1],
                    (d, lax.rem(place + k, column) * 2 + core),
                )
            )
        own = fulls[piece].at[aligned(f, rows)]
        send(shards[piece], own, cs.at[piece], cr.at[piece], c_peer).start()
        copy = pltpu.make_async_copy(shards[piece], own, own_sem.at[piece])
        copy.start()
        local.append(copy)
    copy = pltpu.make_async_copy(small, small_full.at[aligned(f, small_rows)], own_sem.at[pieces])
    copy.start()
    local.append(copy)

    def source(k):
        return lax.rem(place - k + column, column)

    def arrived(view, send_sem, recv_sem, device):
        send(view, view, send_sem, recv_sem, device).wait_recv()

    for step in range(pieces + 2):
        piece = step
        if piece < pieces:
            for k in range(1, column):
                at = (piece, k - 1)
                view = block(piece, source(k), d)
                arrived(view, zs.at[at], zr.at[at], x_peer)
                go(send(view, view, xs.at[at], xr.at[at], x_peer))
                go(send(view, view, ys.at[at], yr.at[at], y_peer))
                to_partner(piece, view)
        piece = step - 1
        if 0 <= piece < pieces:
            for k in range(1, column):
                at = (piece, k - 1)
                view = block(piece, source(k), d ^ 1)
                arrived(view, xs.at[at], xr.at[at], x_peer)
                part = block(piece, source(k), d ^ 1, 0)
                go(send(part, part, ds.at[at], dr.at[at], y_peer))
                to_partner(piece, view)
                view = block(piece, source(k), d ^ 2)
                arrived(view, ys.at[at], yr.at[at], y_peer)
                part = block(piece, source(k), d ^ 2, 1)
                go(send(part, part, es.at[at], er.at[at], x_peer))
                to_partner(piece, view)
        piece = step - 2
        if 0 <= piece < pieces:
            for k in range(1, column):
                at = (piece, k - 1)
                for half, (a, b, peer) in enumerate(((ds, dr, y_peer), (es, er, x_peer))):
                    part = block(piece, source(k), d ^ 3, half)
                    arrived(part, a.at[at], b.at[at], peer)
                    to_partner(piece, part)
    for copy in pending:
        copy.wait_send()
    for k in range(1, fsdp_size):
        view = small_full.at[aligned(lax.rem(f - k + fsdp_size, fsdp_size), small_rows)]
        arrived(view, ss.at[k - 1], sr.at[k - 1], c_peer)
    for copy in local:
        copy.wait()
    for piece in range(pieces):
        rows = shards[piece].shape[0] * column
        view = fulls[piece].at[pl.ds(0, rows)]
        send(view, view, cs.at[piece], cr.at[piece], c_peer).wait()


def gather_weights(fsdp_size, shards, small):
    pieces = len(shards)
    hops = fsdp_size // 2 - 1
    hbm = pl.BlockSpec(memory_space=pltpu.HBM)
    dma = pltpu.SemaphoreType.DMA
    return pl.pallas_call(
        functools.partial(gather_kernel, fsdp_size, pieces),
        out_shape=[
            jax.ShapeDtypeStruct((a.shape[0] * fsdp_size, a.shape[1]), a.dtype)
            for a in (*shards, small)
        ],
        in_specs=[hbm] * (pieces + 1),
        out_specs=[hbm] * (pieces + 1),
        scratch_shapes=[dma((pieces + 1,))]
        + [dma((pieces, hops))] * 10
        + [dma((pieces,))] * 2
        + [dma((fsdp_size - 1,))] * 2,
        compiler_params=pltpu.CompilerParams(collective_id=0, has_side_effects=True),
        name="gather_weights",
    )(*shards, small)


def chunk_list(shapes):
    chunks = []
    for piece, (_, _, rows, wide) in enumerate(shapes):
        count = max(1, rows * wide // 262144)
        for part in range(count):
            chunks.append((piece, part * (rows // count), rows // count, wide))
    return chunks


def reduce_kernel(fsdp_size, chunks, pieces, *refs):
    grads = refs[:pieces]
    small = refs[pieces]
    outs = refs[pieces + 1 : 2 * pieces + 1]
    small_out = refs[2 * pieces + 1]
    rest = refs[2 * pieces + 2 :]
    count = len(chunks)
    groups = [rest[i * count : (i + 1) * count] for i in range(8)]
    own_b, core_b, sum_b, one_b, two_b, zed_b, fin_b = groups[:7]
    rest = rest[7 * count :]
    small_a, small_b = rest[:2]
    (own_sem, cs, cr, os_, or_, ts, tr, zs, zr, fs, fr, gs, gr, out_sem, ss, sr, us, ur) = rest[2:]
    column = fsdp_size // 2
    d = lax.axis_index("dp")
    f = lax.axis_index("fsdp")
    core = lax.rem(f, 2)
    place = lax.div(f, 2)
    bits = (lax.rem(d, 2), lax.div(d, 2))
    peers = ((d ^ 1, f), (d ^ 2, f))
    c_peer = (d, f ^ 1)
    greet(d, f, fsdp_size)
    pending = []

    def go(copy):
        copy.start()
        pending.append(copy)

    def arrived(view, send_sem, recv_sem, device):
        send(view, view, send_sem, recv_sem, device).wait_recv()

    for k in range(1, fsdp_size):
        to = lax.rem(f + k, fsdp_size)
        go(send(small.at[to], small_a.at[k - 1], ss.at[k - 1], sr.at[k - 1], (d, to)))
    for i, (piece, row, rows, wide) in enumerate(chunks):
        part = pl.ds(row, rows)
        go(send(grads[piece].at[:, 1 - core, part], core_b[i], cs.at[i], cr.at[i], c_peer))
        pltpu.make_async_copy(grads[piece].at[:, core, part], own_b[i], own_sem.at[i]).start()

    def add_into(target, others, rows):
        strip = 16
        steps = rows // strip

        def body(n, carry):
            z = lax.div(n, steps)
            at = aligned(lax.rem(n, steps), strip)
            total = target[z, at].astype(jnp.float32)
            for other in others:
                total = total + other[z, at].astype(jnp.float32)
            target[z, at] = total.astype(target.dtype)
            return carry

        lax.fori_loop(0, column * steps, body, 0)

    def pair(i):
        piece, row, rows, wide = chunks[i]
        pltpu.make_async_copy(
            grads[piece].at[:, core, pl.ds(row, rows)], own_b[i], own_sem.at[i]
        ).wait()
        arrived(core_b[i], cs.at[i], cr.at[i], c_peer)
        strip = 16
        steps = rows // strip
        part = wide // 8

        def body(n, carry):
            z = lax.div(n, steps)
            at = aligned(lax.rem(n, steps), strip)
            for j in range(8):
                cols = pl.ds(j * part, part)
                total = own_b[i][z, at, cols].astype(jnp.float32) + core_b[i][
                    z, at, cols
                ].astype(jnp.float32)
                sum_b[i][j, z, at] = total.astype(jnp.bfloat16)
            return carry

        lax.fori_loop(0, column * steps, body, 0)
        for half in range(2):
            for b in range(2):
                quarter = far_quarter(half, b)
                go(
                    send(
                        sum_b[i].at[quarter * 2 + half],
                        one_b[i].at[half, b],
                        os_.at[i, half, b],
                        or_.at[i, half, b],
                        peers[half],
                    )
                )

    def far_quarter(half, b):
        if half == 0:
            return (1 - bits[0]) + 2 * b
        return b + 2 * (1 - bits[1])

    def near_quarter(half, b):
        if half == 0:
            return bits[0] + 2 * b
        return b + 2 * bits[1]

    def first(i):
        rows = chunks[i][2]
        for half in range(2):
            for b in range(2):
                arrived(one_b[i].at[half, b], os_.at[i, half, b], or_.at[i, half, b], peers[half])
                quarter = near_quarter(half, b)
                add_into(sum_b[i].at[quarter * 2 + half], [one_b[i].at[half, b]], rows)
            other = d ^ 2 if half == 0 else d ^ 1
            go(
                send(
                    sum_b[i].at[other * 2 + half],
                    two_b[i].at[half],
                    ts.at[i, half],
                    tr.at[i, half],
                    peers[1 - half],
                )
            )

    def second(i):
        rows = chunks[i][2]
        for half in range(2):
            arrived(two_b[i].at[half], ts.at[i, half], tr.at[i, half], peers[1 - half])
            mine = sum_b[i].at[d * 2 + half]
            add_into(mine, [two_b[i].at[half]], rows)
            for k in range(1, column):
                to = lax.rem(place + k, column)
                go(
                    send(
                        mine.at[to],
                        zed_b[i].at[half, k - 1],
                        zs.at[i, half, k - 1],
                        zr.at[i, half, k - 1],
                        (d, to * 2 + core),
                    )
                )

    def last(i):
        piece, row, rows, wide = chunks[i]
        part = wide // 8
        for half in range(2):
            for k in range(1, column):
                arrived(
                    zed_b[i].at[half, k - 1],
                    zs.at[i, half, k - 1],
                    zr.at[i, half, k - 1],
                    c_peer,
                )
            total = sum_b[i][d * 2 + half, place].astype(jnp.float32)
            for k in range(1, column):
                total = total + zed_b[i][half, k - 1].astype(jnp.float32)
            fin_b[i][half] = total.astype(jnp.bfloat16)
        for half in range(2):
            place_out = outs[piece].at[pl.ds(row, rows), aligned(d * 2 + half, part)]
            pltpu.make_async_copy(fin_b[i].at[half], place_out, out_sem.at[i, half]).start()
            for axis in range(2):
                go(
                    send(
                        fin_b[i].at[half],
                        place_out,
                        fs.at[i, half, axis],
                        fr.at[i, half, axis],
                        peers[axis],
                    )
                )

    def spread(i):
        piece, row, rows, wide = chunks[i]
        part = wide // 8
        for half in range(2):
            for axis in range(2):
                view = outs[piece].at[
                    pl.ds(row, rows), aligned((d ^ (1 + axis)) * 2 + half, part)
                ]
                arrived(view, fs.at[i, half, axis], fr.at[i, half, axis], peers[axis])
                if half == axis:
                    go(send(view, view, gs.at[i, half], gr.at[i, half], peers[1 - axis]))

    def finish(i):
        piece, row, rows, wide = chunks[i]
        part = wide // 8
        for half in range(2):
            view = outs[piece].at[pl.ds(row, rows), aligned((d ^ 3) * 2 + half, part)]
            arrived(view, gs.at[i, half], gr.at[i, half], peers[1 - half])
            mine = outs[piece].at[pl.ds(row, rows), aligned(d * 2 + half, part)]
            pltpu.make_async_copy(fin_b[i].at[half], mine, out_sem.at[i, half]).wait()

    stages = (pair, first, second, last, spread, finish)
    for step in range(count + len(stages) - 1):
        for n, stage in enumerate(stages):
            if 0 <= step - n < count:
                stage(step - n)
        if step == 1:
            total = small[f]
            for k in range(1, fsdp_size):
                arrived(small_a.at[k - 1], ss.at[k - 1], sr.at[k - 1], c_peer)
                total = total + small_a[k - 1]
            small_b[d] = total
        if step == 2:
            for k in range(1, 4):
                go(
                    send(
                        small_b.at[d],
                        small_b.at[d],
                        us.at[k - 1],
                        ur.at[k - 1],
                        (d ^ k, f),
                    )
                )
        if step == 4:
            for k in range(1, 4):
                arrived(small_b.at[d ^ k], us.at[k - 1], ur.at[k - 1], c_peer)
            small_out[...] = (small_b[0] + small_b[1]) + (small_b[2] + small_b[3])
    for copy in pending:
        copy.wait_send()


def reduce_grads(fsdp_size, grads, small):
    column = fsdp_size // 2
    views = [g.reshape(column, 2, g.shape[0] // fsdp_size, g.shape[1]) for g in grads]
    pieces = len(views)
    chunks = chunk_list([v.shape for v in views])
    count = len(chunks)
    hbm = pl.BlockSpec(memory_space=pltpu.HBM)
    vmem = pl.BlockSpec(memory_space=pltpu.VMEM)
    dma = pltpu.SemaphoreType.DMA
    low = jnp.bfloat16
    scratch = []
    for lead in ((), (), (8,), (2, 2), (2,), "z", "f"):
        for _, _, rows, wide in chunks:
            if lead == "z":
                shape = (2, column - 1, rows, wide // 8)
            elif lead == "f":
                shape = (2, rows, wide // 8)
            elif lead == ():
                shape = (column, rows, wide)
            else:
                shape = (*lead, column, rows, wide // 8)
            scratch.append(pltpu.VMEM(shape, low))
    scratch += [pltpu.VMEM((fsdp_size - 1, 8, 128), jnp.float32), pltpu.VMEM((4, 8, 128), jnp.float32)]
    scratch += [dma((count,))] * 3 + [dma((count, 2, 2))] * 2 + [dma((count, 2))] * 2
    scratch += [dma((count, 2, column - 1))] * 2 + [dma((count, 2, 2))] * 2 + [dma((count, 2))] * 2
    scratch += [dma((count, 2))] + [dma((fsdp_size - 1,))] * 2 + [dma((3,))] * 2
    return pl.pallas_call(
        functools.partial(reduce_kernel, fsdp_size, chunks, pieces),
        out_shape=[jax.ShapeDtypeStruct(v.shape[2:], low) for v in views]
        + [jax.ShapeDtypeStruct((8, 128), jnp.float32)],
        in_specs=[hbm] * pieces + [vmem],
        out_specs=[hbm] * pieces + [vmem],
        scratch_shapes=scratch,
        compiler_params=pltpu.CompilerParams(
            collective_id=1, has_side_effects=True, vmem_limit_bytes=62 << 20
        ),
        name="reduce_grads",
    )(*views, small)


def on_device_wide(
    scenes_in,
    scene_lengths,
    cotangent,
    qkv_weight,
    out_weight,
    up_weight,
    down_weight,
    gain_one,
    bias_one,
    gain_two,
    bias_two,
):
    params = (
        lax.all_gather(qkv_weight, "fsdp", axis=0, tiled=True),
        lax.all_gather(out_weight, "fsdp", axis=0, tiled=True),
        lax.all_gather(up_weight, "fsdp", axis=0, tiled=True),
        lax.all_gather(down_weight, "fsdp", axis=0, tiled=True),
        lax.all_gather(gain_one, "fsdp", axis=0, tiled=True),
        lax.all_gather(bias_one, "fsdp", axis=0, tiled=True),
        lax.all_gather(gain_two, "fsdp", axis=0, tiled=True),
        lax.all_gather(bias_two, "fsdp", axis=0, tiled=True),
    )
    inputs = scenes_in[0].astype(jnp.float32)
    seq_len = inputs.shape[0]
    positions = jnp.arange(seq_len, dtype=jnp.int32)
    key_valid = positions < scene_lengths[0]
    row_mask = key_valid.astype(jnp.float32)[:, None]
    saved = forward_pass(inputs, key_valid, params)
    layer_out = (saved[0] * row_mask).astype(jnp.bfloat16)[None]
    grad_out = cotangent[0].astype(jnp.float32) * row_mask
    params_back = (
        lax.all_gather(qkv_weight, "fsdp", axis=0, tiled=True),
        lax.all_gather(out_weight, "fsdp", axis=0, tiled=True),
        lax.all_gather(up_weight, "fsdp", axis=0, tiled=True),
        lax.all_gather(down_weight, "fsdp", axis=0, tiled=True),
        lax.all_gather(gain_one, "fsdp", axis=0, tiled=True),
        lax.all_gather(bias_one, "fsdp", axis=0, tiled=True),
        lax.all_gather(gain_two, "fsdp", axis=0, tiled=True),
        lax.all_gather(bias_two, "fsdp", axis=0, tiled=True),
    )
    saved_back = forward_pass(inputs, key_valid, params_back)
    grad_resid, up_grad, down_grad, gain_two_grad, bias_two_grad = mlp_back(
        grad_out, saved_back, params_back
    )
    input_grad, qkv_grad, out_grad, gain_one_grad, bias_one_grad = attn_back(
        grad_resid, saved_back, params_back
    )
    shares = (
        lax.psum_scatter(qkv_grad, "fsdp", scatter_dimension=0, tiled=True),
        lax.psum_scatter(out_grad, "fsdp", scatter_dimension=0, tiled=True),
        lax.psum_scatter(up_grad, "fsdp", scatter_dimension=0, tiled=True),
        lax.psum_scatter(down_grad, "fsdp", scatter_dimension=0, tiled=True),
        lax.psum_scatter(gain_one_grad, "fsdp", scatter_dimension=0, tiled=True),
        lax.psum_scatter(bias_one_grad, "fsdp", scatter_dimension=0, tiled=True),
        lax.psum_scatter(gain_two_grad, "fsdp", scatter_dimension=0, tiled=True),
        lax.psum_scatter(bias_two_grad, "fsdp", scatter_dimension=0, tiled=True),
    )
    summed = (
        lax.psum(shares[0].astype(jnp.bfloat16), "dp").astype(jnp.float32),
        lax.psum(shares[1].astype(jnp.bfloat16), "dp").astype(jnp.float32),
        lax.psum(shares[2].astype(jnp.bfloat16), "dp").astype(jnp.float32),
        lax.psum(shares[3].astype(jnp.bfloat16), "dp").astype(jnp.float32),
        lax.psum(shares[4].astype(jnp.bfloat16), "dp").astype(jnp.float32),
        lax.psum(shares[5].astype(jnp.bfloat16), "dp").astype(jnp.float32),
        lax.psum(shares[6].astype(jnp.bfloat16), "dp").astype(jnp.float32),
        lax.psum(shares[7].astype(jnp.bfloat16), "dp").astype(jnp.float32),
    )
    qkv_total, out_total, up_total, down_total = (summed[0], summed[1], summed[2], summed[3])
    gain_one_total, bias_one_total, gain_two_total, bias_two_total = (
        summed[4],
        summed[5],
        summed[6],
        summed[7],
    )
    input_out = input_grad.astype(jnp.bfloat16)[None]
    return (
        layer_out,
        input_out,
        qkv_total,
        out_total,
        up_total,
        down_total,
        gain_one_total,
        bias_one_total,
        gain_two_total,
        bias_two_total,
    )


def on_device(
    scenes_in,
    scene_lengths,
    cotangent,
    qkv_weight,
    out_weight,
    up_weight,
    down_weight,
    gain_one,
    bias_one,
    gain_two,
    bias_two,
):
    rows = gain_one.shape[0]
    fsdp_size = D // rows
    small = jnp.stack([gain_one, bias_one, gain_two, bias_two])
    small = jnp.pad(small, ((0, 12), (0, 128 - rows)))
    qkv_all, out_all, up_all, down_all, small_all = gather_weights(
        fsdp_size, (qkv_weight, out_weight, up_weight, down_weight), small
    )
    vectors = small_all.reshape(fsdp_size, 16, 128)[:, :4, :rows].transpose(1, 0, 2).reshape(4, D)
    params = (qkv_all, out_all, up_all, down_all, vectors[0], vectors[1], vectors[2], vectors[3])
    inputs = scenes_in[0].astype(jnp.float32)
    seq_len = inputs.shape[0]
    positions = jnp.arange(seq_len, dtype=jnp.int32)
    key_valid = positions < scene_lengths[0]
    row_mask = key_valid.astype(jnp.float32)[:, None]
    saved = forward_pass(inputs, key_valid, params)
    layer_out = (saved[0] * row_mask).astype(jnp.bfloat16)[None]
    grad_out = cotangent[0].astype(jnp.float32) * row_mask
    grad_resid, up_grad, down_grad, gain_two_grad, bias_two_grad = mlp_back(
        grad_out, saved, params
    )
    input_grad, qkv_grad, out_grad, gain_one_grad, bias_one_grad = attn_back(
        grad_resid, saved, params
    )
    low = jnp.bfloat16
    small_grad = jnp.stack([gain_one_grad, bias_one_grad, gain_two_grad, bias_two_grad])
    small_grad = small_grad.reshape(4, fsdp_size, rows).transpose(1, 0, 2)
    small_grad = jnp.pad(small_grad, ((0, 0), (0, 4), (0, 128 - rows)))
    down_sum, up_sum, out_sum, qkv_sum, small_sum = reduce_grads(
        fsdp_size,
        (down_grad.astype(low), up_grad.astype(low), out_grad.astype(low), qkv_grad.astype(low)),
        small_grad,
    )
    wide = jnp.float32
    return (
        layer_out,
        input_grad.astype(low)[None],
        qkv_sum.astype(wide),
        out_sum.astype(wide),
        up_sum.astype(wide),
        down_sum.astype(wide),
        small_sum[0, :rows],
        small_sum[1, :rows],
        small_sum[2, :rows],
        small_sum[3, :rows],
    )


def solution(mesh):
    placed = (
        P(("dp", "fsdp"), None, None),
        P(("dp", "fsdp")),
        P(("dp", "fsdp"), None, None),
        P("fsdp", None),
        P("fsdp", None),
        P("fsdp", None),
        P("fsdp", None),
        P("fsdp"),
        P("fsdp"),
        P("fsdp"),
        P("fsdp"),
    )
    body = on_device if mesh.shape["dp"] == 4 and mesh.shape["fsdp"] == 8 else on_device_wide
    return jax.shard_map(
        body,
        mesh=mesh,
        in_specs=placed,
        out_specs=(
            P(("dp", "fsdp"), None, None),
            P(("dp", "fsdp"), None, None),
            P("fsdp", None),
            P("fsdp", None),
            P("fsdp", None),
            P("fsdp", None),
            P("fsdp"),
            P("fsdp"),
            P("fsdp"),
            P("fsdp"),
        ),
        check_vma=False,
    )
```

```python
import functools
import math

import jax
import jax.numpy as jnp
from jax import lax
from jax.experimental import pallas as pl
from jax.experimental.pallas import tpu as pltpu
from jax.sharding import PartitionSpec as P

D = 1024
HEADS = 16
HEAD_DIM = 64


epsilon = 1e-05


def norm_rows(values_in):
    row_mean = jnp.mean(values_in, axis=-1, keepdims=True)
    centered = values_in - row_mean
    variance = jnp.mean(centered * centered, axis=-1, keepdims=True)
    inverse = lax.rsqrt(variance + epsilon)
    return (centered * inverse, inverse)


def norm_back(grad_normed, normed, inverse):
    first_mean = jnp.mean(grad_normed, axis=-1, keepdims=True)
    second_mean = jnp.mean(grad_normed * normed, axis=-1, keepdims=True)
    return inverse * (grad_normed - first_mean - normed * second_mean)


def inner_rows(left, right):
    return lax.dot_general(
        left, right, (((0,), (0,)), ((), ())), preferred_element_type=jnp.float32
    )


def outer_cols(left, right):
    return lax.dot_general(
        left, right, (((1,), (1,)), ((), ())), preferred_element_type=jnp.float32
    )


def forward_pass(inputs, key_valid, params):
    qkv_weight, out_weight, up_weight, down_weight, gain_one, bias_one, gain_two, bias_two = params
    seq_len = inputs.shape[0]
    normed_one, inverse_one = norm_rows(inputs)
    hidden_one = (normed_one * gain_one.astype(jnp.float32) + bias_one.astype(jnp.float32)).astype(
        jnp.bfloat16
    )
    qkv_low = jnp.dot(hidden_one, qkv_weight, preferred_element_type=jnp.float32).astype(
        jnp.bfloat16
    )
    split_view = qkv_low.reshape(seq_len, 3, HEADS, HEAD_DIM)
    queries = split_view[:, 0]
    keys_all = split_view[:, 1]
    values_all = split_view[:, 2]
    scale_factor = 1.0 / math.sqrt(HEAD_DIM)
    scores = (
        jnp.einsum("qhd,khd->hqk", queries, keys_all, preferred_element_type=jnp.float32)
        * scale_factor
    )
    masked = jnp.where(key_valid[None, None, :], scores, -1e30)
    highest = jnp.max(masked, axis=-1, keepdims=True)
    expont = jnp.exp(masked - highest)
    probs = expont / jnp.sum(expont, axis=-1, keepdims=True)
    probs_low = probs.astype(jnp.bfloat16)
    attended = jnp.einsum("hqk,khd->qhd", probs_low, values_all, preferred_element_type=jnp.float32)
    attn_low = attended.reshape(seq_len, D).astype(jnp.bfloat16)
    resid_one = inputs + jnp.dot(attn_low, out_weight, preferred_element_type=jnp.float32)
    normed_two, inverse_two = norm_rows(resid_one)
    hidden_two = (normed_two * gain_two.astype(jnp.float32) + bias_two.astype(jnp.float32)).astype(
        jnp.bfloat16
    )
    hidden_pre = jnp.dot(hidden_two, up_weight, preferred_element_type=jnp.float32)
    activated = jax.nn.gelu(hidden_pre, approximate=False).astype(jnp.bfloat16)
    result = resid_one + jnp.dot(activated, down_weight, preferred_element_type=jnp.float32)
    return (
        result,
        normed_one,
        inverse_one,
        hidden_one,
        queries,
        keys_all,
        values_all,
        probs,
        probs_low,
        attn_low,
        normed_two,
        inverse_two,
        hidden_two,
        hidden_pre,
        activated,
    )


def mlp_back(grad_out, saved, params):
    up_weight, down_weight, gain_two = (params[2], params[3], params[6])
    normed_two, inverse_two, hidden_two, hidden_pre, activated = (
        saved[10],
        saved[11],
        saved[12],
        saved[13],
        saved[14],
    )
    grad_low = grad_out.astype(jnp.bfloat16)
    down_grad = inner_rows(activated, grad_low)
    grad_act = outer_cols(grad_low, down_weight)
    cumul = 0.5 * (1.0 + lax.erf(hidden_pre * (1.0 / math.sqrt(2.0))))
    density = jnp.exp(-0.5 * hidden_pre * hidden_pre) * (1.0 / math.sqrt(2.0 * math.pi))
    grad_pre = (grad_act * (cumul + hidden_pre * density)).astype(jnp.bfloat16)
    up_grad = inner_rows(hidden_two, grad_pre)
    grad_hidden = outer_cols(grad_pre, up_weight)
    gain_two_grad = jnp.sum(grad_hidden * normed_two, axis=0)
    bias_two_grad = jnp.sum(grad_hidden, axis=0)
    grad_resid = grad_out + norm_back(
        grad_hidden * gain_two.astype(jnp.float32), normed_two, inverse_two
    )
    return (grad_resid, up_grad, down_grad, gain_two_grad, bias_two_grad)


def attn_back(grad_resid, saved, params):
    qkv_weight, out_weight, gain_one = (params[0], params[1], params[4])
    normed_one, inverse_one, hidden_one = (saved[1], saved[2], saved[3])
    queries, keys_all, values_all, probs, probs_low, attn_low = (
        saved[4],
        saved[5],
        saved[6],
        saved[7],
        saved[8],
        saved[9],
    )
    seq_len = grad_resid.shape[0]
    scale_factor = 1.0 / math.sqrt(HEAD_DIM)
    resid_low = grad_resid.astype(jnp.bfloat16)
    out_grad = inner_rows(attn_low, resid_low)
    grad_attn = (
        outer_cols(resid_low, out_weight).astype(jnp.bfloat16).reshape(seq_len, HEADS, HEAD_DIM)
    )
    grad_probs = jnp.einsum(
        "qhd,khd->hqk", grad_attn, values_all, preferred_element_type=jnp.float32
    )
    row_dot = jnp.sum(probs * grad_probs, axis=-1, keepdims=True)
    grad_scores = (probs * (grad_probs - row_dot)).astype(jnp.bfloat16)
    grad_values = jnp.einsum(
        "hqk,qhd->khd", probs_low, grad_attn, preferred_element_type=jnp.float32
    )
    grad_queries = (
        jnp.einsum("hqk,khd->qhd", grad_scores, keys_all, preferred_element_type=jnp.float32)
        * scale_factor
    )
    grad_keys = (
        jnp.einsum("hqk,qhd->khd", grad_scores, queries, preferred_element_type=jnp.float32)
        * scale_factor
    )
    grad_qkv = (
        jnp.stack([grad_queries, grad_keys, grad_values], axis=1)
        .reshape(seq_len, 3 * D)
        .astype(jnp.bfloat16)
    )
    qkv_grad = inner_rows(hidden_one, grad_qkv)
    grad_hidden = outer_cols(grad_qkv, qkv_weight)
    gain_one_grad = jnp.sum(grad_hidden * normed_one, axis=0)
    bias_one_grad = jnp.sum(grad_hidden, axis=0)
    input_grad = grad_resid + norm_back(
        grad_hidden * gain_one.astype(jnp.float32), normed_one, inverse_one
    )
    return (input_grad, qkv_grad, out_grad, gain_one_grad, bias_one_grad)


MESH_ID = pl.DeviceIdType.MESH


def aligned(index, size):
    return pl.ds(pl.multiple_of(index * size, size), size)


def greet(dp_index, fsdp_index, fsdp_size):
    barrier = pltpu.get_barrier_semaphore()
    peers = [(dp_index ^ 1, fsdp_index), (dp_index ^ 2, fsdp_index), (dp_index ^ 3, fsdp_index)]
    peers += [(dp_index, lax.rem(fsdp_index + k, fsdp_size)) for k in range(1, fsdp_size)]
    for peer in peers:
        pl.semaphore_signal(barrier, inc=1, device_id=peer, device_id_type=MESH_ID)
    pl.semaphore_wait(barrier, len(peers))


def send(src, dst, send_sem, recv_sem, device):
    return pltpu.make_async_remote_copy(
        src_ref=src,
        dst_ref=dst,
        send_sem=send_sem,
        recv_sem=recv_sem,
        device_id=device,
        device_id_type=MESH_ID,
    )


def gelu_parts(u):
    cumul = 0.5 * (1.0 + lax.erf(u * (1.0 / math.sqrt(2.0))))
    density = jnp.exp(-0.5 * u * u) * (1.0 / math.sqrt(2.0 * math.pi))
    return u * cumul, cumul + u * density


def head_scores(q_head, keys, key_valid):
    scores = outer_cols(q_head, keys) * (1.0 / math.sqrt(HEAD_DIM))
    masked = jnp.where(key_valid, scores, -1e30)
    expont = jnp.exp(masked - jnp.max(masked, axis=-1, keepdims=True))
    return expont / jnp.sum(expont, axis=-1, keepdims=True)


def vector_row(small, row, fsdp_size):
    values = small[...].astype(jnp.float32)
    return jnp.concatenate([values[16 * f + row : 16 * f + row + 1] for f in range(fsdp_size)], axis=1)


def transposed(target, source, fsdp_size):
    rows = target.shape[2]

    def body(n, carry):
        target[lax.rem(n, 2), lax.div(n, 2)] = jnp.transpose(source[:, aligned(n, rows)])
        return carry

    lax.fori_loop(0, fsdp_size, body, 0)


def forward_kernel(fsdp_size, *refs):
    pieces = 4
    length, scenes = refs[:2]
    shards = refs[2:6]
    small = refs[6]
    fulls = refs[7:11]
    layer_out, small_out = refs[11:13]
    saved_out = refs[13:20]
    rest = refs[20:]
    weights = rest[:4]
    small_full, hidden, qkv, attn, resid, normed, active = rest[4:11]
    saved = rest[11:16]
    (own_sem, zs, zr, xs, xr, ys, yr, ds, dr, es, er, cs, cr, ss, sr, load_sem, save_sem) = rest[16:]
    hidden_t, hidden_two_t, attn_t, active_t, slope = saved
    column = fsdp_size // 2
    low, wide = jnp.bfloat16, jnp.float32
    d = lax.axis_index("dp")
    f = lax.axis_index("fsdp")
    core = lax.rem(f, 2)
    place = lax.div(f, 2)
    x_peer, y_peer, c_peer = (d ^ 1, f), (d ^ 2, f), (d, f ^ 1)
    seq_len = scenes.shape[0]

    def block(piece, place_from, quarter, half=None):
        rows = shards[piece].shape[0]
        span = shards[piece].shape[1] // 4
        row_part = aligned(place_from * 2 + core, rows)
        if half is None:
            return fulls[piece].at[row_part, aligned(quarter, span)]
        return fulls[piece].at[row_part, aligned(quarter * 2 + half, span // 2)]

    pending = []

    def go(copy):
        copy.start()
        pending.append(copy)

    def to_partner(piece, view):
        send(view, view, cs.at[piece], cr.at[piece], c_peer).start()

    def source(k):
        return lax.rem(place - k + column, column)

    def arrived(view, send_sem, recv_sem, device):
        send(view, view, send_sem, recv_sem, device).wait_recv()

    def from_column(piece, k):
        at = (piece, k - 1)
        view = block(piece, source(k), d)
        arrived(view, zs.at[at], zr.at[at], x_peer)
        go(send(view, view, xs.at[at], xr.at[at], x_peer))
        go(send(view, view, ys.at[at], yr.at[at], y_peer))
        to_partner(piece, view)

    def from_sides(piece, k):
        at = (piece, k - 1)
        view = block(piece, source(k), d ^ 1)
        arrived(view, xs.at[at], xr.at[at], x_peer)
        part = block(piece, source(k), d ^ 1, 0)
        go(send(part, part, ds.at[at], dr.at[at], y_peer))
        to_partner(piece, view)
        view = block(piece, source(k), d ^ 2)
        arrived(view, ys.at[at], yr.at[at], y_peer)
        part = block(piece, source(k), d ^ 2, 1)
        go(send(part, part, es.at[at], er.at[at], x_peer))
        to_partner(piece, view)

    def from_corner(piece, k):
        at = (piece, k - 1)
        for half, (a, b, peer) in enumerate(((ds, dr, y_peer), (es, er, x_peer))):
            part = block(piece, source(k), d ^ 3, half)
            arrived(part, a.at[at], b.at[at], peer)
            to_partner(piece, part)

    def load(piece, part):
        rows = fulls[piece].shape[0] // 8
        at = pl.ds(part * rows, rows)
        return pltpu.make_async_copy(fulls[piece].at[at], weights[piece].at[at], load_sem.at[piece, part])

    def from_partner(piece, k):
        rows = shards[piece].shape[0]
        view = fulls[piece].at[pl.ds(0, rows * column)]
        send(view, view, cs.at[piece], cr.at[piece], c_peer).wait()
        own = fulls[piece].at[aligned(f, rows)]
        pltpu.make_async_copy(weights[piece].at[aligned(f, rows)], own, own_sem.at[1, piece]).wait()
        for part in range(8):
            load(piece, part).start()

    every = range(1, column)
    order = []
    order += [(from_column, 0, k) for k in every]
    order += [(from_sides, 0, k) for k in every]
    order += [(from_column, 1, k) for k in every]
    order += [(from_corner, 0, k) for k in every] + [(from_partner, 0, 0)]
    for piece in (1, 2, 3):
        for k in every:
            if piece < 3:
                order.append((from_column, piece + 1, k))
            order.append((from_sides, piece, k))
        order += [(from_corner, piece, k) for k in every] + [(from_partner, piece, 0)]
    done = []

    def pump(count=1):
        for _ in range(count):
            if len(done) < len(order):
                action, piece, k = order[len(done)]
                done.append(1)
                action(piece, k)

    def pump_to(entry):
        while order.index(entry) >= len(done):
            pump()

    greet(d, f, fsdp_size)
    small_rows = small.shape[0]
    for k in range(1, fsdp_size):
        go(
            send(
                small,
                small_full.at[aligned(f, small_rows)],
                ss.at[k - 1],
                sr.at[k - 1],
                (d, lax.rem(f + k, fsdp_size)),
            )
        )
    pltpu.make_async_copy(small, small_full.at[aligned(f, small_rows)], own_sem.at[0, pieces]).start()
    for piece in range(pieces):
        rows = shards[piece].shape[0]
        span = shards[piece].shape[1] // 4
        for k in every:
            go(
                send(
                    shards[piece].at[:, aligned(d, span)],
                    block(piece, place, d),
                    zs.at[piece, k - 1],
                    zr.at[piece, k - 1],
                    (d, lax.rem(place + k, column) * 2 + core),
                )
            )
        own = aligned(f, rows)
        send(shards[piece], fulls[piece].at[own], cs.at[piece], cr.at[piece], c_peer).start()
        pltpu.make_async_copy(shards[piece], weights[piece].at[own], own_sem.at[0, piece]).start()
    for piece in range(pieces):
        own = aligned(f, shards[piece].shape[0])
        pltpu.make_async_copy(shards[piece], weights[piece].at[own], own_sem.at[0, piece]).wait()
        pltpu.make_async_copy(weights[piece].at[own], fulls[piece].at[own], own_sem.at[1, piece]).start()

    inputs = scenes[...].astype(wide)
    normed_one, _ = norm_rows(inputs)
    for k in range(1, fsdp_size):
        view = small_full.at[aligned(lax.rem(f - k + fsdp_size, fsdp_size), small_rows)]
        arrived(view, ss.at[k - 1], sr.at[k - 1], c_peer)
    pltpu.make_async_copy(small, small_full.at[aligned(f, small_rows)], own_sem.at[0, pieces]).wait()
    gain, bias = vector_row(small_full, 0, fsdp_size), vector_row(small_full, 1, fsdp_size)
    hidden[...] = (normed_one * gain + bias).astype(low)
    small_out[...] = small_full[...]
    pump(2)
    transposed(hidden_t, hidden, fsdp_size)
    saves = []

    def save(index, ref):
        copy = pltpu.make_async_copy(ref, saved_out[index], save_sem.at[index])
        saves.append(copy)
        return copy

    pump_to((from_partner, 0, 0))
    save(0, hidden_t).start()
    for part in range(8):
        load(0, part).wait()

    def project(n, carry):
        cols = aligned(n, 512)
        qkv[:, cols] = jnp.dot(hidden[...], weights[0][:, cols], preferred_element_type=wide).astype(low)
        return carry

    tiles = qkv.shape[1] // 512
    lax.fori_loop(0, tiles // 2, project, 0)
    pump(2)
    lax.fori_loop(tiles // 2, tiles, project, 0)
    pump(2)
    save(1, qkv).start()
    key_valid = lax.broadcasted_iota(jnp.int32, (1, seq_len), 1) < length[0]
    first_half = lax.broadcasted_iota(jnp.int32, (1, 128), 1) < HEAD_DIM
    halves = (first_half.astype(wide).astype(low), 1 - first_half.astype(wide).astype(low))
    pairs = D // 128

    def attend(j, carry):
        queries, keys, values = (qkv[:, aligned(j + i * pairs, 128)] for i in range(3))
        found = []
        for half in halves:
            probs = head_scores(queries * half, keys, key_valid)
            found.append(jnp.dot(probs.astype(low), values, preferred_element_type=wide))
        attn[:, aligned(j, 128)] = jnp.where(first_half, found[0], found[1]).astype(low)
        return carry

    for j in range(0, pairs, 2):
        lax.fori_loop(j, j + 2, attend, 0)
        pump(2)
    pump_to((from_partner, 1, 0))
    transposed(attn_t, attn, fsdp_size)
    save(2, attn_t).start()
    for part in range(8):
        load(1, part).wait()

    def second(n, carry):
        cols = aligned(n, 512)
        resid[:, cols] = scenes[:, cols].astype(wide) + jnp.dot(
            attn[...], weights[1][:, cols], preferred_element_type=wide
        )
        return carry

    lax.fori_loop(0, D // 512, second, 0)
    save(3, resid).start()
    normed_two, _ = norm_rows(resid[...])
    gain, bias = vector_row(small_full, 2, fsdp_size), vector_row(small_full, 3, fsdp_size)
    normed[...] = (normed_two * gain + bias).astype(low)
    transposed(hidden_two_t, normed, fsdp_size)
    save(4, hidden_two_t).start()
    pump_to((from_partner, 2, 0))
    for part in range(8):
        load(2, part).wait()

    def expand(n, carry):
        cols = aligned(n, 256)
        hidden_pre = jnp.dot(normed[...], weights[2][:, cols], preferred_element_type=wide)
        acts, grads = gelu_parts(hidden_pre)
        active[:, cols] = acts.astype(low)
        slope[:, cols] = grads.astype(low)
        return carry

    spans = active.shape[1] // 256
    for n in range(0, spans, 4):
        lax.fori_loop(n, n + 4, expand, 0)
        pump(1)
    save(5, slope).start()
    transposed(active_t, active, fsdp_size)
    save(6, active_t).start()
    pump_to((from_partner, 3, 0))
    row_valid = lax.broadcasted_iota(jnp.int32, (seq_len, 1), 0) < length[0]
    for part in range(8):
        load(3, part).wait()
        rows = pl.ds(part * (active.shape[1] // 8), active.shape[1] // 8)
        resid_part = jnp.dot(active[:, rows], weights[3][rows], preferred_element_type=wide)
        if part == 0:
            saves[3].wait()
        resid[...] += resid_part
    layer_out[...] = jnp.where(row_valid, resid[...], 0.0).astype(low)
    for copy in pending:
        copy.wait_send()
    for n, copy in enumerate(saves):
        if n != 3:
            copy.wait()


def gather_forward(fsdp_size, length, scenes, shards, small):
    pieces = len(shards)
    hops = fsdp_size // 2 - 1
    column = fsdp_size // 2
    seq_len = scenes.shape[0]
    ff = shards[3].shape[0] * fsdp_size
    hbm = pl.BlockSpec(memory_space=pltpu.HBM)
    vmem = pl.BlockSpec(memory_space=pltpu.VMEM)
    smem = pl.BlockSpec(memory_space=pltpu.SMEM)
    dma = pltpu.SemaphoreType.DMA
    low, wide = jnp.bfloat16, jnp.float32
    shape = jax.ShapeDtypeStruct
    saved = [
        ((2, column, D // fsdp_size, seq_len), low),
        ((seq_len, 3 * D), low),
        ((2, column, D // fsdp_size, seq_len), low),
        ((seq_len, D), wide),
        ((2, column, D // fsdp_size, seq_len), low),
        ((seq_len, ff), low),
        ((2, column, ff // fsdp_size, seq_len), low),
    ]
    full_shapes = [(a.shape[0] * fsdp_size, a.shape[1]) for a in shards]
    small_shape = (small.shape[0] * fsdp_size, small.shape[1])
    return pl.pallas_call(
        functools.partial(forward_kernel, fsdp_size),
        out_shape=[shape(s, low) for s in full_shapes]
        + [shape((seq_len, D), low), shape(small_shape, low)]
        + [shape(*s) for s in saved],
        in_specs=[smem, vmem] + [hbm] * (pieces + 1),
        out_specs=[hbm] * pieces + [vmem, vmem] + [hbm] * len(saved),
        scratch_shapes=[pltpu.VMEM(s, low) for s in full_shapes]
        + [
            pltpu.VMEM(small_shape, low),
            pltpu.VMEM((seq_len, D), low),
            pltpu.VMEM((seq_len, 3 * D), low),
            pltpu.VMEM((seq_len, D), low),
            pltpu.VMEM((seq_len, D), wide),
            pltpu.VMEM((seq_len, D), low),
            pltpu.VMEM((seq_len, ff), low),
        ]
        + [pltpu.VMEM(*saved[i]) for i in (0, 4, 2, 6, 5)]
        + [dma((2, pieces + 1))]
        + [dma((pieces, hops))] * 10
        + [dma((pieces,))] * 2
        + [dma((fsdp_size - 1,))] * 2
        + [dma((pieces, 8)), dma((len(saved),))],
        compiler_params=pltpu.CompilerParams(
            collective_id=0, has_side_effects=True, vmem_limit_bytes=62 << 20
        ),
        name="gather_forward",
    )(length, scenes, *shards, small)


def chunk_list(shapes):
    chunks = []
    for piece, (rows, span) in enumerate(shapes):
        part = span // 8
        high = min(rows, 128)
        width = 256 if part % 256 == 0 else 128
        for row in range(0, rows, high):
            for col in range(0, part, width):
                chunks.append((piece, row, high, part, col, width))
    return chunks


def backward_kernel(fsdp_size, chunks, *refs):
    pieces = 4
    count = len(chunks)
    column = fsdp_size // 2
    low, wide = jnp.bfloat16, jnp.float32
    length, scenes, cotangent, small_full = refs[:4]
    saved_in = refs[4:11]
    fulls = refs[11:15]
    outs = refs[15:19]
    input_grad, small_out = refs[19:21]
    rest = refs[21:]
    sum_b, one_b, two_b, zed_b, fin_b = (rest[i * count : (i + 1) * count] for i in range(5))
    rest = rest[5 * count :]
    (other_b, core_b, weight, hidden_t, qkv, attn_t, resid, hidden_two_t, slope, active_t) = rest[:10]
    (grad_low, grad_pre, grad_hidden, grad_resid, grad_attn, small_g, small_a, small_b) = rest[10:18]
    (cs, cr, os_, or_, ts, tr, zs, zr, fs, fr, gs, gr, out_sem, ss, sr, us, ur) = rest[18:35]
    save_sem, load_sem, credit = rest[35:]
    d = lax.axis_index("dp")
    f = lax.axis_index("fsdp")
    core = lax.rem(f, 2)
    place = lax.div(f, 2)
    bits = (lax.rem(d, 2), lax.div(d, 2))
    peers = ((d ^ 1, f), (d ^ 2, f))
    c_peer = (d, f ^ 1)
    seq_len = scenes.shape[0]
    slots_other, slots_core = other_b.shape[0], core_b.shape[0]
    pending = []
    core_sends = {}

    def go(copy):
        copy.start()
        pending.append(copy)
        return copy

    def arrived(view, send_sem, recv_sem, device):
        send(view, view, send_sem, recv_sem, device).wait_recv()

    def slot_view(ref, slot, i):
        _, _, high, _, _, width = chunks[i]
        return ref.at[slot, :, pl.ds(0, column * high), pl.ds(0, width)]

    def fetch(index, ref):
        return pltpu.make_async_copy(saved_in[index], ref, save_sem.at[index])

    def grams(i, left_t, right):
        piece, row, high, part, col, width = chunks[i]
        slot = i % slots_other
        if i >= slots_other:
            core_sends[i - slots_other].wait_send()
        step = 2 if width == part and width == 128 else 1

        def fill(half, target):
            left = left_t[half, :, pl.ds(row, high), :].reshape(column * high, seq_len)

            def body(n, carry):
                start = pl.multiple_of(n * step * part + col, 128)
                found = jnp.dot(
                    left, right[:, pl.ds(start, step * width)], preferred_element_type=wide
                ).astype(low)
                for m in range(step):
                    target[n * step + m] = found[:, m * width : (m + 1) * width]
                return carry

            lax.fori_loop(0, 8 // step, body, 0)

        fill(1 - core, slot_view(other_b, slot, i))
        if i >= slots_core:
            pl.semaphore_wait(credit, 1)
        fill(core, sum_b[i])
        copy = send(
            slot_view(other_b, slot, i),
            slot_view(core_b, i % slots_core, i),
            cs.at[i],
            cr.at[i],
            c_peer,
        )
        copy.start()
        core_sends[i] = copy

    def add_into(target, other):
        rows = target.shape[0]
        strip = 64

        def body(n, carry):
            at = aligned(n, strip)
            target[at] = (target[at].astype(wide) + other[at].astype(wide)).astype(low)
            return carry

        lax.fori_loop(0, rows // strip, body, 0)

    def far_quarter(half, b):
        if half == 0:
            return (1 - bits[0]) + 2 * b
        return b + 2 * (1 - bits[1])

    def near_quarter(half, b):
        if half == 0:
            return bits[0] + 2 * b
        return b + 2 * bits[1]

    def pair(i):
        view = slot_view(core_b, i % slots_core, i)
        arrived(view, cs.at[i], cr.at[i], c_peer)

        def add(quarter, half):
            add_into(sum_b[i].at[quarter * 2 + half], view.at[quarter * 2 + half])

        for b in range(2):
            for half in range(2):
                add(far_quarter(half, b), half)
            for half in range(2):
                go(
                    send(
                        sum_b[i].at[far_quarter(half, b) * 2 + half],
                        one_b[i].at[half, b],
                        os_.at[i, half, b],
                        or_.at[i, half, b],
                        peers[half],
                    )
                )
        for b in range(2):
            for half in range(2):
                add(near_quarter(half, b), half)
        if i + slots_core < count:
            pl.semaphore_signal(credit, inc=1, device_id=c_peer, device_id_type=MESH_ID)

    def first(i):
        for half in range(2):
            for b in range(2):
                arrived(one_b[i].at[half, b], os_.at[i, half, b], or_.at[i, half, b], peers[half])
                add_into(sum_b[i].at[near_quarter(half, b) * 2 + half], one_b[i].at[half, b])
            other = d ^ 2 if half == 0 else d ^ 1
            go(
                send(
                    sum_b[i].at[other * 2 + half],
                    two_b[i].at[half],
                    ts.at[i, half],
                    tr.at[i, half],
                    peers[1 - half],
                )
            )

    def second(i):
        _, _, high, _, _, _ = chunks[i]
        for half in range(2):
            arrived(two_b[i].at[half], ts.at[i, half], tr.at[i, half], peers[1 - half])
            mine = sum_b[i].at[d * 2 + half]
            add_into(mine, two_b[i].at[half])
            for k in range(1, column):
                to = lax.rem(place + k, column)
                go(
                    send(
                        mine.at[aligned(to, high)],
                        zed_b[i].at[half, k - 1],
                        zs.at[i, half, k - 1],
                        zr.at[i, half, k - 1],
                        (d, to * 2 + core),
                    )
                )

    def result(i, quarter, half):
        piece, row, high, part, col, width = chunks[i]
        start = pl.multiple_of((quarter * 2 + half) * part + col, 128)
        return outs[piece].at[pl.ds(row, high), pl.ds(start, width)]

    def last(i):
        _, _, high, _, _, _ = chunks[i]
        for half in range(2):
            for k in range(1, column):
                at = (i, half, k - 1)
                arrived(zed_b[i].at[half, k - 1], zs.at[at], zr.at[at], c_peer)
            total = sum_b[i][d * 2 + half, aligned(place, high)].astype(wide)
            for k in range(1, column):
                total = total + zed_b[i][half, k - 1].astype(wide)
            fin_b[i][half] = total.astype(low)
        for half in range(2):
            mine = result(i, d, half)
            pltpu.make_async_copy(fin_b[i].at[half], mine, out_sem.at[i, half]).start()
            for axis in range(2):
                at = (i, half, axis)
                go(send(fin_b[i].at[half], mine, fs.at[at], fr.at[at], peers[axis]))

    def spread(i):
        for half in range(2):
            for axis in range(2):
                at = (i, half, axis)
                view = result(i, d ^ (1 + axis), half)
                arrived(view, fs.at[at], fr.at[at], peers[axis])
                if half == axis:
                    go(send(view, view, gs.at[i, half], gr.at[i, half], peers[1 - axis]))

    def finish(i):
        for half in range(2):
            view = result(i, d ^ 3, half)
            arrived(view, gs.at[i, half], gr.at[i, half], peers[1 - half])
            pltpu.make_async_copy(fin_b[i].at[half], result(i, d, half), out_sem.at[i, half]).wait()

    stages = (first, second, last, spread, finish)
    order = []
    for step in range(count + len(stages) - 1):
        for n, stage in enumerate(stages):
            if 0 <= step - n < count:
                order.append((stage, step - n))
    done = []
    waiting = []
    paired = []

    def pair_up(keep=0):
        while len(waiting) > keep:
            i = waiting.pop(0)
            pair(i)
            paired.append(i)

    def pump(limit=1):
        pair_up()
        for _ in range(limit):
            if len(done) < len(order):
                stage, i = order[len(done)]
                if i not in paired:
                    return
                done.append(1)
                stage(i)

    def produce(piece, left_t, right, limit):
        for i in range(count):
            if chunks[i][0] == piece:
                grams(i, left_t, right)
                waiting.append(i)
                pair_up(1)
                for _ in range(limit):
                    if len(done) < len(order) and order[len(done)][1] in paired:
                        stage, n = order[len(done)]
                        done.append(1)
                        stage(n)

    greet(d, f, fsdp_size)
    big = weight
    ff = fulls[3].shape[0]

    def down_load(part):
        rows = ff // 8
        at = pl.ds(part * rows, rows)
        return pltpu.make_async_copy(fulls[3].at[at], big.at[at], load_sem.at[3, part])

    def up_load(part):
        return pltpu.make_async_copy(
            fulls[2].at[:, pl.ds(part * D, D)], big.at[pl.ds(part * D, D)], load_sem.at[2, part]
        )

    def qkv_load(part):
        return pltpu.make_async_copy(
            fulls[0].at[:, pl.ds(part * D, D)], big.at[pl.ds(part * D, D)], load_sem.at[0, part]
        )

    def out_load():
        return pltpu.make_async_copy(fulls[1], big.at[pl.ds(3 * D, D)], load_sem.at[1, 0])

    index = {"hidden_t": 0, "qkv": 1, "attn_t": 2, "resid": 3, "hidden_two_t": 4, "slope": 5, "active_t": 6}
    held = dict(
        hidden_t=hidden_t, qkv=qkv, attn_t=attn_t, resid=resid, hidden_two_t=hidden_two_t,
        slope=slope, active_t=active_t,
    )
    for name in ("active_t", "slope"):
        fetch(index[name], held[name]).start()
    for part in range(8):
        down_load(part).start()
    for name in ("hidden_two_t", "resid", "attn_t", "qkv", "hidden_t"):
        fetch(index[name], held[name]).start()

    def got(name):
        fetch(index[name], held[name]).wait()

    row_valid = lax.broadcasted_iota(jnp.int32, (seq_len, 1), 0) < length[0]
    grad_low[...] = jnp.where(row_valid, cotangent[...].astype(wide), 0.0).astype(low)
    got("active_t")
    produce(0, active_t, grad_low, 0)
    got("slope")
    for part in range(8):
        down_load(part).wait()
    tile = 512

    def pre(n, carry):
        at = aligned(n, tile)
        back = outer_cols(grad_low[...], big[at])
        grad_pre[:, at] = (back * slope[:, at].astype(wide)).astype(low)
        return carry

    for n in range(0, ff // tile, 2):
        lax.fori_loop(n, n + 2, pre, 0)
        pump(1)
    for part in range(ff // D):
        up_load(part).start()
    got("hidden_two_t")
    produce(1, hidden_two_t, grad_pre, 2)
    for part in range(ff // D):
        up_load(part).wait()
        back = outer_cols(grad_pre[:, pl.ds(part * D, D)], big[pl.ds(part * D, D)])
        if part == 0:
            grad_hidden[...] = back
        else:
            grad_hidden[...] += back
        pump(1)
    for part in range(3):
        qkv_load(part).start()
    out_load().start()
    got("resid")
    pump(1)

    def norm_step(values, grads, gain, base, row, target):
        normed, inverse = norm_rows(values)
        for n, total in enumerate((grads * normed, grads)):
            sums = jnp.sum(total, axis=0, keepdims=True)
            rows = D // fsdp_size
            for to in range(fsdp_size):
                small_g[to, row + n : row + n + 1, :] = sums[:, to * rows : (to + 1) * rows]
        target[...] = base + norm_back(grads * gain, normed, inverse)

    small_g[...] = jnp.zeros_like(small_g)
    gain = vector_row(small_full, 2, fsdp_size)
    base = jnp.where(row_valid, cotangent[...].astype(wide), 0.0)
    norm_step(resid[...], grad_hidden[...], gain, base, 2, grad_resid)
    grad_low[...] = grad_resid[...].astype(low)
    pump(1)
    got("attn_t")
    produce(2, attn_t, grad_low, 2)
    out_load().wait()

    def attn_in(n, carry):
        at = aligned(n, 256)
        grad_attn[:, at] = outer_cols(
            grad_low[...], big[pl.ds(pl.multiple_of(3 * D + n * 256, 256), 256)]
        ).astype(low)
        return carry

    lax.fori_loop(0, D // 256, attn_in, 0)
    got("qkv")
    key_valid = lax.broadcasted_iota(jnp.int32, (1, seq_len), 1) < length[0]
    first_half = lax.broadcasted_iota(jnp.int32, (1, 128), 1) < HEAD_DIM
    halves = (first_half.astype(wide).astype(low), 1 - first_half.astype(wide).astype(low))
    pairs = D // 128
    factor = 1.0 / math.sqrt(HEAD_DIM)

    def attend(j, carry):
        queries, keys, values = (qkv[:, aligned(j + i * pairs, 128)] for i in range(3))
        grads = grad_attn[:, aligned(j, 128)]
        found = []
        for half in halves:
            probs = head_scores(queries * half, keys, key_valid)
            grad_probs = outer_cols(grads * half, values)
            row_dot = jnp.sum(probs * grad_probs, axis=-1, keepdims=True)
            scores = (probs * (grad_probs - row_dot)).astype(low)
            found.append(
                (
                    jnp.dot(scores, keys, preferred_element_type=wide) * factor,
                    inner_rows(scores, queries) * factor,
                    inner_rows(probs.astype(low), grads),
                )
            )
        for i in range(3):
            grad_pre[:, aligned(j + i * pairs, 128)] = jnp.where(
                first_half, found[0][i], found[1][i]
            ).astype(low)
        return carry

    for j in range(0, pairs, 2):
        lax.fori_loop(j, j + 2, attend, 0)
        pump(1)
    got("hidden_t")
    produce(3, hidden_t, grad_pre, 2)
    for part in range(3):
        qkv_load(part).wait()
    for part in range(3):
        total = outer_cols(grad_pre[:, pl.ds(part * D, D)], big[pl.ds(part * D, D)])
        if part == 0:
            grad_hidden[...] = total
        else:
            grad_hidden[...] += total
    gain = vector_row(small_full, 0, fsdp_size)
    norm_step(scenes[...].astype(wide), grad_hidden[...], gain, grad_resid[...], 0, grad_resid)
    input_grad[...] = grad_resid[...].astype(low)
    for k in range(1, fsdp_size):
        to = lax.rem(f + k, fsdp_size)
        go(send(small_g.at[to], small_a.at[k - 1], ss.at[k - 1], sr.at[k - 1], (d, to)))
    pump(2)
    total = small_g[f]
    for k in range(1, fsdp_size):
        arrived(small_a.at[k - 1], ss.at[k - 1], sr.at[k - 1], c_peer)
        total = total + small_a[k - 1]
    small_b[d] = total
    pump(2)
    for k in range(1, 4):
        go(send(small_b.at[d], small_b.at[d], us.at[k - 1], ur.at[k - 1], (d ^ k, f)))
    pump(4)
    for k in range(1, 4):
        arrived(small_b.at[d ^ k], us.at[k - 1], ur.at[k - 1], c_peer)
    small_out[...] = (small_b[0] + small_b[1]) + (small_b[2] + small_b[3])
    pump(len(order))
    for copy in pending:
        copy.wait_send()
    for i in range(max(0, count - slots_other), count):
        core_sends[i].wait_send()


def reduce_backward(fsdp_size, length, scenes, cotangent, small_full, saved, fulls):
    column = fsdp_size // 2
    seq_len = scenes.shape[0]
    ff = fulls[3].shape[0]
    low, wide = jnp.bfloat16, jnp.float32
    by_need = (fulls[3], fulls[2], fulls[1], fulls[0])
    chunks = chunk_list([(w.shape[0] // fsdp_size, w.shape[1]) for w in by_need])
    count = len(chunks)
    hbm = pl.BlockSpec(memory_space=pltpu.HBM)
    vmem = pl.BlockSpec(memory_space=pltpu.VMEM)
    smem = pl.BlockSpec(memory_space=pltpu.SMEM)
    dma = pltpu.SemaphoreType.DMA
    scratch = []
    for kind in ("sum", "one", "two", "zed", "fin"):
        for _, _, high, _, _, width in chunks:
            scratch.append(
                pltpu.VMEM(
                    {
                        "sum": (8, column * high, width),
                        "one": (2, 2, column * high, width),
                        "two": (2, column * high, width),
                        "zed": (2, column - 1, high, width),
                        "fin": (2, high, width),
                    }[kind],
                    low,
                )
            )
    tall = max(c[2] for c in chunks) * column
    broad = max(c[5] for c in chunks)
    scratch += [
        pltpu.VMEM((2, 8, tall, broad), low),
        pltpu.VMEM((2, 8, tall, broad), low),
        pltpu.VMEM((ff, D), low),
    ]
    scratch += [pltpu.VMEM(a.shape, a.dtype) for a in saved]
    scratch += [
        pltpu.VMEM((seq_len, D), low),
        pltpu.VMEM((seq_len, ff), low),
        pltpu.VMEM((seq_len, D), wide),
        pltpu.VMEM((seq_len, D), wide),
        pltpu.VMEM((seq_len, D), low),
        pltpu.VMEM((fsdp_size, 8, D // fsdp_size), wide),
        pltpu.VMEM((fsdp_size - 1, 8, D // fsdp_size), wide),
        pltpu.VMEM((4, 8, D // fsdp_size), wide),
    ]
    scratch += [dma((count,))] * 2 + [dma((count, 2, 2))] * 2 + [dma((count, 2))] * 2
    scratch += [dma((count, 2, column - 1))] * 2 + [dma((count, 2, 2))] * 2 + [dma((count, 2))] * 2
    scratch += [dma((count, 2))] + [dma((fsdp_size - 1,))] * 2 + [dma((3,))] * 2
    scratch += [dma((len(saved),)), dma((4, 8)), pltpu.SemaphoreType.REGULAR]
    shape = jax.ShapeDtypeStruct
    return pl.pallas_call(
        functools.partial(backward_kernel, fsdp_size, chunks),
        out_shape=[shape((w.shape[0] // fsdp_size, w.shape[1]), low) for w in by_need]
        + [shape((seq_len, D), low), shape((8, D // fsdp_size), wide)],
        in_specs=[smem, vmem, vmem, vmem] + [hbm] * (len(saved) + 4),
        out_specs=[hbm] * 4 + [vmem, vmem],
        scratch_shapes=scratch,
        compiler_params=pltpu.CompilerParams(
            collective_id=1, has_side_effects=True, vmem_limit_bytes=67043328
        ),
        name="reduce_backward",
    )(length, scenes, cotangent, small_full, *saved, *fulls)


def on_device_wide(
    scenes_in,
    scene_lengths,
    cotangent,
    qkv_weight,
    out_weight,
    up_weight,
    down_weight,
    gain_one,
    bias_one,
    gain_two,
    bias_two,
):
    params = (
        lax.all_gather(qkv_weight, "fsdp", axis=0, tiled=True),
        lax.all_gather(out_weight, "fsdp", axis=0, tiled=True),
        lax.all_gather(up_weight, "fsdp", axis=0, tiled=True),
        lax.all_gather(down_weight, "fsdp", axis=0, tiled=True),
        lax.all_gather(gain_one, "fsdp", axis=0, tiled=True),
        lax.all_gather(bias_one, "fsdp", axis=0, tiled=True),
        lax.all_gather(gain_two, "fsdp", axis=0, tiled=True),
        lax.all_gather(bias_two, "fsdp", axis=0, tiled=True),
    )
    inputs = scenes_in[0].astype(jnp.float32)
    seq_len = inputs.shape[0]
    positions = jnp.arange(seq_len, dtype=jnp.int32)
    key_valid = positions < scene_lengths[0]
    row_mask = key_valid.astype(jnp.float32)[:, None]
    saved = forward_pass(inputs, key_valid, params)
    layer_out = (saved[0] * row_mask).astype(jnp.bfloat16)[None]
    grad_out = cotangent[0].astype(jnp.float32) * row_mask
    params_back = (
        lax.all_gather(qkv_weight, "fsdp", axis=0, tiled=True),
        lax.all_gather(out_weight, "fsdp", axis=0, tiled=True),
        lax.all_gather(up_weight, "fsdp", axis=0, tiled=True),
        lax.all_gather(down_weight, "fsdp", axis=0, tiled=True),
        lax.all_gather(gain_one, "fsdp", axis=0, tiled=True),
        lax.all_gather(bias_one, "fsdp", axis=0, tiled=True),
        lax.all_gather(gain_two, "fsdp", axis=0, tiled=True),
        lax.all_gather(bias_two, "fsdp", axis=0, tiled=True),
    )
    saved_back = forward_pass(inputs, key_valid, params_back)
    grad_resid, up_grad, down_grad, gain_two_grad, bias_two_grad = mlp_back(
        grad_out, saved_back, params_back
    )
    input_grad, qkv_grad, out_grad, gain_one_grad, bias_one_grad = attn_back(
        grad_resid, saved_back, params_back
    )
    shares = (
        lax.psum_scatter(qkv_grad, "fsdp", scatter_dimension=0, tiled=True),
        lax.psum_scatter(out_grad, "fsdp", scatter_dimension=0, tiled=True),
        lax.psum_scatter(up_grad, "fsdp", scatter_dimension=0, tiled=True),
        lax.psum_scatter(down_grad, "fsdp", scatter_dimension=0, tiled=True),
        lax.psum_scatter(gain_one_grad, "fsdp", scatter_dimension=0, tiled=True),
        lax.psum_scatter(bias_one_grad, "fsdp", scatter_dimension=0, tiled=True),
        lax.psum_scatter(gain_two_grad, "fsdp", scatter_dimension=0, tiled=True),
        lax.psum_scatter(bias_two_grad, "fsdp", scatter_dimension=0, tiled=True),
    )
    summed = (
        lax.psum(shares[0].astype(jnp.bfloat16), "dp").astype(jnp.float32),
        lax.psum(shares[1].astype(jnp.bfloat16), "dp").astype(jnp.float32),
        lax.psum(shares[2].astype(jnp.bfloat16), "dp").astype(jnp.float32),
        lax.psum(shares[3].astype(jnp.bfloat16), "dp").astype(jnp.float32),
        lax.psum(shares[4].astype(jnp.bfloat16), "dp").astype(jnp.float32),
        lax.psum(shares[5].astype(jnp.bfloat16), "dp").astype(jnp.float32),
        lax.psum(shares[6].astype(jnp.bfloat16), "dp").astype(jnp.float32),
        lax.psum(shares[7].astype(jnp.bfloat16), "dp").astype(jnp.float32),
    )
    qkv_total, out_total, up_total, down_total = (summed[0], summed[1], summed[2], summed[3])
    gain_one_total, bias_one_total, gain_two_total, bias_two_total = (
        summed[4],
        summed[5],
        summed[6],
        summed[7],
    )
    input_out = input_grad.astype(jnp.bfloat16)[None]
    return (
        layer_out,
        input_out,
        qkv_total,
        out_total,
        up_total,
        down_total,
        gain_one_total,
        bias_one_total,
        gain_two_total,
        bias_two_total,
    )


def on_device(
    scenes_in,
    scene_lengths,
    cotangent,
    qkv_weight,
    out_weight,
    up_weight,
    down_weight,
    gain_one,
    bias_one,
    gain_two,
    bias_two,
):
    rows = gain_one.shape[0]
    fsdp_size = D // rows
    small = jnp.stack([gain_one, bias_one, gain_two, bias_two])
    small = jnp.pad(small, ((0, 12), (0, 0)))
    results = gather_forward(
        fsdp_size,
        scene_lengths,
        scenes_in[0],
        (qkv_weight, out_weight, up_weight, down_weight),
        small,
    )
    fulls, layer_out, small_full, saved = results[:4], results[4], results[5], results[6:]
    down_sum, up_sum, out_sum, qkv_sum, input_grad, small_sum = reduce_backward(
        fsdp_size,
        scene_lengths,
        scenes_in[0],
        cotangent[0],
        small_full,
        saved,
        fulls,
    )
    wide = jnp.float32
    return (
        layer_out[None],
        input_grad[None],
        qkv_sum.astype(wide),
        out_sum.astype(wide),
        up_sum.astype(wide),
        down_sum.astype(wide),
        small_sum[0],
        small_sum[1],
        small_sum[2],
        small_sum[3],
    )


def solution(mesh):
    placed = (
        P(("dp", "fsdp"), None, None),
        P(("dp", "fsdp")),
        P(("dp", "fsdp"), None, None),
        P("fsdp", None),
        P("fsdp", None),
        P("fsdp", None),
        P("fsdp", None),
        P("fsdp"),
        P("fsdp"),
        P("fsdp"),
        P("fsdp"),
    )
    body = on_device if mesh.shape["dp"] == 4 and mesh.shape["fsdp"] == 8 else on_device_wide
    return jax.shard_map(
        body,
        mesh=mesh,
        in_specs=placed,
        out_specs=(
            P(("dp", "fsdp"), None, None),
            P(("dp", "fsdp"), None, None),
            P("fsdp", None),
            P("fsdp", None),
            P("fsdp", None),
            P("fsdp", None),
            P("fsdp"),
            P("fsdp"),
            P("fsdp"),
            P("fsdp"),
        ),
        check_vma=False,
    )
```

```python
import functools
import math

import jax
import jax.numpy as jnp
from jax import lax
from jax.experimental import pallas as pl
from jax.experimental.pallas import tpu as pltpu
from jax.sharding import PartitionSpec as P

D = 1024
HEADS = 16
HEAD_DIM = 64


epsilon = 1e-05


def norm_rows(values_in):
    row_mean = jnp.mean(values_in, axis=-1, keepdims=True)
    centered = values_in - row_mean
    variance = jnp.mean(centered * centered, axis=-1, keepdims=True)
    inverse = lax.rsqrt(variance + epsilon)
    return (centered * inverse, inverse)


def norm_back(grad_normed, normed, inverse):
    first_mean = jnp.mean(grad_normed, axis=-1, keepdims=True)
    second_mean = jnp.mean(grad_normed * normed, axis=-1, keepdims=True)
    return inverse * (grad_normed - first_mean - normed * second_mean)


def inner_rows(left, right):
    return lax.dot_general(
        left, right, (((0,), (0,)), ((), ())), preferred_element_type=jnp.float32
    )


def outer_cols(left, right):
    return lax.dot_general(
        left, right, (((1,), (1,)), ((), ())), preferred_element_type=jnp.float32
    )


def forward_pass(inputs, key_valid, params):
    qkv_weight, out_weight, up_weight, down_weight, gain_one, bias_one, gain_two, bias_two = params
    seq_len = inputs.shape[0]
    normed_one, inverse_one = norm_rows(inputs)
    hidden_one = (normed_one * gain_one.astype(jnp.float32) + bias_one.astype(jnp.float32)).astype(
        jnp.bfloat16
    )
    qkv_low = jnp.dot(hidden_one, qkv_weight, preferred_element_type=jnp.float32).astype(
        jnp.bfloat16
    )
    split_view = qkv_low.reshape(seq_len, 3, HEADS, HEAD_DIM)
    queries = split_view[:, 0]
    keys_all = split_view[:, 1]
    values_all = split_view[:, 2]
    scale_factor = 1.0 / math.sqrt(HEAD_DIM)
    scores = (
        jnp.einsum("qhd,khd->hqk", queries, keys_all, preferred_element_type=jnp.float32)
        * scale_factor
    )
    masked = jnp.where(key_valid[None, None, :], scores, -1e30)
    highest = jnp.max(masked, axis=-1, keepdims=True)
    expont = jnp.exp(masked - highest)
    probs = expont / jnp.sum(expont, axis=-1, keepdims=True)
    probs_low = probs.astype(jnp.bfloat16)
    attended = jnp.einsum("hqk,khd->qhd", probs_low, values_all, preferred_element_type=jnp.float32)
    attn_low = attended.reshape(seq_len, D).astype(jnp.bfloat16)
    resid_one = inputs + jnp.dot(attn_low, out_weight, preferred_element_type=jnp.float32)
    normed_two, inverse_two = norm_rows(resid_one)
    hidden_two = (normed_two * gain_two.astype(jnp.float32) + bias_two.astype(jnp.float32)).astype(
        jnp.bfloat16
    )
    hidden_pre = jnp.dot(hidden_two, up_weight, preferred_element_type=jnp.float32)
    activated = jax.nn.gelu(hidden_pre, approximate=False).astype(jnp.bfloat16)
    result = resid_one + jnp.dot(activated, down_weight, preferred_element_type=jnp.float32)
    return (
        result,
        normed_one,
        inverse_one,
        hidden_one,
        queries,
        keys_all,
        values_all,
        probs,
        probs_low,
        attn_low,
        normed_two,
        inverse_two,
        hidden_two,
        hidden_pre,
        activated,
    )


def mlp_back(grad_out, saved, params):
    up_weight, down_weight, gain_two = (params[2], params[3], params[6])
    normed_two, inverse_two, hidden_two, hidden_pre, activated = (
        saved[10],
        saved[11],
        saved[12],
        saved[13],
        saved[14],
    )
    grad_low = grad_out.astype(jnp.bfloat16)
    down_grad = inner_rows(activated, grad_low)
    grad_act = outer_cols(grad_low, down_weight)
    cumul = 0.5 * (1.0 + lax.erf(hidden_pre * (1.0 / math.sqrt(2.0))))
    density = jnp.exp(-0.5 * hidden_pre * hidden_pre) * (1.0 / math.sqrt(2.0 * math.pi))
    grad_pre = (grad_act * (cumul + hidden_pre * density)).astype(jnp.bfloat16)
    up_grad = inner_rows(hidden_two, grad_pre)
    grad_hidden = outer_cols(grad_pre, up_weight)
    gain_two_grad = jnp.sum(grad_hidden * normed_two, axis=0)
    bias_two_grad = jnp.sum(grad_hidden, axis=0)
    grad_resid = grad_out + norm_back(
        grad_hidden * gain_two.astype(jnp.float32), normed_two, inverse_two
    )
    return (grad_resid, up_grad, down_grad, gain_two_grad, bias_two_grad)


def attn_back(grad_resid, saved, params):
    qkv_weight, out_weight, gain_one = (params[0], params[1], params[4])
    normed_one, inverse_one, hidden_one = (saved[1], saved[2], saved[3])
    queries, keys_all, values_all, probs, probs_low, attn_low = (
        saved[4],
        saved[5],
        saved[6],
        saved[7],
        saved[8],
        saved[9],
    )
    seq_len = grad_resid.shape[0]
    scale_factor = 1.0 / math.sqrt(HEAD_DIM)
    resid_low = grad_resid.astype(jnp.bfloat16)
    out_grad = inner_rows(attn_low, resid_low)
    grad_attn = (
        outer_cols(resid_low, out_weight).astype(jnp.bfloat16).reshape(seq_len, HEADS, HEAD_DIM)
    )
    grad_probs = jnp.einsum(
        "qhd,khd->hqk", grad_attn, values_all, preferred_element_type=jnp.float32
    )
    row_dot = jnp.sum(probs * grad_probs, axis=-1, keepdims=True)
    grad_scores = (probs * (grad_probs - row_dot)).astype(jnp.bfloat16)
    grad_values = jnp.einsum(
        "hqk,qhd->khd", probs_low, grad_attn, preferred_element_type=jnp.float32
    )
    grad_queries = (
        jnp.einsum("hqk,khd->qhd", grad_scores, keys_all, preferred_element_type=jnp.float32)
        * scale_factor
    )
    grad_keys = (
        jnp.einsum("hqk,qhd->khd", grad_scores, queries, preferred_element_type=jnp.float32)
        * scale_factor
    )
    grad_qkv = (
        jnp.stack([grad_queries, grad_keys, grad_values], axis=1)
        .reshape(seq_len, 3 * D)
        .astype(jnp.bfloat16)
    )
    qkv_grad = inner_rows(hidden_one, grad_qkv)
    grad_hidden = outer_cols(grad_qkv, qkv_weight)
    gain_one_grad = jnp.sum(grad_hidden * normed_one, axis=0)
    bias_one_grad = jnp.sum(grad_hidden, axis=0)
    input_grad = grad_resid + norm_back(
        grad_hidden * gain_one.astype(jnp.float32), normed_one, inverse_one
    )
    return (input_grad, qkv_grad, out_grad, gain_one_grad, bias_one_grad)


MESH_ID = pl.DeviceIdType.MESH


def aligned(index, size):
    return pl.ds(pl.multiple_of(index * size, size), size)


def greet(dp_index, fsdp_index, fsdp_size):
    barrier = pltpu.get_barrier_semaphore()
    peers = [(dp_index ^ 1, fsdp_index), (dp_index ^ 2, fsdp_index), (dp_index ^ 3, fsdp_index)]
    peers += [(dp_index, lax.rem(fsdp_index + k, fsdp_size)) for k in range(1, fsdp_size)]
    for peer in peers:
        pl.semaphore_signal(barrier, inc=1, device_id=peer, device_id_type=MESH_ID)
    pl.semaphore_wait(barrier, len(peers))


def send(src, dst, send_sem, recv_sem, device):
    return pltpu.make_async_remote_copy(
        src_ref=src,
        dst_ref=dst,
        send_sem=send_sem,
        recv_sem=recv_sem,
        device_id=device,
        device_id_type=MESH_ID,
    )


def gelu_parts(u):
    cumul = 0.5 * (1.0 + lax.erf(u * (1.0 / math.sqrt(2.0))))
    density = jnp.exp(-0.5 * u * u) * (1.0 / math.sqrt(2.0 * math.pi))
    return u * cumul, cumul + u * density


def head_scores(q_head, keys, key_valid):
    scores = outer_cols(q_head, keys) * (1.0 / math.sqrt(HEAD_DIM))
    masked = jnp.where(key_valid, scores, -1e30)
    expont = jnp.exp(masked - jnp.max(masked, axis=-1, keepdims=True))
    return expont / jnp.sum(expont, axis=-1, keepdims=True)


def transposed(target, source, fsdp_size):
    rows = target.shape[2]

    def body(n, carry):
        target[lax.rem(n, 2), lax.div(n, 2)] = jnp.transpose(source[:, aligned(n, rows)])
        return carry

    lax.fori_loop(0, fsdp_size, body, 0)


SLOTS = 2


def chunk_list(shapes):
    chunks = []
    for piece, (rows, span) in enumerate(shapes):
        part = span // 8
        high = min(rows, 128)
        width = 256 if part % 256 == 0 else 128
        for row in range(0, rows, high):
            for col in range(0, part, width):
                chunks.append((piece, row, high, part, col, width))
    return chunks


def layer_kernel(fsdp_size, chunks, *refs):
    pieces = 4
    count = len(chunks)
    column = fsdp_size // 2
    low, wide = jnp.bfloat16, jnp.float32
    length, scenes, cotangent = refs[:3]
    shards = refs[3:7]
    small = refs[7]
    fulls = refs[8:12]
    outs = refs[12:16]
    layer_out, input_grad, small_out = refs[16:19]
    rest = refs[19:]
    sum_b, one_b, two_b, zed_b, fin_b = (rest[i * count : (i + 1) * count] for i in range(5))
    rest = rest[5 * count :]
    other_b, core_b, big, small_full, hidden, hidden_t, qkv, attn, attn_t = rest[:9]
    resid, hidden_two_t, wide_low, slope, active_t, grad_low, grad_hidden, grad_resid = rest[9:17]
    small_g, small_a, small_b = rest[17:20]
    own_sem, az, bz, ax, bx, ay, by, ad, bd, ae, be, ac, bc, sv, rv = rest[20:35]
    (cs, cr, os_, or_, ts, tr, zs, zr, fs, fr, gs, gr, out_sem, ss, sr, us, ur) = rest[35:52]
    load_sem, credit = rest[52:]
    d = lax.axis_index("dp")
    f = lax.axis_index("fsdp")
    core = lax.rem(f, 2)
    place = lax.div(f, 2)
    bits = (lax.rem(d, 2), lax.div(d, 2))
    x_peer, y_peer, c_peer = (d ^ 1, f), (d ^ 2, f), (d, f ^ 1)
    peers = (x_peer, y_peer)
    seq_len = scenes.shape[0]
    ff = wide_low.shape[1]
    slots_other, slots_core = other_b.shape[0], core_b.shape[0]
    pending = []
    core_sends = {}

    def go(copy):
        copy.start()
        pending.append(copy)

    def arrived(view, send_sem, recv_sem, device):
        send(view, view, send_sem, recv_sem, device).wait_recv()

    def block(piece, place_from, quarter, half=None):
        rows = shards[piece].shape[0]
        span = shards[piece].shape[1] // 4
        row_part = aligned(place_from * 2 + core, rows)
        if half is None:
            return fulls[piece].at[row_part, aligned(quarter, span)]
        return fulls[piece].at[row_part, aligned(quarter * 2 + half, span // 2)]

    def to_partner(piece, view):
        send(view, view, ac.at[piece], bc.at[piece], c_peer).start()

    def source(k):
        return lax.rem(place - k + column, column)

    def from_column(piece, k):
        at = (piece, k - 1)
        view = block(piece, source(k), d)
        arrived(view, az.at[at], bz.at[at], x_peer)
        go(send(view, view, ax.at[at], bx.at[at], x_peer))
        go(send(view, view, ay.at[at], by.at[at], y_peer))
        to_partner(piece, view)

    def from_sides(piece, k):
        at = (piece, k - 1)
        view = block(piece, source(k), d ^ 1)
        arrived(view, ax.at[at], bx.at[at], x_peer)
        part = block(piece, source(k), d ^ 1, 0)
        go(send(part, part, ad.at[at], bd.at[at], y_peer))
        to_partner(piece, view)
        view = block(piece, source(k), d ^ 2)
        arrived(view, ay.at[at], by.at[at], y_peer)
        part = block(piece, source(k), d ^ 2, 1)
        go(send(part, part, ae.at[at], be.at[at], x_peer))
        to_partner(piece, view)

    def from_corner(piece, k):
        at = (piece, k - 1)
        for half, (a, b, peer) in enumerate(((ad, bd, y_peer), (ae, be, x_peer))):
            part = block(piece, source(k), d ^ 3, half)
            arrived(part, a.at[at], b.at[at], peer)
            to_partner(piece, part)

    def from_partner(piece):
        rows = shards[piece].shape[0]
        view = fulls[piece].at[pl.ds(0, rows * column)]
        send(view, view, ac.at[piece], bc.at[piece], c_peer).wait()

    def loads(piece):
        if piece == 3:
            parts = [(fulls[3].at[pl.ds(n * D, D)], pl.ds(n * D, D)) for n in range(ff // D)]
        elif piece == 1:
            parts = [(fulls[1], pl.ds(3 * D, D))]
        else:
            parts = [
                (fulls[piece].at[:, pl.ds(n * D, D)], pl.ds(n * D, D))
                for n in range(fulls[piece].shape[1] // D)
            ]
        return [
            pltpu.make_async_copy(view, big.at[at], load_sem.at[piece, n])
            for n, (view, at) in enumerate(parts)
        ]

    def own_parts(piece, back):
        rows, span = shards[piece].shape
        first_row = sum(s.shape[0] * (s.shape[1] // D) for s in shards[:piece])
        parts = []
        for n in range(span // D):
            stage = big.at[pl.ds(first_row + n * rows, rows)]
            cols = pl.ds(n * D, D)
            whole = fulls[piece].at[aligned(f, rows), cols]
            ends = (stage, whole) if back else (shards[piece].at[:, cols], stage)
            parts.append(pltpu.make_async_copy(*ends, own_sem.at[int(back), piece, n]))
        return parts

    every = range(1, column)
    blocks = [(piece, k) for piece in range(pieces) for k in every]
    gather_order = []
    for n in range(len(blocks) + 4):
        for action, lag in ((from_column, 0), (from_sides, 1), (from_corner, 2)):
            if 0 <= n - lag < len(blocks):
                gather_order.append((action, *blocks[n - lag]))
    gathered = []

    def gather_step(limit=1):
        for _ in range(limit):
            if len(gathered) < len(gather_order):
                action, piece, k = gather_order[len(gathered)]
                gathered.append(1)
                action(piece, k)

    def gather_to(action, piece):
        last_one = gather_order.index((action, piece, column - 1))
        while len(gathered) <= last_one:
            gather_step()

    def slot_view(ref, slot, i):
        _, _, high, _, _, width = chunks[i]
        return ref.at[slot, :, pl.ds(0, column * high), pl.ds(0, width)]

    def grams(i, left_t, right):
        piece, row, high, part, col, width = chunks[i]
        slot = i % slots_other
        if i >= slots_other:
            core_sends[i - slots_other].wait_send()
        step = 2 if width == part and width == 128 else 1

        def fill(half, target):
            left = left_t[half, :, pl.ds(row, high), :].reshape(column * high, seq_len)

            def body(n, carry):
                start = pl.multiple_of(n * step * part + col, 128)
                found = jnp.dot(
                    left, right[:, pl.ds(start, step * width)], preferred_element_type=wide
                ).astype(low)
                for m in range(step):
                    target[n * step + m] = found[:, m * width : (m + 1) * width]
                return carry

            lax.fori_loop(0, 8 // step, body, 0)

        fill(1 - core, slot_view(other_b, slot, i))
        if i >= slots_core:
            pl.semaphore_wait(credit, 1)
        fill(core, sum_b[i])
        copy = send(
            slot_view(other_b, slot, i),
            slot_view(core_b, i % slots_core, i),
            cs.at[i],
            cr.at[i],
            c_peer,
        )
        copy.start()
        core_sends[i] = copy

    def add_into(target, other):
        rows = target.shape[0]
        strip = 64

        def body(n, carry):
            at = aligned(n, strip)
            target[at] = (target[at].astype(wide) + other[at].astype(wide)).astype(low)
            return carry

        lax.fori_loop(0, rows // strip, body, 0)

    def far_quarter(half, b):
        if half == 0:
            return (1 - bits[0]) + 2 * b
        return b + 2 * (1 - bits[1])

    def near_quarter(half, b):
        if half == 0:
            return bits[0] + 2 * b
        return b + 2 * bits[1]

    def pair(i):
        view = slot_view(core_b, i % slots_core, i)
        arrived(view, cs.at[i], cr.at[i], c_peer)

        def add(quarter, half):
            add_into(sum_b[i].at[quarter * 2 + half], view.at[quarter * 2 + half])

        for b in range(2):
            for half in range(2):
                add(far_quarter(half, b), half)
            for half in range(2):
                go(
                    send(
                        sum_b[i].at[far_quarter(half, b) * 2 + half],
                        one_b[i].at[half, b],
                        os_.at[i, half, b],
                        or_.at[i, half, b],
                        peers[half],
                    )
                )
        for b in range(2):
            for half in range(2):
                add(near_quarter(half, b), half)
        if i + slots_core < count:
            pl.semaphore_signal(credit, inc=1, device_id=c_peer, device_id_type=MESH_ID)

    def first(i):
        for half in range(2):
            for b in range(2):
                arrived(one_b[i].at[half, b], os_.at[i, half, b], or_.at[i, half, b], peers[half])
                add_into(sum_b[i].at[near_quarter(half, b) * 2 + half], one_b[i].at[half, b])
            other = d ^ 2 if half == 0 else d ^ 1
            go(
                send(
                    sum_b[i].at[other * 2 + half],
                    two_b[i].at[half],
                    ts.at[i, half],
                    tr.at[i, half],
                    peers[1 - half],
                )
            )

    def second(i):
        _, _, high, _, _, _ = chunks[i]
        for half in range(2):
            arrived(two_b[i].at[half], ts.at[i, half], tr.at[i, half], peers[1 - half])
            mine = sum_b[i].at[d * 2 + half]
            add_into(mine, two_b[i].at[half])
            for k in range(1, column):
                to = lax.rem(place + k, column)
                go(
                    send(
                        mine.at[aligned(to, high)],
                        zed_b[i].at[half, k - 1],
                        zs.at[i, half, k - 1],
                        zr.at[i, half, k - 1],
                        (d, to * 2 + core),
                    )
                )

    def result(i, quarter, half):
        piece, row, high, part, col, width = chunks[i]
        start = pl.multiple_of((quarter * 2 + half) * part + col, 128)
        return outs[piece].at[pl.ds(row, high), pl.ds(start, width)]

    def last(i):
        _, _, high, _, _, _ = chunks[i]
        for half in range(2):
            for k in range(1, column):
                at = (i, half, k - 1)
                arrived(zed_b[i].at[half, k - 1], zs.at[at], zr.at[at], c_peer)
            total = sum_b[i][d * 2 + half, aligned(place, high)].astype(wide)
            for k in range(1, column):
                total = total + zed_b[i][half, k - 1].astype(wide)
            fin_b[i][half] = total.astype(low)
        for half in range(2):
            mine = result(i, d, half)
            pltpu.make_async_copy(fin_b[i].at[half], mine, out_sem.at[i, half]).start()
            for axis in range(2):
                at = (i, half, axis)
                go(send(fin_b[i].at[half], mine, fs.at[at], fr.at[at], peers[axis]))

    def spread(i):
        for half in range(2):
            for axis in range(2):
                at = (i, half, axis)
                view = result(i, d ^ (1 + axis), half)
                arrived(view, fs.at[at], fr.at[at], peers[axis])
                if half == axis:
                    go(send(view, view, gs.at[i, half], gr.at[i, half], peers[1 - axis]))

    def finish(i):
        for half in range(2):
            view = result(i, d ^ 3, half)
            arrived(view, gs.at[i, half], gr.at[i, half], peers[1 - half])
            pltpu.make_async_copy(fin_b[i].at[half], result(i, d, half), out_sem.at[i, half]).wait()

    stages = (first, second, last, spread, finish)
    order = []
    for step in range(count + len(stages) - 1):
        for n, stage in enumerate(stages):
            if 0 <= step - n < count:
                order.append((stage, step - n))
    done = []
    waiting = []
    paired = []

    def pair_up(keep=0):
        while len(waiting) > keep:
            i = waiting.pop(0)
            pair(i)
            paired.append(i)

    def advance(limit):
        for _ in range(limit):
            if len(done) < len(order) and order[len(done)][1] in paired:
                stage, i = order[len(done)]
                done.append(1)
                stage(i)

    def pump(limit=1):
        pair_up()
        advance(limit)

    def produce(some, left_t, right, limit, keep=1):
        for i in some:
            pair_up(slots_core - 1)
            grams(i, left_t, right)
            waiting.append(i)
            pair_up(keep)
            advance(limit)

    by_piece = [[i for i in range(count) if chunks[i][0] == piece] for piece in range(pieces)]

    greet(d, f, fsdp_size)
    small_rows = small.shape[0]
    for k in range(1, fsdp_size):
        to = lax.rem(f + k, fsdp_size)
        go(send(small, small_full.at[aligned(f, small_rows)], sv.at[k - 1], rv.at[k - 1], (d, to)))
    own_small = pltpu.make_async_copy(
        small, small_full.at[aligned(f, small_rows)], own_sem.at[0, 0, pieces]
    )
    own_small.start()
    for piece in range(pieces):
        rows, span = shards[piece].shape
        for k in every:
            go(
                send(
                    shards[piece].at[:, aligned(d, span // 4)],
                    block(piece, place, d),
                    az.at[piece, k - 1],
                    bz.at[piece, k - 1],
                    (d, lax.rem(place + k, column) * 2 + core),
                )
            )
        own = fulls[piece].at[aligned(f, rows)]
        send(shards[piece], own, ac.at[piece], bc.at[piece], c_peer).start()
        for copy in own_parts(piece, False):
            copy.start()
    for piece in range(pieces):
        for copy in own_parts(piece, False):
            copy.wait()
        for copy in own_parts(piece, True):
            copy.start()

    normed_one, _ = norm_rows(scenes[...].astype(wide))
    for k in range(1, fsdp_size):
        view = small_full.at[aligned(lax.rem(f - k + fsdp_size, fsdp_size), small_rows)]
        arrived(view, sv.at[k - 1], rv.at[k - 1], c_peer)
    own_small.wait()

    def vector(row):
        values = small_full[...].astype(wide)
        at = range(row, small_rows * fsdp_size, small_rows)
        return jnp.concatenate([values[n : n + 1] for n in at], axis=1)

    hidden[...] = (normed_one * vector(0) + vector(1)).astype(low)
    gather_step(2)
    transposed(hidden_t, hidden, fsdp_size)
    for piece in range(pieces):
        for copy in own_parts(piece, True):
            copy.wait()
    gather_to(from_corner, 0)
    gather_step(3)
    from_partner(0)
    for copy in loads(0):
        copy.start()
    gather_step(1)
    for copy in loads(0):
        copy.wait()

    def project(n, carry):
        cols = aligned(n, 512)
        rows = aligned(lax.div(n, D // 512), D)
        weight = big[rows, aligned(lax.rem(n, D // 512), 512)]
        qkv[:, cols] = jnp.dot(hidden[...], weight, preferred_element_type=wide).astype(low)
        return carry

    tiles = qkv.shape[1] // 512
    lax.fori_loop(0, tiles // 2, project, 0)
    gather_step(2)
    lax.fori_loop(tiles // 2, tiles, project, 0)
    gather_step(2)
    key_valid = lax.broadcasted_iota(jnp.int32, (1, seq_len), 1) < length[0]
    row_valid = lax.broadcasted_iota(jnp.int32, (seq_len, 1), 0) < length[0]
    first_half = lax.broadcasted_iota(jnp.int32, (1, 128), 1) < HEAD_DIM
    halves = (first_half.astype(wide).astype(low), 1 - first_half.astype(wide).astype(low))
    pairs = D // 128

    def attend(j, carry):
        queries, keys, values = (qkv[:, aligned(j + i * pairs, 128)] for i in range(3))
        found = []
        for half in halves:
            probs = head_scores(queries * half, keys, key_valid)
            found.append(jnp.dot(probs.astype(low), values, preferred_element_type=wide))
        attn[:, aligned(j, 128)] = jnp.where(first_half, found[0], found[1]).astype(low)
        return carry

    for j in range(0, pairs, 2):
        lax.fori_loop(j, j + 2, attend, 0)
        gather_step(2)
    transposed(attn_t, attn, fsdp_size)
    gather_to(from_corner, 1)
    gather_step(1)
    from_partner(1)
    for copy in loads(1):
        copy.start()
    for copy in loads(1):
        copy.wait()

    def second_in(n, carry):
        cols = aligned(n, 512)
        resid[:, cols] = scenes[:, cols].astype(wide) + jnp.dot(
            attn[...], big[pl.ds(3 * D, D), cols], preferred_element_type=wide
        )
        return carry

    lax.fori_loop(0, D // 512, second_in, 0)
    normed_two, _ = norm_rows(resid[...])
    hidden[...] = (normed_two * vector(2) + vector(3)).astype(low)
    transposed(hidden_two_t, hidden, fsdp_size)
    gather_to(from_corner, 2)
    gather_step(2)
    from_partner(2)
    for copy in loads(2):
        copy.start()
    span = D // 256

    def expand(n, carry):
        cols = aligned(n, 256)
        rows = aligned(lax.div(n, span), D)
        weight = big[rows, aligned(lax.rem(n, span), 256)]
        acts, grads = gelu_parts(jnp.dot(hidden[...], weight, preferred_element_type=wide))
        wide_low[:, cols] = acts.astype(low)
        slope[:, cols] = grads.astype(low)
        return carry

    for part, copy in enumerate(loads(2)):
        copy.wait()
        lax.fori_loop(part * span, (part + 1) * span, expand, 0)
        gather_step(2)
    transposed(active_t, wide_low, fsdp_size)
    grad_low[...] = jnp.where(row_valid, cotangent[...].astype(wide), 0.0).astype(low)
    early = by_piece[0][: slots_core - 1]
    produce(early, active_t, grad_low, 0, slots_core)
    gather_to(from_sides, pieces - 1)
    pair_up()
    gather_to(from_corner, pieces - 1)
    produce(by_piece[0][len(early) :][:1], active_t, grad_low, 0)
    from_partner(3)
    for copy in loads(3):
        copy.start()
    produce(by_piece[0][len(early) + 1 :], active_t, grad_low, 0)
    for part, copy in enumerate(loads(3)):
        copy.wait()
        at = pl.ds(part * D, D)
        term = jnp.dot(wide_low[:, at], big[at], preferred_element_type=wide)
        if part == 0:
            grad_hidden[...] = resid[...] + term
        else:
            grad_hidden[...] += term
        pair_up()
    layer_out[...] = jnp.where(row_valid, grad_hidden[...], 0.0).astype(low)
    pump(1)

    tile = 512

    def pre(n, carry):
        at = aligned(n, tile)
        back = outer_cols(grad_low[...], big[at])
        wide_low[:, at] = (back * slope[:, at].astype(wide)).astype(low)
        return carry

    for n in range(0, ff // tile, 2):
        lax.fori_loop(n, n + 2, pre, 0)
        pump(1)
    for copy in loads(2):
        copy.start()
    produce(by_piece[1], hidden_two_t, wide_low, 2)
    for part, copy in enumerate(loads(2)):
        copy.wait()
        back = outer_cols(wide_low[:, pl.ds(part * D, D)], big[pl.ds(part * D, D)])
        if part == 0:
            grad_hidden[...] = back
        else:
            grad_hidden[...] += back
        pump(1)
    for piece in (1, 0):
        for copy in loads(piece):
            copy.start()
    pump(1)

    def norm_step(values, grads, gain, base, row):
        normed, inverse = norm_rows(values)
        rows = D // fsdp_size
        for n, total in enumerate((grads * normed, grads)):
            sums = jnp.sum(total, axis=0, keepdims=True)
            for to in range(fsdp_size):
                small_g[to, row + n : row + n + 1, :] = sums[:, to * rows : (to + 1) * rows]
        return base + norm_back(grads * gain, normed, inverse)

    small_g[...] = jnp.zeros_like(small_g)
    base = jnp.where(row_valid, cotangent[...].astype(wide), 0.0)
    grad_resid[...] = norm_step(resid[...], grad_hidden[...], vector(2), base, 2)
    grad_low[...] = grad_resid[...].astype(low)
    pump(1)
    produce(by_piece[2], attn_t, grad_low, 2)
    for copy in loads(1):
        copy.wait()

    def attn_in(n, carry):
        rows = pl.ds(pl.multiple_of(3 * D + n * 256, 256), 256)
        attn[:, aligned(n, 256)] = outer_cols(grad_low[...], big[rows]).astype(low)
        return carry

    lax.fori_loop(0, D // 256, attn_in, 0)
    pump(1)
    factor = 1.0 / math.sqrt(HEAD_DIM)

    def attend_back(j, carry):
        queries, keys, values = (qkv[:, aligned(j + i * pairs, 128)] for i in range(3))
        grads = attn[:, aligned(j, 128)]
        found = []
        for half in halves:
            probs = head_scores(queries * half, keys, key_valid)
            grad_probs = outer_cols(grads * half, values)
            row_dot = jnp.sum(probs * grad_probs, axis=-1, keepdims=True)
            scores = (probs * (grad_probs - row_dot)).astype(low)
            found.append(
                (
                    jnp.dot(scores, keys, preferred_element_type=wide) * factor,
                    inner_rows(scores, queries) * factor,
                    inner_rows(probs.astype(low), grads),
                )
            )
        for i in range(3):
            wide_low[:, aligned(j + i * pairs, 128)] = jnp.where(
                first_half, found[0][i], found[1][i]
            ).astype(low)
        return carry

    for j in range(0, pairs, 2):
        lax.fori_loop(j, j + 2, attend_back, 0)
        pump(1)
    produce(by_piece[3], hidden_t, wide_low, 2)
    for part, copy in enumerate(loads(0)):
        copy.wait()
        total = outer_cols(wide_low[:, pl.ds(part * D, D)], big[pl.ds(part * D, D)])
        if part == 0:
            grad_hidden[...] = total
        else:
            grad_hidden[...] += total
    pump(1)
    total = norm_step(scenes[...].astype(wide), grad_hidden[...], vector(0), grad_resid[...], 0)
    input_grad[...] = total.astype(low)
    for k in range(1, fsdp_size):
        to = lax.rem(f + k, fsdp_size)
        go(send(small_g.at[to], small_a.at[k - 1], ss.at[k - 1], sr.at[k - 1], (d, to)))
    pump(2)
    total = small_g[f]
    for k in range(1, fsdp_size):
        arrived(small_a.at[k - 1], ss.at[k - 1], sr.at[k - 1], c_peer)
        total = total + small_a[k - 1]
    small_b[d] = total
    pump(2)
    for k in range(1, 4):
        go(send(small_b.at[d], small_b.at[d], us.at[k - 1], ur.at[k - 1], (d ^ k, f)))
    pump(4)
    for k in range(1, 4):
        arrived(small_b.at[d ^ k], us.at[k - 1], ur.at[k - 1], c_peer)
    small_out[...] = (small_b[0] + small_b[1]) + (small_b[2] + small_b[3])
    pump(len(order))
    for copy in pending:
        copy.wait_send()
    for i in range(max(0, count - slots_other), count):
        core_sends[i].wait_send()


def layer_step(fsdp_size, length, scenes, cotangent, shards, small):
    column = fsdp_size // 2
    hops = column - 1
    seq_len = scenes.shape[0]
    ff = shards[3].shape[0] * fsdp_size
    low, wide = jnp.bfloat16, jnp.float32
    by_need = (shards[3], shards[2], shards[1], shards[0])
    chunks = chunk_list([w.shape for w in by_need])
    count = len(chunks)
    hbm = pl.BlockSpec(memory_space=pltpu.HBM)
    vmem = pl.BlockSpec(memory_space=pltpu.VMEM)
    smem = pl.BlockSpec(memory_space=pltpu.SMEM)
    dma = pltpu.SemaphoreType.DMA
    shape = jax.ShapeDtypeStruct
    scratch = []
    for kind in ("sum", "one", "two", "zed", "fin"):
        for _, _, high, _, _, width in chunks:
            buffers = {
                "sum": (8, column * high, width),
                "one": (2, 2, column * high, width),
                "two": (2, column * high, width),
                "zed": (2, hops, high, width),
                "fin": (2, high, width),
            }
            scratch.append(pltpu.VMEM(buffers[kind], low))
    tall = max(c[2] for c in chunks) * column
    broad = max(c[5] for c in chunks)
    rows = D // fsdp_size
    turned = pltpu.VMEM((2, column, rows, seq_len), low)
    scratch += [pltpu.VMEM((SLOTS, 8, tall, broad), low)] * 2
    scratch += [
        pltpu.VMEM((ff, D), low),
        pltpu.VMEM((small.shape[0] * fsdp_size, small.shape[1]), low),
        pltpu.VMEM((seq_len, D), low),
        turned,
        pltpu.VMEM((seq_len, 3 * D), low),
        pltpu.VMEM((seq_len, D), low),
        turned,
        pltpu.VMEM((seq_len, D), wide),
        turned,
        pltpu.VMEM((seq_len, ff), low),
        pltpu.VMEM((seq_len, ff), low),
        pltpu.VMEM((2, column, ff // fsdp_size, seq_len), low),
        pltpu.VMEM((seq_len, D), low),
        pltpu.VMEM((seq_len, D), wide),
        pltpu.VMEM((seq_len, D), wide),
        pltpu.VMEM((fsdp_size, 8, rows), wide),
        pltpu.VMEM((fsdp_size - 1, 8, rows), wide),
        pltpu.VMEM((4, 8, rows), wide),
    ]
    scratch += [dma((2, 4, 5))] + [dma((4, hops))] * 10 + [dma((4,))] * 2 + [dma((fsdp_size - 1,))] * 2
    scratch += [dma((count,))] * 2 + [dma((count, 2, 2))] * 2 + [dma((count, 2))] * 2
    scratch += [dma((count, 2, hops))] * 2 + [dma((count, 2, 2))] * 2 + [dma((count, 2))] * 2
    scratch += [dma((count, 2))] + [dma((fsdp_size - 1,))] * 2 + [dma((3,))] * 2
    scratch += [dma((4, 4)), pltpu.SemaphoreType.REGULAR]
    return pl.pallas_call(
        functools.partial(layer_kernel, fsdp_size, chunks),
        out_shape=[shape((a.shape[0] * fsdp_size, a.shape[1]), low) for a in shards]
        + [shape(w.shape, low) for w in by_need]
        + [shape((seq_len, D), low)] * 2
        + [shape((8, rows), wide)],
        in_specs=[smem, vmem, vmem] + [hbm] * 5,
        out_specs=[hbm] * 8 + [vmem] * 3,
        scratch_shapes=scratch,
        compiler_params=pltpu.CompilerParams(
            collective_id=0, has_side_effects=True, vmem_limit_bytes=67043328
        ),
        name="layer_step",
    )(length, scenes, cotangent, *shards, small)


def on_device_wide(
    scenes_in,
    scene_lengths,
    cotangent,
    qkv_weight,
    out_weight,
    up_weight,
    down_weight,
    gain_one,
    bias_one,
    gain_two,
    bias_two,
):
    params = (
        lax.all_gather(qkv_weight, "fsdp", axis=0, tiled=True),
        lax.all_gather(out_weight, "fsdp", axis=0, tiled=True),
        lax.all_gather(up_weight, "fsdp", axis=0, tiled=True),
        lax.all_gather(down_weight, "fsdp", axis=0, tiled=True),
        lax.all_gather(gain_one, "fsdp", axis=0, tiled=True),
        lax.all_gather(bias_one, "fsdp", axis=0, tiled=True),
        lax.all_gather(gain_two, "fsdp", axis=0, tiled=True),
        lax.all_gather(bias_two, "fsdp", axis=0, tiled=True),
    )
    inputs = scenes_in[0].astype(jnp.float32)
    seq_len = inputs.shape[0]
    positions = jnp.arange(seq_len, dtype=jnp.int32)
    key_valid = positions < scene_lengths[0]
    row_mask = key_valid.astype(jnp.float32)[:, None]
    saved = forward_pass(inputs, key_valid, params)
    layer_out = (saved[0] * row_mask).astype(jnp.bfloat16)[None]
    grad_out = cotangent[0].astype(jnp.float32) * row_mask
    params_back = (
        lax.all_gather(qkv_weight, "fsdp", axis=0, tiled=True),
        lax.all_gather(out_weight, "fsdp", axis=0, tiled=True),
        lax.all_gather(up_weight, "fsdp", axis=0, tiled=True),
        lax.all_gather(down_weight, "fsdp", axis=0, tiled=True),
        lax.all_gather(gain_one, "fsdp", axis=0, tiled=True),
        lax.all_gather(bias_one, "fsdp", axis=0, tiled=True),
        lax.all_gather(gain_two, "fsdp", axis=0, tiled=True),
        lax.all_gather(bias_two, "fsdp", axis=0, tiled=True),
    )
    saved_back = forward_pass(inputs, key_valid, params_back)
    grad_resid, up_grad, down_grad, gain_two_grad, bias_two_grad = mlp_back(
        grad_out, saved_back, params_back
    )
    input_grad, qkv_grad, out_grad, gain_one_grad, bias_one_grad = attn_back(
        grad_resid, saved_back, params_back
    )
    shares = (
        lax.psum_scatter(qkv_grad, "fsdp", scatter_dimension=0, tiled=True),
        lax.psum_scatter(out_grad, "fsdp", scatter_dimension=0, tiled=True),
        lax.psum_scatter(up_grad, "fsdp", scatter_dimension=0, tiled=True),
        lax.psum_scatter(down_grad, "fsdp", scatter_dimension=0, tiled=True),
        lax.psum_scatter(gain_one_grad, "fsdp", scatter_dimension=0, tiled=True),
        lax.psum_scatter(bias_one_grad, "fsdp", scatter_dimension=0, tiled=True),
        lax.psum_scatter(gain_two_grad, "fsdp", scatter_dimension=0, tiled=True),
        lax.psum_scatter(bias_two_grad, "fsdp", scatter_dimension=0, tiled=True),
    )
    summed = (
        lax.psum(shares[0].astype(jnp.bfloat16), "dp").astype(jnp.float32),
        lax.psum(shares[1].astype(jnp.bfloat16), "dp").astype(jnp.float32),
        lax.psum(shares[2].astype(jnp.bfloat16), "dp").astype(jnp.float32),
        lax.psum(shares[3].astype(jnp.bfloat16), "dp").astype(jnp.float32),
        lax.psum(shares[4].astype(jnp.bfloat16), "dp").astype(jnp.float32),
        lax.psum(shares[5].astype(jnp.bfloat16), "dp").astype(jnp.float32),
        lax.psum(shares[6].astype(jnp.bfloat16), "dp").astype(jnp.float32),
        lax.psum(shares[7].astype(jnp.bfloat16), "dp").astype(jnp.float32),
    )
    qkv_total, out_total, up_total, down_total = (summed[0], summed[1], summed[2], summed[3])
    gain_one_total, bias_one_total, gain_two_total, bias_two_total = (
        summed[4],
        summed[5],
        summed[6],
        summed[7],
    )
    input_out = input_grad.astype(jnp.bfloat16)[None]
    return (
        layer_out,
        input_out,
        qkv_total,
        out_total,
        up_total,
        down_total,
        gain_one_total,
        bias_one_total,
        gain_two_total,
        bias_two_total,
    )


def on_device(
    scenes_in,
    scene_lengths,
    cotangent,
    qkv_weight,
    out_weight,
    up_weight,
    down_weight,
    gain_one,
    bias_one,
    gain_two,
    bias_two,
):
    rows = gain_one.shape[0]
    fsdp_size = D // rows
    small = jnp.stack([gain_one, bias_one, gain_two, bias_two])
    small = jnp.pad(small, ((0, 12), (0, 0)))
    results = layer_step(
        fsdp_size,
        scene_lengths,
        scenes_in[0],
        cotangent[0],
        (qkv_weight, out_weight, up_weight, down_weight),
        small,
    )
    down_sum, up_sum, out_sum, qkv_sum, layer_out, input_grad, small_sum = results[4:]
    wide = jnp.float32
    return (
        layer_out[None],
        input_grad[None],
        qkv_sum.astype(wide),
        out_sum.astype(wide),
        up_sum.astype(wide),
        down_sum.astype(wide),
        small_sum[0],
        small_sum[1],
        small_sum[2],
        small_sum[3],
    )


def solution(mesh):
    placed = (
        P(("dp", "fsdp"), None, None),
        P(("dp", "fsdp")),
        P(("dp", "fsdp"), None, None),
        P("fsdp", None),
        P("fsdp", None),
        P("fsdp", None),
        P("fsdp", None),
        P("fsdp"),
        P("fsdp"),
        P("fsdp"),
        P("fsdp"),
    )
    body = on_device if mesh.shape["dp"] == 4 and mesh.shape["fsdp"] == 8 else on_device_wide
    return jax.shard_map(
        body,
        mesh=mesh,
        in_specs=placed,
        out_specs=(
            P(("dp", "fsdp"), None, None),
            P(("dp", "fsdp"), None, None),
            P("fsdp", None),
            P("fsdp", None),
            P("fsdp", None),
            P("fsdp", None),
            P("fsdp"),
            P("fsdp"),
            P("fsdp"),
            P("fsdp"),
        ),
        check_vma=False,
    )
```

```python
import functools
import math

import jax
import jax.numpy as jnp
from jax import lax
from jax.experimental import pallas as pl
from jax.experimental.pallas import tpu as pltpu
from jax.sharding import PartitionSpec as P

D = 1024
HEADS = 16
HEAD_DIM = 64


epsilon = 1e-05


def norm_rows(values_in):
    row_mean = jnp.mean(values_in, axis=-1, keepdims=True)
    centered = values_in - row_mean
    variance = jnp.mean(centered * centered, axis=-1, keepdims=True)
    inverse = lax.rsqrt(variance + epsilon)
    return (centered * inverse, inverse)


def norm_back(grad_normed, normed, inverse):
    first_mean = jnp.mean(grad_normed, axis=-1, keepdims=True)
    second_mean = jnp.mean(grad_normed * normed, axis=-1, keepdims=True)
    return inverse * (grad_normed - first_mean - normed * second_mean)


def inner_rows(left, right):
    return lax.dot_general(
        left, right, (((0,), (0,)), ((), ())), preferred_element_type=jnp.float32
    )


def outer_cols(left, right):
    return lax.dot_general(
        left, right, (((1,), (1,)), ((), ())), preferred_element_type=jnp.float32
    )


def forward_pass(inputs, key_valid, params):
    qkv_weight, out_weight, up_weight, down_weight, gain_one, bias_one, gain_two, bias_two = params
    seq_len = inputs.shape[0]
    normed_one, inverse_one = norm_rows(inputs)
    hidden_one = (normed_one * gain_one.astype(jnp.float32) + bias_one.astype(jnp.float32)).astype(
        jnp.bfloat16
    )
    qkv_low = jnp.dot(hidden_one, qkv_weight, preferred_element_type=jnp.float32).astype(
        jnp.bfloat16
    )
    split_view = qkv_low.reshape(seq_len, 3, HEADS, HEAD_DIM)
    queries = split_view[:, 0]
    keys_all = split_view[:, 1]
    values_all = split_view[:, 2]
    scale_factor = 1.0 / math.sqrt(HEAD_DIM)
    scores = (
        jnp.einsum("qhd,khd->hqk", queries, keys_all, preferred_element_type=jnp.float32)
        * scale_factor
    )
    masked = jnp.where(key_valid[None, None, :], scores, -1e30)
    highest = jnp.max(masked, axis=-1, keepdims=True)
    expont = jnp.exp(masked - highest)
    probs = expont / jnp.sum(expont, axis=-1, keepdims=True)
    probs_low = probs.astype(jnp.bfloat16)
    attended = jnp.einsum("hqk,khd->qhd", probs_low, values_all, preferred_element_type=jnp.float32)
    attn_low = attended.reshape(seq_len, D).astype(jnp.bfloat16)
    resid_one = inputs + jnp.dot(attn_low, out_weight, preferred_element_type=jnp.float32)
    normed_two, inverse_two = norm_rows(resid_one)
    hidden_two = (normed_two * gain_two.astype(jnp.float32) + bias_two.astype(jnp.float32)).astype(
        jnp.bfloat16
    )
    hidden_pre = jnp.dot(hidden_two, up_weight, preferred_element_type=jnp.float32)
    activated = jax.nn.gelu(hidden_pre, approximate=False).astype(jnp.bfloat16)
    result = resid_one + jnp.dot(activated, down_weight, preferred_element_type=jnp.float32)
    return (
        result,
        normed_one,
        inverse_one,
        hidden_one,
        queries,
        keys_all,
        values_all,
        probs,
        probs_low,
        attn_low,
        normed_two,
        inverse_two,
        hidden_two,
        hidden_pre,
        activated,
    )


def mlp_back(grad_out, saved, params):
    up_weight, down_weight, gain_two = (params[2], params[3], params[6])
    normed_two, inverse_two, hidden_two, hidden_pre, activated = (
        saved[10],
        saved[11],
        saved[12],
        saved[13],
        saved[14],
    )
    grad_low = grad_out.astype(jnp.bfloat16)
    down_grad = inner_rows(activated, grad_low)
    grad_act = outer_cols(grad_low, down_weight)
    cumul = 0.5 * (1.0 + lax.erf(hidden_pre * (1.0 / math.sqrt(2.0))))
    density = jnp.exp(-0.5 * hidden_pre * hidden_pre) * (1.0 / math.sqrt(2.0 * math.pi))
    grad_pre = (grad_act * (cumul + hidden_pre * density)).astype(jnp.bfloat16)
    up_grad = inner_rows(hidden_two, grad_pre)
    grad_hidden = outer_cols(grad_pre, up_weight)
    gain_two_grad = jnp.sum(grad_hidden * normed_two, axis=0)
    bias_two_grad = jnp.sum(grad_hidden, axis=0)
    grad_resid = grad_out + norm_back(
        grad_hidden * gain_two.astype(jnp.float32), normed_two, inverse_two
    )
    return (grad_resid, up_grad, down_grad, gain_two_grad, bias_two_grad)


def attn_back(grad_resid, saved, params):
    qkv_weight, out_weight, gain_one = (params[0], params[1], params[4])
    normed_one, inverse_one, hidden_one = (saved[1], saved[2], saved[3])
    queries, keys_all, values_all, probs, probs_low, attn_low = (
        saved[4],
        saved[5],
        saved[6],
        saved[7],
        saved[8],
        saved[9],
    )
    seq_len = grad_resid.shape[0]
    scale_factor = 1.0 / math.sqrt(HEAD_DIM)
    resid_low = grad_resid.astype(jnp.bfloat16)
    out_grad = inner_rows(attn_low, resid_low)
    grad_attn = (
        outer_cols(resid_low, out_weight).astype(jnp.bfloat16).reshape(seq_len, HEADS, HEAD_DIM)
    )
    grad_probs = jnp.einsum(
        "qhd,khd->hqk", grad_attn, values_all, preferred_element_type=jnp.float32
    )
    row_dot = jnp.sum(probs * grad_probs, axis=-1, keepdims=True)
    grad_scores = (probs * (grad_probs - row_dot)).astype(jnp.bfloat16)
    grad_values = jnp.einsum(
        "hqk,qhd->khd", probs_low, grad_attn, preferred_element_type=jnp.float32
    )
    grad_queries = (
        jnp.einsum("hqk,khd->qhd", grad_scores, keys_all, preferred_element_type=jnp.float32)
        * scale_factor
    )
    grad_keys = (
        jnp.einsum("hqk,qhd->khd", grad_scores, queries, preferred_element_type=jnp.float32)
        * scale_factor
    )
    grad_qkv = (
        jnp.stack([grad_queries, grad_keys, grad_values], axis=1)
        .reshape(seq_len, 3 * D)
        .astype(jnp.bfloat16)
    )
    qkv_grad = inner_rows(hidden_one, grad_qkv)
    grad_hidden = outer_cols(grad_qkv, qkv_weight)
    gain_one_grad = jnp.sum(grad_hidden * normed_one, axis=0)
    bias_one_grad = jnp.sum(grad_hidden, axis=0)
    input_grad = grad_resid + norm_back(
        grad_hidden * gain_one.astype(jnp.float32), normed_one, inverse_one
    )
    return (input_grad, qkv_grad, out_grad, gain_one_grad, bias_one_grad)


MESH_ID = pl.DeviceIdType.MESH


def aligned(index, size):
    return pl.ds(pl.multiple_of(index * size, size), size)


def greet(dp_index, fsdp_index, fsdp_size):
    barrier = pltpu.get_barrier_semaphore()
    peers = [(dp_index ^ 1, fsdp_index), (dp_index ^ 2, fsdp_index), (dp_index ^ 3, fsdp_index)]
    peers += [(dp_index, lax.rem(fsdp_index + k, fsdp_size)) for k in range(1, fsdp_size)]
    for peer in peers:
        pl.semaphore_signal(barrier, inc=1, device_id=peer, device_id_type=MESH_ID)
    pl.semaphore_wait(barrier, len(peers))


def send(src, dst, send_sem, recv_sem, device):
    return pltpu.make_async_remote_copy(
        src_ref=src,
        dst_ref=dst,
        send_sem=send_sem,
        recv_sem=recv_sem,
        device_id=device,
        device_id_type=MESH_ID,
    )


def gelu_parts(u):
    cumul = 0.5 * (1.0 + lax.erf(u * (1.0 / math.sqrt(2.0))))
    density = jnp.exp(-0.5 * u * u) * (1.0 / math.sqrt(2.0 * math.pi))
    return u * cumul, cumul + u * density


def head_scores(q_head, keys, key_valid):
    scores = outer_cols(q_head, keys) * (1.0 / math.sqrt(HEAD_DIM))
    masked = jnp.where(key_valid, scores, -1e30)
    expont = jnp.exp(masked - jnp.max(masked, axis=-1, keepdims=True))
    return expont / jnp.sum(expont, axis=-1, keepdims=True)


def transposed(target, source, fsdp_size):
    rows = target.shape[2]

    def body(n, carry):
        target[lax.rem(n, 2), lax.div(n, 2)] = jnp.transpose(source[:, aligned(n, rows)])
        return carry

    lax.fori_loop(0, fsdp_size, body, 0)


SLOTS = 2


def chunk_list(shapes):
    chunks = []
    for piece, (rows, span) in enumerate(shapes):
        part = span // 8
        high = min(rows, 128)
        width = 256 if part % 256 == 0 else 128
        for row in range(0, rows, high):
            for col in range(0, part, width):
                chunks.append((piece, row, high, part, col, width))
    return chunks


def layer_kernel(fsdp_size, chunks, *refs):
    pieces = 4
    count = len(chunks)
    column = fsdp_size // 2
    low, wide = jnp.bfloat16, jnp.float32
    length, scenes, cotangent = refs[:3]
    shards = refs[3:7]
    small = refs[7]
    fulls = refs[8:12]
    outs = refs[12:16]
    layer_out, input_grad, small_out = refs[16:19]
    rest = refs[19:]
    sum_b, one_b, two_b, zed_b, fin_b = (rest[i * count : (i + 1) * count] for i in range(5))
    rest = rest[5 * count :]
    other_b, core_b, big, small_full, hidden, hidden_t, qkv, attn, attn_t = rest[:9]
    resid, hidden_two_t, wide_low, slope, active_t, grad_low, grad_hidden, grad_resid = rest[9:17]
    small_g, small_a, small_b = rest[17:20]
    own_sem, az, bz, ax, bx, ay, by, ad, bd, ae, be, ac, bc, sv, rv = rest[20:35]
    (cs, cr, os_, or_, ts, tr, zs, zr, fs, fr, gs, gr, out_sem, ss, sr, us, ur) = rest[35:52]
    load_sem, credit = rest[52:]
    d = lax.axis_index("dp")
    f = lax.axis_index("fsdp")
    core = lax.rem(f, 2)
    place = lax.div(f, 2)
    bits = (lax.rem(d, 2), lax.div(d, 2))
    x_peer, y_peer, c_peer = (d ^ 1, f), (d ^ 2, f), (d, f ^ 1)
    peers = (x_peer, y_peer)
    seq_len = scenes.shape[0]
    ff = wide_low.shape[1]
    slots_other, slots_core = other_b.shape[0], core_b.shape[0]
    pending = []
    core_sends = {}

    def go(copy):
        copy.start()
        pending.append(copy)

    def arrived(view, send_sem, recv_sem, device):
        send(view, view, send_sem, recv_sem, device).wait_recv()

    def block(piece, place_from, quarter, half=None):
        rows = shards[piece].shape[0]
        span = shards[piece].shape[1] // 4
        row_part = aligned(place_from * 2 + core, rows)
        if half is None:
            return fulls[piece].at[row_part, aligned(quarter, span)]
        return fulls[piece].at[row_part, aligned(quarter * 2 + half, span // 2)]

    def to_partner(piece, view):
        send(view, view, ac.at[piece], bc.at[piece], c_peer).start()

    def source(k):
        return place ^ k

    def from_column(piece, k):
        at = (piece, k - 1)
        view = block(piece, source(k), d)
        arrived(view, az.at[at], bz.at[at], x_peer)
        go(send(view, view, ax.at[at], bx.at[at], x_peer))
        go(send(view, view, ay.at[at], by.at[at], y_peer))
        to_partner(piece, view)

    def from_sides(piece, k):
        at = (piece, k - 1)
        view = block(piece, source(k), d ^ 1)
        arrived(view, ax.at[at], bx.at[at], x_peer)
        part = block(piece, source(k), d ^ 1, 0)
        go(send(part, part, ad.at[at], bd.at[at], y_peer))
        to_partner(piece, view)
        view = block(piece, source(k), d ^ 2)
        arrived(view, ay.at[at], by.at[at], y_peer)
        part = block(piece, source(k), d ^ 2, 1)
        go(send(part, part, ae.at[at], be.at[at], x_peer))
        to_partner(piece, view)

    def from_corner(piece, k):
        at = (piece, k - 1)
        for half, (a, b, peer) in enumerate(((ad, bd, y_peer), (ae, be, x_peer))):
            part = block(piece, source(k), d ^ 3, half)
            arrived(part, a.at[at], b.at[at], peer)
            to_partner(piece, part)

    def from_partner(piece):
        rows = shards[piece].shape[0]
        view = fulls[piece].at[pl.ds(0, rows * column)]
        send(view, view, ac.at[piece], bc.at[piece], c_peer).wait()

    def loads(piece):
        if piece == 3:
            parts = [(fulls[3].at[pl.ds(n * D, D)], pl.ds(n * D, D)) for n in range(ff // D)]
        elif piece == 1:
            parts = [(fulls[1], pl.ds(3 * D, D))]
        else:
            parts = [
                (fulls[piece].at[:, pl.ds(n * D, D)], pl.ds(n * D, D))
                for n in range(fulls[piece].shape[1] // D)
            ]
        return [
            pltpu.make_async_copy(view, big.at[at], load_sem.at[piece, n])
            for n, (view, at) in enumerate(parts)
        ]

    def own_parts(piece, back):
        rows, span = shards[piece].shape
        first_row = sum(s.shape[0] * (s.shape[1] // D) for s in shards[:piece])
        parts = []
        for n in range(span // D):
            stage = big.at[pl.ds(first_row + n * rows, rows)]
            cols = pl.ds(n * D, D)
            whole = fulls[piece].at[aligned(f, rows), cols]
            ends = (stage, whole) if back else (shards[piece].at[:, cols], stage)
            parts.append(pltpu.make_async_copy(*ends, own_sem.at[int(back), piece, n]))
        return parts

    every = range(1, column)
    blocks = [(piece, k) for piece in range(pieces) for k in every]
    gather_order = []
    for n in range(len(blocks) + 4):
        for action, lag in ((from_column, 0), (from_sides, 1), (from_corner, 2)):
            if 0 <= n - lag < len(blocks):
                gather_order.append((action, *blocks[n - lag]))
    gathered = []

    def gather_step(limit=1):
        for _ in range(limit):
            if len(gathered) < len(gather_order):
                action, piece, k = gather_order[len(gathered)]
                gathered.append(1)
                action(piece, k)

    def gather_to(action, piece):
        last_one = gather_order.index((action, piece, column - 1))
        while len(gathered) <= last_one:
            gather_step()

    def slot_view(ref, slot, i):
        _, _, high, _, _, width = chunks[i]
        return ref.at[slot, :, pl.ds(0, column * high), pl.ds(0, width)]

    def grams(i, left_t, right):
        piece, row, high, part, col, width = chunks[i]
        slot = i % slots_other
        if i >= slots_other:
            core_sends[i - slots_other].wait_send()
        step = 2 if width == part and width == 128 else 1

        def fill(half, target):
            left = left_t[half, :, pl.ds(row, high), :].reshape(column * high, seq_len)

            def body(n, carry):
                start = pl.multiple_of(n * step * part + col, 128)
                found = jnp.dot(
                    left, right[:, pl.ds(start, step * width)], preferred_element_type=wide
                ).astype(low)
                for m in range(step):
                    target[n * step + m] = found[:, m * width : (m + 1) * width]
                return carry

            lax.fori_loop(0, 8 // step, body, 0)

        fill(1 - core, slot_view(other_b, slot, i))
        if i >= slots_core:
            pl.semaphore_wait(credit, 1)
        fill(core, sum_b[i])
        copy = send(
            slot_view(other_b, slot, i),
            slot_view(core_b, i % slots_core, i),
            cs.at[i],
            cr.at[i],
            c_peer,
        )
        copy.start()
        core_sends[i] = copy

    def add_into(target, other):
        rows = target.shape[0]
        strip = 64

        def body(n, carry):
            at = aligned(n, strip)
            target[at] = (target[at].astype(wide) + other[at].astype(wide)).astype(low)
            return carry

        lax.fori_loop(0, rows // strip, body, 0)

    def far_quarter(half, b):
        if half == 0:
            return (1 - bits[0]) + 2 * b
        return b + 2 * (1 - bits[1])

    def near_quarter(half, b):
        if half == 0:
            return bits[0] + 2 * b
        return b + 2 * bits[1]

    def pair(i):
        view = slot_view(core_b, i % slots_core, i)
        arrived(view, cs.at[i], cr.at[i], c_peer)

        def add(quarter, half):
            add_into(sum_b[i].at[quarter * 2 + half], view.at[quarter * 2 + half])

        for b in range(2):
            for half in range(2):
                add(far_quarter(half, b), half)
            for half in range(2):
                go(
                    send(
                        sum_b[i].at[far_quarter(half, b) * 2 + half],
                        one_b[i].at[half, b],
                        os_.at[i, half, b],
                        or_.at[i, half, b],
                        peers[half],
                    )
                )
        for b in range(2):
            for half in range(2):
                add(near_quarter(half, b), half)
        if i + slots_core < count:
            pl.semaphore_signal(credit, inc=1, device_id=c_peer, device_id_type=MESH_ID)

    def first(i):
        for half in range(2):
            for b in range(2):
                arrived(one_b[i].at[half, b], os_.at[i, half, b], or_.at[i, half, b], peers[half])
                add_into(sum_b[i].at[near_quarter(half, b) * 2 + half], one_b[i].at[half, b])
            other = d ^ 2 if half == 0 else d ^ 1
            go(
                send(
                    sum_b[i].at[other * 2 + half],
                    two_b[i].at[half],
                    ts.at[i, half],
                    tr.at[i, half],
                    peers[1 - half],
                )
            )

    def second(i):
        _, _, high, _, _, _ = chunks[i]
        for half in range(2):
            arrived(two_b[i].at[half], ts.at[i, half], tr.at[i, half], peers[1 - half])
            mine = sum_b[i].at[d * 2 + half]
            add_into(mine, two_b[i].at[half])
            for k in range(1, column):
                to = place ^ k
                go(
                    send(
                        mine.at[aligned(to, high)],
                        zed_b[i].at[half, k - 1],
                        zs.at[i, half, k - 1],
                        zr.at[i, half, k - 1],
                        (d, to * 2 + core),
                    )
                )

    def result(i, quarter, half):
        piece, row, high, part, col, width = chunks[i]
        start = pl.multiple_of((quarter * 2 + half) * part + col, 128)
        return outs[piece].at[pl.ds(row, high), pl.ds(start, width)]

    def last(i):
        _, _, high, _, _, _ = chunks[i]
        for half in range(2):
            for k in range(1, column):
                at = (i, half, k - 1)
                arrived(zed_b[i].at[half, k - 1], zs.at[at], zr.at[at], c_peer)
            total = sum_b[i][d * 2 + half, aligned(place, high)].astype(wide)
            for k in range(1, column):
                total = total + zed_b[i][half, k - 1].astype(wide)
            fin_b[i][half] = total.astype(low)
        for half in range(2):
            mine = result(i, d, half)
            pltpu.make_async_copy(fin_b[i].at[half], mine, out_sem.at[i, half]).start()
            for axis in range(2):
                at = (i, half, axis)
                go(send(fin_b[i].at[half], mine, fs.at[at], fr.at[at], peers[axis]))

    def spread(i):
        for half in range(2):
            for axis in range(2):
                at = (i, half, axis)
                view = result(i, d ^ (1 + axis), half)
                arrived(view, fs.at[at], fr.at[at], peers[axis])
                if half == axis:
                    go(send(view, view, gs.at[i, half], gr.at[i, half], peers[1 - axis]))

    def finish(i):
        for half in range(2):
            view = result(i, d ^ 3, half)
            arrived(view, gs.at[i, half], gr.at[i, half], peers[1 - half])
            pltpu.make_async_copy(fin_b[i].at[half], result(i, d, half), out_sem.at[i, half]).wait()

    stages = (first, second, last, spread, finish)
    order = []
    for step in range(count + len(stages) - 1):
        for n, stage in enumerate(stages):
            if 0 <= step - n < count:
                order.append((stage, step - n))
    done = []
    waiting = []
    paired = []

    def pair_up(keep=0):
        while len(waiting) > keep:
            i = waiting.pop(0)
            pair(i)
            paired.append(i)

    def advance(limit):
        for _ in range(limit):
            if len(done) < len(order) and order[len(done)][1] in paired:
                stage, i = order[len(done)]
                done.append(1)
                stage(i)

    def pump(limit=1):
        pair_up()
        advance(limit)

    def produce(some, left_t, right, limit, keep=1):
        for i in some:
            pair_up(slots_core - 1)
            grams(i, left_t, right)
            waiting.append(i)
            pair_up(keep)
            advance(limit)

    by_piece = [[i for i in range(count) if chunks[i][0] == piece] for piece in range(pieces)]

    greet(d, f, fsdp_size)
    small_rows = small.shape[0]
    for k in range(1, fsdp_size):
        to = lax.rem(f + k, fsdp_size)
        go(send(small, small_full.at[aligned(f, small_rows)], sv.at[k - 1], rv.at[k - 1], (d, to)))
    own_small = pltpu.make_async_copy(
        small, small_full.at[aligned(f, small_rows)], own_sem.at[0, 0, pieces]
    )
    own_small.start()
    for piece in range(pieces):
        rows, span = shards[piece].shape
        for k in every:
            go(
                send(
                    shards[piece].at[:, aligned(d, span // 4)],
                    block(piece, place, d),
                    az.at[piece, k - 1],
                    bz.at[piece, k - 1],
                    (d, (place ^ k) * 2 + core),
                )
            )
        own = fulls[piece].at[aligned(f, rows)]
        send(shards[piece], own, ac.at[piece], bc.at[piece], c_peer).start()
        for copy in own_parts(piece, False):
            copy.start()
    for piece in range(pieces):
        for copy in own_parts(piece, False):
            copy.wait()
        for copy in own_parts(piece, True):
            copy.start()

    normed_one, _ = norm_rows(scenes[...].astype(wide))
    for k in range(1, fsdp_size):
        view = small_full.at[aligned(lax.rem(f - k + fsdp_size, fsdp_size), small_rows)]
        arrived(view, sv.at[k - 1], rv.at[k - 1], c_peer)
    own_small.wait()

    def vector(row):
        values = small_full[...].astype(wide)
        at = range(row, small_rows * fsdp_size, small_rows)
        return jnp.concatenate([values[n : n + 1] for n in at], axis=1)

    hidden[...] = (normed_one * vector(0) + vector(1)).astype(low)
    gather_step(2)
    transposed(hidden_t, hidden, fsdp_size)
    for piece in range(pieces):
        for copy in own_parts(piece, True):
            copy.wait()
    gather_to(from_corner, 0)
    gather_step(3)
    from_partner(0)
    for copy in loads(0):
        copy.start()
    gather_step(1)
    for copy in loads(0):
        copy.wait()

    def project(n, carry):
        cols = aligned(n, 512)
        rows = aligned(lax.div(n, D // 512), D)
        weight = big[rows, aligned(lax.rem(n, D // 512), 512)]
        qkv[:, cols] = jnp.dot(hidden[...], weight, preferred_element_type=wide).astype(low)
        return carry

    tiles = qkv.shape[1] // 512
    lax.fori_loop(0, tiles // 2, project, 0)
    gather_step(2)
    lax.fori_loop(tiles // 2, tiles, project, 0)
    gather_step(2)
    key_valid = lax.broadcasted_iota(jnp.int32, (1, seq_len), 1) < length[0]
    row_valid = lax.broadcasted_iota(jnp.int32, (seq_len, 1), 0) < length[0]
    first_half = lax.broadcasted_iota(jnp.int32, (1, 128), 1) < HEAD_DIM
    halves = (first_half.astype(wide).astype(low), 1 - first_half.astype(wide).astype(low))
    pairs = D // 128

    def attend(j, carry):
        queries, keys, values = (qkv[:, aligned(j + i * pairs, 128)] for i in range(3))
        found = []
        for half in halves:
            probs = head_scores(queries * half, keys, key_valid)
            found.append(jnp.dot(probs.astype(low), values, preferred_element_type=wide))
        attn[:, aligned(j, 128)] = jnp.where(first_half, found[0], found[1]).astype(low)
        return carry

    for j in range(0, pairs, 2):
        lax.fori_loop(j, j + 2, attend, 0)
        gather_step(2)
    transposed(attn_t, attn, fsdp_size)
    gather_to(from_corner, 1)
    gather_step(1)
    from_partner(1)
    for copy in loads(1):
        copy.start()
    for copy in loads(1):
        copy.wait()

    def second_in(n, carry):
        cols = aligned(n, 512)
        resid[:, cols] = scenes[:, cols].astype(wide) + jnp.dot(
            attn[...], big[pl.ds(3 * D, D), cols], preferred_element_type=wide
        )
        return carry

    lax.fori_loop(0, D // 512, second_in, 0)
    normed_two, _ = norm_rows(resid[...])
    hidden[...] = (normed_two * vector(2) + vector(3)).astype(low)
    transposed(hidden_two_t, hidden, fsdp_size)
    gather_to(from_corner, 2)
    gather_step(2)
    from_partner(2)
    for copy in loads(2):
        copy.start()
    span = D // 256

    def expand(n, carry):
        cols = aligned(n, 256)
        rows = aligned(lax.div(n, span), D)
        weight = big[rows, aligned(lax.rem(n, span), 256)]
        acts, grads = gelu_parts(jnp.dot(hidden[...], weight, preferred_element_type=wide))
        wide_low[:, cols] = acts.astype(low)
        slope[:, cols] = grads.astype(low)
        return carry

    for part, copy in enumerate(loads(2)):
        copy.wait()
        lax.fori_loop(part * span, (part + 1) * span, expand, 0)
        gather_step(2)
    transposed(active_t, wide_low, fsdp_size)
    grad_low[...] = jnp.where(row_valid, cotangent[...].astype(wide), 0.0).astype(low)
    early = by_piece[0][: slots_core - 1]
    produce(early, active_t, grad_low, 0, slots_core)
    gather_to(from_sides, pieces - 1)
    pair_up()
    gather_to(from_corner, pieces - 1)
    produce(by_piece[0][len(early) :][:1], active_t, grad_low, 0)
    from_partner(3)
    for copy in loads(3):
        copy.start()
    produce(by_piece[0][len(early) + 1 :], active_t, grad_low, 0)
    for part, copy in enumerate(loads(3)):
        copy.wait()
        at = pl.ds(part * D, D)
        term = jnp.dot(wide_low[:, at], big[at], preferred_element_type=wide)
        if part == 0:
            grad_hidden[...] = resid[...] + term
        else:
            grad_hidden[...] += term
        pair_up()
    layer_out[...] = jnp.where(row_valid, grad_hidden[...], 0.0).astype(low)
    pump(1)

    tile = 512

    def pre(n, carry):
        at = aligned(n, tile)
        back = outer_cols(grad_low[...], big[at])
        wide_low[:, at] = (back * slope[:, at].astype(wide)).astype(low)
        return carry

    for n in range(0, ff // tile, 2):
        lax.fori_loop(n, n + 2, pre, 0)
        pump(1)
    for copy in loads(2):
        copy.start()
    produce(by_piece[1], hidden_two_t, wide_low, 2)
    for part, copy in enumerate(loads(2)):
        copy.wait()
        back = outer_cols(wide_low[:, pl.ds(part * D, D)], big[pl.ds(part * D, D)])
        if part == 0:
            grad_hidden[...] = back
        else:
            grad_hidden[...] += back
        pump(1)
    for piece in (1, 0):
        for copy in loads(piece):
            copy.start()
    pump(1)

    def norm_step(values, grads, gain, base, row):
        normed, inverse = norm_rows(values)
        rows = D // fsdp_size
        for n, total in enumerate((grads * normed, grads)):
            sums = jnp.sum(total, axis=0, keepdims=True)
            for to in range(fsdp_size):
                small_g[to, row + n : row + n + 1, :] = sums[:, to * rows : (to + 1) * rows]
        return base + norm_back(grads * gain, normed, inverse)

    small_g[...] = jnp.zeros_like(small_g)
    base = jnp.where(row_valid, cotangent[...].astype(wide), 0.0)
    grad_resid[...] = norm_step(resid[...], grad_hidden[...], vector(2), base, 2)
    grad_low[...] = grad_resid[...].astype(low)
    pump(1)
    produce(by_piece[2], attn_t, grad_low, 2)
    for copy in loads(1):
        copy.wait()

    def attn_in(n, carry):
        rows = pl.ds(pl.multiple_of(3 * D + n * 256, 256), 256)
        attn[:, aligned(n, 256)] = outer_cols(grad_low[...], big[rows]).astype(low)
        return carry

    lax.fori_loop(0, D // 256, attn_in, 0)
    pump(1)
    factor = 1.0 / math.sqrt(HEAD_DIM)

    def attend_back(j, carry):
        queries, keys, values = (qkv[:, aligned(j + i * pairs, 128)] for i in range(3))
        grads = attn[:, aligned(j, 128)]
        found = []
        for half in halves:
            probs = head_scores(queries * half, keys, key_valid)
            grad_probs = outer_cols(grads * half, values)
            row_dot = jnp.sum(probs * grad_probs, axis=-1, keepdims=True)
            scores = (probs * (grad_probs - row_dot)).astype(low)
            found.append(
                (
                    jnp.dot(scores, keys, preferred_element_type=wide) * factor,
                    inner_rows(scores, queries) * factor,
                    inner_rows(probs.astype(low), grads),
                )
            )
        for i in range(3):
            wide_low[:, aligned(j + i * pairs, 128)] = jnp.where(
                first_half, found[0][i], found[1][i]
            ).astype(low)
        return carry

    for j in range(0, pairs, 2):
        lax.fori_loop(j, j + 2, attend_back, 0)
        pump(1)
    produce(by_piece[3], hidden_t, wide_low, 2)
    for part, copy in enumerate(loads(0)):
        copy.wait()
        total = outer_cols(wide_low[:, pl.ds(part * D, D)], big[pl.ds(part * D, D)])
        if part == 0:
            grad_hidden[...] = total
        else:
            grad_hidden[...] += total
    pump(1)
    total = norm_step(scenes[...].astype(wide), grad_hidden[...], vector(0), grad_resid[...], 0)
    input_grad[...] = total.astype(low)
    for k in range(1, fsdp_size):
        to = lax.rem(f + k, fsdp_size)
        go(send(small_g.at[to], small_a.at[k - 1], ss.at[k - 1], sr.at[k - 1], (d, to)))
    pump(2)
    total = small_g[f]
    for k in range(1, fsdp_size):
        arrived(small_a.at[k - 1], ss.at[k - 1], sr.at[k - 1], c_peer)
        total = total + small_a[k - 1]
    small_b[d] = total
    pump(2)
    for k in range(1, 4):
        go(send(small_b.at[d], small_b.at[d], us.at[k - 1], ur.at[k - 1], (d ^ k, f)))
    pump(4)
    for k in range(1, 4):
        arrived(small_b.at[d ^ k], us.at[k - 1], ur.at[k - 1], c_peer)
    small_out[...] = (small_b[0] + small_b[1]) + (small_b[2] + small_b[3])
    pump(len(order))
    for copy in pending:
        copy.wait_send()
    for i in range(max(0, count - slots_other), count):
        core_sends[i].wait_send()


def layer_step(fsdp_size, length, scenes, cotangent, shards, small):
    column = fsdp_size // 2
    hops = column - 1
    seq_len = scenes.shape[0]
    ff = shards[3].shape[0] * fsdp_size
    low, wide = jnp.bfloat16, jnp.float32
    by_need = (shards[3], shards[2], shards[1], shards[0])
    chunks = chunk_list([w.shape for w in by_need])
    count = len(chunks)
    hbm = pl.BlockSpec(memory_space=pltpu.HBM)
    vmem = pl.BlockSpec(memory_space=pltpu.VMEM)
    smem = pl.BlockSpec(memory_space=pltpu.SMEM)
    dma = pltpu.SemaphoreType.DMA
    shape = jax.ShapeDtypeStruct
    scratch = []
    for kind in ("sum", "one", "two", "zed", "fin"):
        for _, _, high, _, _, width in chunks:
            buffers = {
                "sum": (8, column * high, width),
                "one": (2, 2, column * high, width),
                "two": (2, column * high, width),
                "zed": (2, hops, high, width),
                "fin": (2, high, width),
            }
            scratch.append(pltpu.VMEM(buffers[kind], low))
    tall = max(c[2] for c in chunks) * column
    broad = max(c[5] for c in chunks)
    rows = D // fsdp_size
    turned = pltpu.VMEM((2, column, rows, seq_len), low)
    scratch += [pltpu.VMEM((SLOTS, 8, tall, broad), low)] * 2
    scratch += [
        pltpu.VMEM((ff, D), low),
        pltpu.VMEM((small.shape[0] * fsdp_size, small.shape[1]), low),
        pltpu.VMEM((seq_len, D), low),
        turned,
        pltpu.VMEM((seq_len, 3 * D), low),
        pltpu.VMEM((seq_len, D), low),
        turned,
        pltpu.VMEM((seq_len, D), wide),
        turned,
        pltpu.VMEM((seq_len, ff), low),
        pltpu.VMEM((seq_len, ff), low),
        pltpu.VMEM((2, column, ff // fsdp_size, seq_len), low),
        pltpu.VMEM((seq_len, D), low),
        pltpu.VMEM((seq_len, D), wide),
        pltpu.VMEM((seq_len, D), wide),
        pltpu.VMEM((fsdp_size, 8, rows), wide),
        pltpu.VMEM((fsdp_size - 1, 8, rows), wide),
        pltpu.VMEM((4, 8, rows), wide),
    ]
    scratch += [dma((2, 4, 5))] + [dma((4, hops))] * 10 + [dma((4,))] * 2 + [dma((fsdp_size - 1,))] * 2
    scratch += [dma((count,))] * 2 + [dma((count, 2, 2))] * 2 + [dma((count, 2))] * 2
    scratch += [dma((count, 2, hops))] * 2 + [dma((count, 2, 2))] * 2 + [dma((count, 2))] * 2
    scratch += [dma((count, 2))] + [dma((fsdp_size - 1,))] * 2 + [dma((3,))] * 2
    scratch += [dma((4, 4)), pltpu.SemaphoreType.REGULAR]
    return pl.pallas_call(
        functools.partial(layer_kernel, fsdp_size, chunks),
        out_shape=[shape((a.shape[0] * fsdp_size, a.shape[1]), low) for a in shards]
        + [shape(w.shape, low) for w in by_need]
        + [shape((seq_len, D), low)] * 2
        + [shape((8, rows), wide)],
        in_specs=[smem, vmem, vmem] + [hbm] * 5,
        out_specs=[hbm] * 8 + [vmem] * 3,
        scratch_shapes=scratch,
        compiler_params=pltpu.CompilerParams(
            collective_id=0, has_side_effects=True, vmem_limit_bytes=67043328
        ),
        name="layer_step",
    )(length, scenes, cotangent, *shards, small)


def widen_kernel(parts, *refs):
    count = len(parts)
    small = refs[6]
    outs, small_outs = refs[7:13], refs[13:17]
    stages, wides = refs[17 : 17 + count], refs[17 + count : 17 + 2 * count]
    in_sem, out_sem = refs[17 + 2 * count :]
    copies = []
    for n, (which, at) in enumerate(parts):
        copies.append(pltpu.make_async_copy(refs[which].at[at], stages[n], in_sem.at[n]))
        copies[n].start()
    for row, out in enumerate(small_outs):
        out[...] = small[row]
    backs = []
    for n, (which, at) in enumerate(parts):
        copies[n].wait()
        source = stages[n]
        if outs[which].dtype != source.dtype:
            wides[n][...] = source[...].astype(jnp.float32)
            source = wides[n]
        backs.append(pltpu.make_async_copy(source, outs[which].at[at], out_sem.at[n]))
        backs[n].start()
    for copy in backs:
        copy.wait()


def widen(sums, rows, small):
    low, wide = jnp.bfloat16, jnp.float32
    parts, stages, wides = [], [], []
    for which, array in enumerate((*sums, *rows)):
        high, span = array.shape
        step = max(16, min(high, 1 << ((BLOCK // span).bit_length() - 1)))
        for row in range(0, high, step):
            parts.append((which, pl.ds(row, step)))
            stages.append(pltpu.VMEM((step, span), low))
            wides.append(pltpu.VMEM((step, span) if which < len(sums) else (8, 128), wide))
    shape = jax.ShapeDtypeStruct
    hbm = pl.BlockSpec(memory_space=pltpu.HBM)
    vmem = pl.BlockSpec(memory_space=pltpu.VMEM)
    dma = pltpu.SemaphoreType.DMA
    return pl.pallas_call(
        functools.partial(widen_kernel, parts),
        out_shape=[shape(a.shape, wide) for a in sums]
        + [shape(a.shape, low) for a in rows]
        + [shape((small.shape[1],), wide)] * 4,
        in_specs=[hbm] * 6 + [vmem],
        out_specs=[hbm] * 6 + [vmem] * 4,
        scratch_shapes=stages + wides + [dma((len(parts),))] * 2,
        compiler_params=pltpu.CompilerParams(vmem_limit_bytes=67043328),
        name="widen",
    )(*sums, *rows, small)


BLOCK = 131072


def on_device_wide(
    scenes_in,
    scene_lengths,
    cotangent,
    qkv_weight,
    out_weight,
    up_weight,
    down_weight,
    gain_one,
    bias_one,
    gain_two,
    bias_two,
):
    params = (
        lax.all_gather(qkv_weight, "fsdp", axis=0, tiled=True),
        lax.all_gather(out_weight, "fsdp", axis=0, tiled=True),
        lax.all_gather(up_weight, "fsdp", axis=0, tiled=True),
        lax.all_gather(down_weight, "fsdp", axis=0, tiled=True),
        lax.all_gather(gain_one, "fsdp", axis=0, tiled=True),
        lax.all_gather(bias_one, "fsdp", axis=0, tiled=True),
        lax.all_gather(gain_two, "fsdp", axis=0, tiled=True),
        lax.all_gather(bias_two, "fsdp", axis=0, tiled=True),
    )
    inputs = scenes_in[0].astype(jnp.float32)
    seq_len = inputs.shape[0]
    positions = jnp.arange(seq_len, dtype=jnp.int32)
    key_valid = positions < scene_lengths[0]
    row_mask = key_valid.astype(jnp.float32)[:, None]
    saved = forward_pass(inputs, key_valid, params)
    layer_out = (saved[0] * row_mask).astype(jnp.bfloat16)[None]
    grad_out = cotangent[0].astype(jnp.float32) * row_mask
    params_back = (
        lax.all_gather(qkv_weight, "fsdp", axis=0, tiled=True),
        lax.all_gather(out_weight, "fsdp", axis=0, tiled=True),
        lax.all_gather(up_weight, "fsdp", axis=0, tiled=True),
        lax.all_gather(down_weight, "fsdp", axis=0, tiled=True),
        lax.all_gather(gain_one, "fsdp", axis=0, tiled=True),
        lax.all_gather(bias_one, "fsdp", axis=0, tiled=True),
        lax.all_gather(gain_two, "fsdp", axis=0, tiled=True),
        lax.all_gather(bias_two, "fsdp", axis=0, tiled=True),
    )
    saved_back = forward_pass(inputs, key_valid, params_back)
    grad_resid, up_grad, down_grad, gain_two_grad, bias_two_grad = mlp_back(
        grad_out, saved_back, params_back
    )
    input_grad, qkv_grad, out_grad, gain_one_grad, bias_one_grad = attn_back(
        grad_resid, saved_back, params_back
    )
    shares = (
        lax.psum_scatter(qkv_grad, "fsdp", scatter_dimension=0, tiled=True),
        lax.psum_scatter(out_grad, "fsdp", scatter_dimension=0, tiled=True),
        lax.psum_scatter(up_grad, "fsdp", scatter_dimension=0, tiled=True),
        lax.psum_scatter(down_grad, "fsdp", scatter_dimension=0, tiled=True),
        lax.psum_scatter(gain_one_grad, "fsdp", scatter_dimension=0, tiled=True),
        lax.psum_scatter(bias_one_grad, "fsdp", scatter_dimension=0, tiled=True),
        lax.psum_scatter(gain_two_grad, "fsdp", scatter_dimension=0, tiled=True),
        lax.psum_scatter(bias_two_grad, "fsdp", scatter_dimension=0, tiled=True),
    )
    summed = (
        lax.psum(shares[0].astype(jnp.bfloat16), "dp").astype(jnp.float32),
        lax.psum(shares[1].astype(jnp.bfloat16), "dp").astype(jnp.float32),
        lax.psum(shares[2].astype(jnp.bfloat16), "dp").astype(jnp.float32),
        lax.psum(shares[3].astype(jnp.bfloat16), "dp").astype(jnp.float32),
        lax.psum(shares[4].astype(jnp.bfloat16), "dp").astype(jnp.float32),
        lax.psum(shares[5].astype(jnp.bfloat16), "dp").astype(jnp.float32),
        lax.psum(shares[6].astype(jnp.bfloat16), "dp").astype(jnp.float32),
        lax.psum(shares[7].astype(jnp.bfloat16), "dp").astype(jnp.float32),
    )
    qkv_total, out_total, up_total, down_total = (summed[0], summed[1], summed[2], summed[3])
    gain_one_total, bias_one_total, gain_two_total, bias_two_total = (
        summed[4],
        summed[5],
        summed[6],
        summed[7],
    )
    input_out = input_grad.astype(jnp.bfloat16)[None]
    return (
        layer_out,
        input_out,
        qkv_total,
        out_total,
        up_total,
        down_total,
        gain_one_total,
        bias_one_total,
        gain_two_total,
        bias_two_total,
    )


def on_device(
    scenes_in,
    scene_lengths,
    cotangent,
    qkv_weight,
    out_weight,
    up_weight,
    down_weight,
    gain_one,
    bias_one,
    gain_two,
    bias_two,
):
    rows = gain_one.shape[0]
    fsdp_size = D // rows
    small = jnp.stack([gain_one, bias_one, gain_two, bias_two])
    small = jnp.pad(small, ((0, 12), (0, 0)))
    results = layer_step(
        fsdp_size,
        scene_lengths,
        scenes_in[0],
        cotangent[0],
        (qkv_weight, out_weight, up_weight, down_weight),
        small,
    )
    down_sum, up_sum, out_sum, qkv_sum, layer_out, input_grad, small_sum = results[4:]
    wide = widen((qkv_sum, out_sum, up_sum, down_sum), (layer_out, input_grad), small_sum)
    return (wide[4][None], wide[5][None], *wide[:4], *wide[6:])


def solution(mesh):
    placed = (
        P(("dp", "fsdp"), None, None),
        P(("dp", "fsdp")),
        P(("dp", "fsdp"), None, None),
        P("fsdp", None),
        P("fsdp", None),
        P("fsdp", None),
        P("fsdp", None),
        P("fsdp"),
        P("fsdp"),
        P("fsdp"),
        P("fsdp"),
    )
    body = on_device if mesh.shape["dp"] == 4 and mesh.shape["fsdp"] == 8 else on_device_wide
    return jax.shard_map(
        body,
        mesh=mesh,
        in_specs=placed,
        out_specs=(
            P(("dp", "fsdp"), None, None),
            P(("dp", "fsdp"), None, None),
            P("fsdp", None),
            P("fsdp", None),
            P("fsdp", None),
            P("fsdp", None),
            P("fsdp"),
            P("fsdp"),
            P("fsdp"),
            P("fsdp"),
        ),
        check_vma=False,
    )
```

```python
import functools
import math

import jax
import jax.numpy as jnp
from jax import lax
from jax.experimental import pallas as pl
from jax.experimental.pallas import tpu as pltpu
from jax.sharding import PartitionSpec as P

D = 1024
HEADS = 16
HEAD_DIM = 64


epsilon = 1e-05


def norm_rows(values_in):
    row_mean = jnp.mean(values_in, axis=-1, keepdims=True)
    centered = values_in - row_mean
    variance = jnp.mean(centered * centered, axis=-1, keepdims=True)
    inverse = lax.rsqrt(variance + epsilon)
    return (centered * inverse, inverse)


def norm_back(grad_normed, normed, inverse):
    first_mean = jnp.mean(grad_normed, axis=-1, keepdims=True)
    second_mean = jnp.mean(grad_normed * normed, axis=-1, keepdims=True)
    return inverse * (grad_normed - first_mean - normed * second_mean)


def inner_rows(left, right):
    return lax.dot_general(
        left, right, (((0,), (0,)), ((), ())), preferred_element_type=jnp.float32
    )


def outer_cols(left, right):
    return lax.dot_general(
        left, right, (((1,), (1,)), ((), ())), preferred_element_type=jnp.float32
    )


def forward_pass(inputs, key_valid, params):
    qkv_weight, out_weight, up_weight, down_weight, gain_one, bias_one, gain_two, bias_two = params
    seq_len = inputs.shape[0]
    normed_one, inverse_one = norm_rows(inputs)
    hidden_one = (normed_one * gain_one.astype(jnp.float32) + bias_one.astype(jnp.float32)).astype(
        jnp.bfloat16
    )
    qkv_low = jnp.dot(hidden_one, qkv_weight, preferred_element_type=jnp.float32).astype(
        jnp.bfloat16
    )
    split_view = qkv_low.reshape(seq_len, 3, HEADS, HEAD_DIM)
    queries = split_view[:, 0]
    keys_all = split_view[:, 1]
    values_all = split_view[:, 2]
    scale_factor = 1.0 / math.sqrt(HEAD_DIM)
    scores = (
        jnp.einsum("qhd,khd->hqk", queries, keys_all, preferred_element_type=jnp.float32)
        * scale_factor
    )
    masked = jnp.where(key_valid[None, None, :], scores, -1e30)
    highest = jnp.max(masked, axis=-1, keepdims=True)
    expont = jnp.exp(masked - highest)
    probs = expont / jnp.sum(expont, axis=-1, keepdims=True)
    probs_low = probs.astype(jnp.bfloat16)
    attended = jnp.einsum("hqk,khd->qhd", probs_low, values_all, preferred_element_type=jnp.float32)
    attn_low = attended.reshape(seq_len, D).astype(jnp.bfloat16)
    resid_one = inputs + jnp.dot(attn_low, out_weight, preferred_element_type=jnp.float32)
    normed_two, inverse_two = norm_rows(resid_one)
    hidden_two = (normed_two * gain_two.astype(jnp.float32) + bias_two.astype(jnp.float32)).astype(
        jnp.bfloat16
    )
    hidden_pre = jnp.dot(hidden_two, up_weight, preferred_element_type=jnp.float32)
    activated = jax.nn.gelu(hidden_pre, approximate=False).astype(jnp.bfloat16)
    result = resid_one + jnp.dot(activated, down_weight, preferred_element_type=jnp.float32)
    return (
        result,
        normed_one,
        inverse_one,
        hidden_one,
        queries,
        keys_all,
        values_all,
        probs,
        probs_low,
        attn_low,
        normed_two,
        inverse_two,
        hidden_two,
        hidden_pre,
        activated,
    )


def mlp_back(grad_out, saved, params):
    up_weight, down_weight, gain_two = (params[2], params[3], params[6])
    normed_two, inverse_two, hidden_two, hidden_pre, activated = (
        saved[10],
        saved[11],
        saved[12],
        saved[13],
        saved[14],
    )
    grad_low = grad_out.astype(jnp.bfloat16)
    down_grad = inner_rows(activated, grad_low)
    grad_act = outer_cols(grad_low, down_weight)
    cumul = 0.5 * (1.0 + lax.erf(hidden_pre * (1.0 / math.sqrt(2.0))))
    density = jnp.exp(-0.5 * hidden_pre * hidden_pre) * (1.0 / math.sqrt(2.0 * math.pi))
    grad_pre = (grad_act * (cumul + hidden_pre * density)).astype(jnp.bfloat16)
    up_grad = inner_rows(hidden_two, grad_pre)
    grad_hidden = outer_cols(grad_pre, up_weight)
    gain_two_grad = jnp.sum(grad_hidden * normed_two, axis=0)
    bias_two_grad = jnp.sum(grad_hidden, axis=0)
    grad_resid = grad_out + norm_back(
        grad_hidden * gain_two.astype(jnp.float32), normed_two, inverse_two
    )
    return (grad_resid, up_grad, down_grad, gain_two_grad, bias_two_grad)


def attn_back(grad_resid, saved, params):
    qkv_weight, out_weight, gain_one = (params[0], params[1], params[4])
    normed_one, inverse_one, hidden_one = (saved[1], saved[2], saved[3])
    queries, keys_all, values_all, probs, probs_low, attn_low = (
        saved[4],
        saved[5],
        saved[6],
        saved[7],
        saved[8],
        saved[9],
    )
    seq_len = grad_resid.shape[0]
    scale_factor = 1.0 / math.sqrt(HEAD_DIM)
    resid_low = grad_resid.astype(jnp.bfloat16)
    out_grad = inner_rows(attn_low, resid_low)
    grad_attn = (
        outer_cols(resid_low, out_weight).astype(jnp.bfloat16).reshape(seq_len, HEADS, HEAD_DIM)
    )
    grad_probs = jnp.einsum(
        "qhd,khd->hqk", grad_attn, values_all, preferred_element_type=jnp.float32
    )
    row_dot = jnp.sum(probs * grad_probs, axis=-1, keepdims=True)
    grad_scores = (probs * (grad_probs - row_dot)).astype(jnp.bfloat16)
    grad_values = jnp.einsum(
        "hqk,qhd->khd", probs_low, grad_attn, preferred_element_type=jnp.float32
    )
    grad_queries = (
        jnp.einsum("hqk,khd->qhd", grad_scores, keys_all, preferred_element_type=jnp.float32)
        * scale_factor
    )
    grad_keys = (
        jnp.einsum("hqk,qhd->khd", grad_scores, queries, preferred_element_type=jnp.float32)
        * scale_factor
    )
    grad_qkv = (
        jnp.stack([grad_queries, grad_keys, grad_values], axis=1)
        .reshape(seq_len, 3 * D)
        .astype(jnp.bfloat16)
    )
    qkv_grad = inner_rows(hidden_one, grad_qkv)
    grad_hidden = outer_cols(grad_qkv, qkv_weight)
    gain_one_grad = jnp.sum(grad_hidden * normed_one, axis=0)
    bias_one_grad = jnp.sum(grad_hidden, axis=0)
    input_grad = grad_resid + norm_back(
        grad_hidden * gain_one.astype(jnp.float32), normed_one, inverse_one
    )
    return (input_grad, qkv_grad, out_grad, gain_one_grad, bias_one_grad)


MESH_ID = pl.DeviceIdType.MESH


def aligned(index, size):
    return pl.ds(pl.multiple_of(index * size, size), size)


def greet(dp_index, fsdp_index, fsdp_size):
    barrier = pltpu.get_barrier_semaphore()
    peers = [(dp_index ^ 1, fsdp_index), (dp_index ^ 2, fsdp_index), (dp_index ^ 3, fsdp_index)]
    peers += [(dp_index, lax.rem(fsdp_index + k, fsdp_size)) for k in range(1, fsdp_size)]
    for peer in peers:
        pl.semaphore_signal(barrier, inc=1, device_id=peer, device_id_type=MESH_ID)
    pl.semaphore_wait(barrier, len(peers))


def send(src, dst, send_sem, recv_sem, device):
    return pltpu.make_async_remote_copy(
        src_ref=src,
        dst_ref=dst,
        send_sem=send_sem,
        recv_sem=recv_sem,
        device_id=device,
        device_id_type=MESH_ID,
    )


def gelu_parts(u):
    cumul = 0.5 * (1.0 + lax.erf(u * (1.0 / math.sqrt(2.0))))
    density = jnp.exp(-0.5 * u * u) * (1.0 / math.sqrt(2.0 * math.pi))
    return u * cumul, cumul + u * density


def head_scores(q_head, keys, key_valid):
    scores = outer_cols(q_head, keys) * (1.0 / math.sqrt(HEAD_DIM))
    masked = jnp.where(key_valid, scores, -1e30)
    expont = jnp.exp(masked - jnp.max(masked, axis=-1, keepdims=True))
    return expont / jnp.sum(expont, axis=-1, keepdims=True)


def transposed(target, source, fsdp_size):
    rows = target.shape[2]

    def body(n, carry):
        target[lax.rem(n, 2), lax.div(n, 2)] = jnp.transpose(source[:, aligned(n, rows)])
        return carry

    lax.fori_loop(0, fsdp_size, body, 0)


SLOTS = 2


def chunk_list(shapes):
    chunks = []
    for piece, (rows, span) in enumerate(shapes):
        part = span // 8
        high = min(rows, 128)
        width = 256 if part % 256 == 0 else 128
        for row in range(0, rows, high):
            for col in range(0, part, width):
                chunks.append((piece, row, high, part, col, width))
    return chunks


def layer_kernel(fsdp_size, chunks, *refs):
    pieces = 4
    count = len(chunks)
    column = fsdp_size // 2
    low, wide = jnp.bfloat16, jnp.float32
    length, scenes, cotangent = refs[:3]
    shards = refs[3:7]
    small = refs[7]
    fulls = refs[8:12]
    outs = refs[12:16]
    layer_out, input_grad, small_out = refs[16:19]
    rest = refs[19:]
    sum_b, one_b, two_b, zed_b, fin_b = (rest[i * count : (i + 1) * count] for i in range(5))
    rest = rest[5 * count :]
    other_b, core_b, big, small_full, hidden, hidden_t, qkv, attn, attn_t = rest[:9]
    resid, hidden_two_t, wide_low, slope, active_t, grad_low, grad_hidden, grad_resid = rest[9:17]
    small_g, small_a, small_b = rest[17:20]
    own_sem, az, bz, ax, bx, ay, by, ad, bd, ae, be, ac, bc, sv, rv = rest[20:35]
    (cs, cr, os_, or_, ts, tr, zs, zr, fs, fr, gs, gr, out_sem, ss, sr, us, ur) = rest[35:52]
    load_sem, credit = rest[52:]
    d = lax.axis_index("dp")
    f = lax.axis_index("fsdp")
    core = lax.rem(f, 2)
    place = lax.div(f, 2)
    bits = (lax.rem(d, 2), lax.div(d, 2))
    x_peer, y_peer, c_peer = (d ^ 1, f), (d ^ 2, f), (d, f ^ 1)
    peers = (x_peer, y_peer)
    seq_len = scenes.shape[0]
    ff = wide_low.shape[1]
    slots_other, slots_core = other_b.shape[0], core_b.shape[0]
    pending = []
    core_sends = {}

    def go(copy):
        copy.start()
        pending.append(copy)

    def arrived(view, send_sem, recv_sem, device):
        send(view, view, send_sem, recv_sem, device).wait_recv()

    def block(piece, place_from, quarter, half=None):
        rows = shards[piece].shape[0]
        span = shards[piece].shape[1] // 4
        row_part = aligned(place_from * 2 + core, rows)
        if half is None:
            return fulls[piece].at[row_part, aligned(quarter, span)]
        return fulls[piece].at[row_part, aligned(quarter * 2 + half, span // 2)]

    def to_partner(piece, view):
        send(view, view, ac.at[piece], bc.at[piece], c_peer).start()

    def source(k):
        return place ^ k

    def from_column(piece, k):
        at = (piece, k - 1)
        view = block(piece, source(k), d)
        arrived(view, az.at[at], bz.at[at], x_peer)
        go(send(view, view, ax.at[at], bx.at[at], x_peer))
        go(send(view, view, ay.at[at], by.at[at], y_peer))
        to_partner(piece, view)

    def from_sides(piece, k):
        at = (piece, k - 1)
        view = block(piece, source(k), d ^ 1)
        arrived(view, ax.at[at], bx.at[at], x_peer)
        part = block(piece, source(k), d ^ 1, 0)
        go(send(part, part, ad.at[at], bd.at[at], y_peer))
        to_partner(piece, view)
        view = block(piece, source(k), d ^ 2)
        arrived(view, ay.at[at], by.at[at], y_peer)
        part = block(piece, source(k), d ^ 2, 1)
        go(send(part, part, ae.at[at], be.at[at], x_peer))
        to_partner(piece, view)

    def from_corner(piece, k):
        at = (piece, k - 1)
        for half, (a, b, peer) in enumerate(((ad, bd, y_peer), (ae, be, x_peer))):
            part = block(piece, source(k), d ^ 3, half)
            arrived(part, a.at[at], b.at[at], peer)
            to_partner(piece, part)

    def from_partner(piece):
        rows = shards[piece].shape[0]
        view = fulls[piece].at[pl.ds(0, rows * column)]
        send(view, view, ac.at[piece], bc.at[piece], c_peer).wait()

    def loads(piece):
        if piece == 3:
            parts = [(fulls[3].at[pl.ds(n * D, D)], pl.ds(n * D, D)) for n in range(ff // D)]
        elif piece == 1:
            parts = [(fulls[1], pl.ds(3 * D, D))]
        else:
            parts = [
                (fulls[piece].at[:, pl.ds(n * D, D)], pl.ds(n * D, D))
                for n in range(fulls[piece].shape[1] // D)
            ]
        return [
            pltpu.make_async_copy(view, big.at[at], load_sem.at[piece, n])
            for n, (view, at) in enumerate(parts)
        ]

    def own_parts(piece, back):
        rows, span = shards[piece].shape
        first_row = sum(s.shape[0] * (s.shape[1] // D) for s in shards[:piece])
        parts = []
        for n in range(span // D):
            stage = big.at[pl.ds(first_row + n * rows, rows)]
            cols = pl.ds(n * D, D)
            whole = fulls[piece].at[aligned(f, rows), cols]
            ends = (stage, whole) if back else (shards[piece].at[:, cols], stage)
            parts.append(pltpu.make_async_copy(*ends, own_sem.at[int(back), piece, n]))
        return parts

    every = range(1, column)
    blocks = [(piece, k) for piece in range(pieces) for k in every]
    gather_order = []
    for n in range(len(blocks) + 4):
        for action, lag in ((from_column, 0), (from_sides, 1), (from_corner, 2)):
            if 0 <= n - lag < len(blocks):
                gather_order.append((action, *blocks[n - lag]))
    gathered = []

    def gather_step(limit=1):
        for _ in range(limit):
            if len(gathered) < len(gather_order):
                action, piece, k = gather_order[len(gathered)]
                gathered.append(1)
                action(piece, k)

    def gather_to(action, piece):
        last_one = gather_order.index((action, piece, column - 1))
        while len(gathered) <= last_one:
            gather_step()

    def slot_view(ref, slot, i):
        _, _, high, _, _, width = chunks[i]
        return ref.at[slot, :, pl.ds(0, column * high), pl.ds(0, width)]

    def grams(i, left_t, right):
        piece, row, high, part, col, width = chunks[i]
        slot = i % slots_other
        if i >= slots_other:
            core_sends[i - slots_other].wait_send()
        step = 2 if width == part and width == 128 else 1

        def fill(half, target):
            left = left_t[half, :, pl.ds(row, high), :].reshape(column * high, seq_len)

            def body(n, carry):
                start = pl.multiple_of(n * step * part + col, 128)
                found = jnp.dot(
                    left, right[:, pl.ds(start, step * width)], preferred_element_type=wide
                ).astype(low)
                for m in range(step):
                    target[n * step + m] = found[:, m * width : (m + 1) * width]
                return carry

            lax.fori_loop(0, 8 // step, body, 0)

        fill(1 - core, slot_view(other_b, slot, i))
        if i >= slots_core:
            pl.semaphore_wait(credit, 1)
        fill(core, sum_b[i])
        copy = send(
            slot_view(other_b, slot, i),
            slot_view(core_b, i % slots_core, i),
            cs.at[i],
            cr.at[i],
            c_peer,
        )
        copy.start()
        core_sends[i] = copy

    def add_into(target, other):
        rows = target.shape[0]
        strip = 64

        def body(n, carry):
            at = aligned(n, strip)
            target[at] = (target[at].astype(wide) + other[at].astype(wide)).astype(low)
            return carry

        lax.fori_loop(0, rows // strip, body, 0)

    def far_quarter(half, b):
        if half == 0:
            return (1 - bits[0]) + 2 * b
        return b + 2 * (1 - bits[1])

    def near_quarter(half, b):
        if half == 0:
            return bits[0] + 2 * b
        return b + 2 * bits[1]

    def pair(i):
        view = slot_view(core_b, i % slots_core, i)
        arrived(view, cs.at[i], cr.at[i], c_peer)

        def add(quarter, half):
            add_into(sum_b[i].at[quarter * 2 + half], view.at[quarter * 2 + half])

        for b in range(2):
            for half in range(2):
                add(far_quarter(half, b), half)
            for half in range(2):
                go(
                    send(
                        sum_b[i].at[far_quarter(half, b) * 2 + half],
                        one_b[i].at[half, b],
                        os_.at[i, half, b],
                        or_.at[i, half, b],
                        peers[half],
                    )
                )
        for b in range(2):
            for half in range(2):
                add(near_quarter(half, b), half)
        if i + slots_core < count:
            pl.semaphore_signal(credit, inc=1, device_id=c_peer, device_id_type=MESH_ID)

    def first(i):
        for half in range(2):
            for b in range(2):
                arrived(one_b[i].at[half, b], os_.at[i, half, b], or_.at[i, half, b], peers[half])
                add_into(sum_b[i].at[near_quarter(half, b) * 2 + half], one_b[i].at[half, b])
            other = d ^ 2 if half == 0 else d ^ 1
            go(
                send(
                    sum_b[i].at[other * 2 + half],
                    two_b[i].at[half],
                    ts.at[i, half],
                    tr.at[i, half],
                    peers[1 - half],
                )
            )

    def second(i):
        _, _, high, _, _, _ = chunks[i]
        for half in range(2):
            arrived(two_b[i].at[half], ts.at[i, half], tr.at[i, half], peers[1 - half])
            mine = sum_b[i].at[d * 2 + half]
            add_into(mine, two_b[i].at[half])
            for k in range(1, column):
                to = place ^ k
                go(
                    send(
                        mine.at[aligned(to, high)],
                        zed_b[i].at[half, k - 1],
                        zs.at[i, half, k - 1],
                        zr.at[i, half, k - 1],
                        (d, to * 2 + core),
                    )
                )

    def result(i, quarter, half):
        piece, row, high, part, col, width = chunks[i]
        start = pl.multiple_of((quarter * 2 + half) * part + col, 128)
        return outs[piece].at[pl.ds(row, high), pl.ds(start, width)]

    def last(i):
        _, _, high, _, _, _ = chunks[i]
        for half in range(2):
            for k in range(1, column):
                at = (i, half, k - 1)
                arrived(zed_b[i].at[half, k - 1], zs.at[at], zr.at[at], c_peer)
            total = sum_b[i][d * 2 + half, aligned(place, high)].astype(wide)
            for k in range(1, column):
                total = total + zed_b[i][half, k - 1].astype(wide)
            fin_b[i][half] = total.astype(low)
        for half in range(2):
            mine = result(i, d, half)
            pltpu.make_async_copy(fin_b[i].at[half], mine, out_sem.at[i, half]).start()
            for axis in range(2):
                at = (i, half, axis)
                go(send(fin_b[i].at[half], mine, fs.at[at], fr.at[at], peers[axis]))

    def spread(i):
        for half in range(2):
            for axis in range(2):
                at = (i, half, axis)
                view = result(i, d ^ (1 + axis), half)
                arrived(view, fs.at[at], fr.at[at], peers[axis])
                if half == axis:
                    go(send(view, view, gs.at[i, half], gr.at[i, half], peers[1 - axis]))

    def finish(i):
        for half in range(2):
            view = result(i, d ^ 3, half)
            arrived(view, gs.at[i, half], gr.at[i, half], peers[1 - half])
            pltpu.make_async_copy(fin_b[i].at[half], result(i, d, half), out_sem.at[i, half]).wait()

    stages = (first, second, last, spread, finish)
    order = []
    lags = (0, 2, 3, 4, 5)
    for step in range(count + lags[-1]):
        for stage, lag in zip(stages, lags):
            if 0 <= step - lag < count:
                order.append((stage, step - lag))
    done = []
    waiting = []
    paired = []

    def pair_up(keep=0):
        while len(waiting) > keep:
            i = waiting.pop(0)
            pair(i)
            paired.append(i)

    owed = [0]

    def advance(limit):
        steps, owed[0] = divmod(owed[0] + limit, 2)
        for _ in range(steps):
            if len(done) < len(order) and order[len(done)][1] in paired:
                stage, i = order[len(done)]
                done.append(1)
                stage(i)

    def pump(limit=1):
        pair_up()
        advance(limit)

    def produce(some, left_t, right, limit, keep=1):
        for i in some:
            pair_up(slots_core - 1)
            grams(i, left_t, right)
            waiting.append(i)
            pair_up(keep)
            advance(limit)

    by_piece = [[i for i in range(count) if chunks[i][0] == piece] for piece in range(pieces)]

    greet(d, f, fsdp_size)
    small_rows = small.shape[0]
    for k in range(1, fsdp_size):
        to = lax.rem(f + k, fsdp_size)
        go(send(small, small_full.at[aligned(f, small_rows)], sv.at[k - 1], rv.at[k - 1], (d, to)))
    own_small = pltpu.make_async_copy(
        small, small_full.at[aligned(f, small_rows)], own_sem.at[0, 0, pieces]
    )
    own_small.start()
    for piece in range(pieces):
        rows, span = shards[piece].shape
        for k in every:
            go(
                send(
                    shards[piece].at[:, aligned(d, span // 4)],
                    block(piece, place, d),
                    az.at[piece, k - 1],
                    bz.at[piece, k - 1],
                    (d, (place ^ k) * 2 + core),
                )
            )
        own = fulls[piece].at[aligned(f, rows)]
        send(shards[piece], own, ac.at[piece], bc.at[piece], c_peer).start()
        for copy in own_parts(piece, False):
            copy.start()
    for piece in range(pieces):
        for copy in own_parts(piece, False):
            copy.wait()
        for copy in own_parts(piece, True):
            copy.start()

    normed_one, _ = norm_rows(scenes[...].astype(wide))
    for k in range(1, fsdp_size):
        view = small_full.at[aligned(lax.rem(f - k + fsdp_size, fsdp_size), small_rows)]
        arrived(view, sv.at[k - 1], rv.at[k - 1], c_peer)
    own_small.wait()

    def vector(row):
        values = small_full[...].astype(wide)
        at = range(row, small_rows * fsdp_size, small_rows)
        return jnp.concatenate([values[n : n + 1] for n in at], axis=1)

    hidden[...] = (normed_one * vector(0) + vector(1)).astype(low)
    gather_step(2)
    transposed(hidden_t, hidden, fsdp_size)
    for piece in range(pieces):
        for copy in own_parts(piece, True):
            copy.wait()
    gather_to(from_corner, 0)
    gather_step(3)
    from_partner(0)
    for copy in loads(0):
        copy.start()
    gather_step(1)
    for copy in loads(0):
        copy.wait()

    def project(n, carry):
        cols = aligned(n, 512)
        rows = aligned(lax.div(n, D // 512), D)
        weight = big[rows, aligned(lax.rem(n, D // 512), 512)]
        qkv[:, cols] = jnp.dot(hidden[...], weight, preferred_element_type=wide).astype(low)
        return carry

    tiles = qkv.shape[1] // 512
    lax.fori_loop(0, tiles // 2, project, 0)
    gather_step(2)
    lax.fori_loop(tiles // 2, tiles, project, 0)
    gather_step(2)
    key_valid = lax.broadcasted_iota(jnp.int32, (1, seq_len), 1) < length[0]
    row_valid = lax.broadcasted_iota(jnp.int32, (seq_len, 1), 0) < length[0]
    first_half = lax.broadcasted_iota(jnp.int32, (1, 128), 1) < HEAD_DIM
    halves = (first_half.astype(wide).astype(low), 1 - first_half.astype(wide).astype(low))
    pairs = D // 128

    def attend(j, carry):
        queries, keys, values = (qkv[:, aligned(j + i * pairs, 128)] for i in range(3))
        found = []
        for half in halves:
            probs = head_scores(queries * half, keys, key_valid)
            found.append(jnp.dot(probs.astype(low), values, preferred_element_type=wide))
        attn[:, aligned(j, 128)] = jnp.where(first_half, found[0], found[1]).astype(low)
        return carry

    for j in range(0, pairs, 2):
        lax.fori_loop(j, j + 2, attend, 0)
        gather_step(2)
    transposed(attn_t, attn, fsdp_size)
    gather_to(from_corner, 1)
    gather_step(1)
    from_partner(1)
    for copy in loads(1):
        copy.start()
    for copy in loads(1):
        copy.wait()

    def second_in(n, carry):
        cols = aligned(n, 512)
        resid[:, cols] = scenes[:, cols].astype(wide) + jnp.dot(
            attn[...], big[pl.ds(3 * D, D), cols], preferred_element_type=wide
        )
        return carry

    lax.fori_loop(0, D // 512, second_in, 0)
    normed_two, _ = norm_rows(resid[...])
    hidden[...] = (normed_two * vector(2) + vector(3)).astype(low)
    transposed(hidden_two_t, hidden, fsdp_size)
    gather_to(from_corner, 2)
    gather_step(2)
    from_partner(2)
    for copy in loads(2):
        copy.start()
    span = D // 256

    def expand(n, carry):
        cols = aligned(n, 256)
        rows = aligned(lax.div(n, span), D)
        weight = big[rows, aligned(lax.rem(n, span), 256)]
        acts, grads = gelu_parts(jnp.dot(hidden[...], weight, preferred_element_type=wide))
        wide_low[:, cols] = acts.astype(low)
        slope[:, cols] = grads.astype(low)
        return carry

    for part, copy in enumerate(loads(2)):
        copy.wait()
        lax.fori_loop(part * span, (part + 1) * span, expand, 0)
        gather_step(2)
    transposed(active_t, wide_low, fsdp_size)
    grad_low[...] = jnp.where(row_valid, cotangent[...].astype(wide), 0.0).astype(low)
    early = by_piece[0][: slots_core - 1]
    produce(early, active_t, grad_low, 0, slots_core)
    gather_to(from_sides, pieces - 1)
    pair_up()
    gather_to(from_corner, pieces - 1)
    produce(by_piece[0][len(early) :][:1], active_t, grad_low, 0)
    from_partner(3)
    for copy in loads(3):
        copy.start()
    produce(by_piece[0][len(early) + 1 :], active_t, grad_low, 0)
    for part, copy in enumerate(loads(3)):
        copy.wait()
        at = pl.ds(part * D, D)
        term = jnp.dot(wide_low[:, at], big[at], preferred_element_type=wide)
        if part == 0:
            grad_hidden[...] = resid[...] + term
        else:
            grad_hidden[...] += term
        pair_up()
    layer_out[...] = jnp.where(row_valid, grad_hidden[...], 0.0).astype(low)
    pump(1)

    tile = 512

    def pre(n, carry):
        at = aligned(n, tile)
        back = outer_cols(grad_low[...], big[at])
        wide_low[:, at] = (back * slope[:, at].astype(wide)).astype(low)
        return carry

    for n in range(0, ff // tile, 2):
        lax.fori_loop(n, n + 2, pre, 0)
        pump(1)
    for copy in loads(2):
        copy.start()
    produce(by_piece[1], hidden_two_t, wide_low, 2)
    for part, copy in enumerate(loads(2)):
        copy.wait()
        back = outer_cols(wide_low[:, pl.ds(part * D, D)], big[pl.ds(part * D, D)])
        if part == 0:
            grad_hidden[...] = back
        else:
            grad_hidden[...] += back
        pump(1)
    for piece in (1, 0):
        for copy in loads(piece):
            copy.start()
    pump(1)

    def norm_step(values, grads, gain, base, row):
        normed, inverse = norm_rows(values)
        rows = D // fsdp_size
        for n, total in enumerate((grads * normed, grads)):
            sums = jnp.sum(total, axis=0, keepdims=True)
            for to in range(fsdp_size):
                small_g[to, row + n : row + n + 1, :] = sums[:, to * rows : (to + 1) * rows]
        return base + norm_back(grads * gain, normed, inverse)

    small_g[...] = jnp.zeros_like(small_g)
    base = jnp.where(row_valid, cotangent[...].astype(wide), 0.0)
    grad_resid[...] = norm_step(resid[...], grad_hidden[...], vector(2), base, 2)
    grad_low[...] = grad_resid[...].astype(low)
    pump(1)
    produce(by_piece[2], attn_t, grad_low, 2)
    for copy in loads(1):
        copy.wait()

    def attn_in(n, carry):
        rows = pl.ds(pl.multiple_of(3 * D + n * 256, 256), 256)
        attn[:, aligned(n, 256)] = outer_cols(grad_low[...], big[rows]).astype(low)
        return carry

    lax.fori_loop(0, D // 256, attn_in, 0)
    pump(1)
    factor = 1.0 / math.sqrt(HEAD_DIM)

    def attend_back(j, carry):
        queries, keys, values = (qkv[:, aligned(j + i * pairs, 128)] for i in range(3))
        grads = attn[:, aligned(j, 128)]
        found = []
        for half in halves:
            probs = head_scores(queries * half, keys, key_valid)
            grad_probs = outer_cols(grads * half, values)
            row_dot = jnp.sum(probs * grad_probs, axis=-1, keepdims=True)
            scores = (probs * (grad_probs - row_dot)).astype(low)
            found.append(
                (
                    jnp.dot(scores, keys, preferred_element_type=wide) * factor,
                    inner_rows(scores, queries) * factor,
                    inner_rows(probs.astype(low), grads),
                )
            )
        for i in range(3):
            wide_low[:, aligned(j + i * pairs, 128)] = jnp.where(
                first_half, found[0][i], found[1][i]
            ).astype(low)
        return carry

    for j in range(0, pairs, 2):
        lax.fori_loop(j, j + 2, attend_back, 0)
        pump(1)
    produce(by_piece[3], hidden_t, wide_low, 2)
    for part, copy in enumerate(loads(0)):
        copy.wait()
        total = outer_cols(wide_low[:, pl.ds(part * D, D)], big[pl.ds(part * D, D)])
        if part == 0:
            grad_hidden[...] = total
        else:
            grad_hidden[...] += total
    pump(1)
    total = norm_step(scenes[...].astype(wide), grad_hidden[...], vector(0), grad_resid[...], 0)
    input_grad[...] = total.astype(low)
    for k in range(1, fsdp_size):
        to = lax.rem(f + k, fsdp_size)
        go(send(small_g.at[to], small_a.at[k - 1], ss.at[k - 1], sr.at[k - 1], (d, to)))
    pump(2)
    total = small_g[f]
    for k in range(1, fsdp_size):
        arrived(small_a.at[k - 1], ss.at[k - 1], sr.at[k - 1], c_peer)
        total = total + small_a[k - 1]
    small_b[d] = total
    pump(2)
    for k in range(1, 4):
        go(send(small_b.at[d], small_b.at[d], us.at[k - 1], ur.at[k - 1], (d ^ k, f)))
    pump(4)
    for k in range(1, 4):
        arrived(small_b.at[d ^ k], us.at[k - 1], ur.at[k - 1], c_peer)
    small_out[...] = (small_b[0] + small_b[1]) + (small_b[2] + small_b[3])
    pump(2 * len(order))
    for copy in pending:
        copy.wait_send()
    for i in range(max(0, count - slots_other), count):
        core_sends[i].wait_send()


def layer_step(fsdp_size, length, scenes, cotangent, shards, small):
    column = fsdp_size // 2
    hops = column - 1
    seq_len = scenes.shape[0]
    ff = shards[3].shape[0] * fsdp_size
    low, wide = jnp.bfloat16, jnp.float32
    by_need = (shards[3], shards[2], shards[1], shards[0])
    chunks = chunk_list([w.shape for w in by_need])
    count = len(chunks)
    hbm = pl.BlockSpec(memory_space=pltpu.HBM)
    vmem = pl.BlockSpec(memory_space=pltpu.VMEM)
    smem = pl.BlockSpec(memory_space=pltpu.SMEM)
    dma = pltpu.SemaphoreType.DMA
    shape = jax.ShapeDtypeStruct
    scratch = []
    for kind in ("sum", "one", "two", "zed", "fin"):
        for _, _, high, _, _, width in chunks:
            buffers = {
                "sum": (8, column * high, width),
                "one": (2, 2, column * high, width),
                "two": (2, column * high, width),
                "zed": (2, hops, high, width),
                "fin": (2, high, width),
            }
            scratch.append(pltpu.VMEM(buffers[kind], low))
    tall = max(c[2] for c in chunks) * column
    broad = max(c[5] for c in chunks)
    rows = D // fsdp_size
    turned = pltpu.VMEM((2, column, rows, seq_len), low)
    scratch += [pltpu.VMEM((SLOTS, 8, tall, broad), low)] * 2
    scratch += [
        pltpu.VMEM((ff, D), low),
        pltpu.VMEM((small.shape[0] * fsdp_size, small.shape[1]), low),
        pltpu.VMEM((seq_len, D), low),
        turned,
        pltpu.VMEM((seq_len, 3 * D), low),
        pltpu.VMEM((seq_len, D), low),
        turned,
        pltpu.VMEM((seq_len, D), wide),
        turned,
        pltpu.VMEM((seq_len, ff), low),
        pltpu.VMEM((seq_len, ff), low),
        pltpu.VMEM((2, column, ff // fsdp_size, seq_len), low),
        pltpu.VMEM((seq_len, D), low),
        pltpu.VMEM((seq_len, D), wide),
        pltpu.VMEM((seq_len, D), wide),
        pltpu.VMEM((fsdp_size, 8, rows), wide),
        pltpu.VMEM((fsdp_size - 1, 8, rows), wide),
        pltpu.VMEM((4, 8, rows), wide),
    ]
    scratch += [dma((2, 4, 5))] + [dma((4, hops))] * 10 + [dma((4,))] * 2 + [dma((fsdp_size - 1,))] * 2
    scratch += [dma((count,))] * 2 + [dma((count, 2, 2))] * 2 + [dma((count, 2))] * 2
    scratch += [dma((count, 2, hops))] * 2 + [dma((count, 2, 2))] * 2 + [dma((count, 2))] * 2
    scratch += [dma((count, 2))] + [dma((fsdp_size - 1,))] * 2 + [dma((3,))] * 2
    scratch += [dma((4, 4)), pltpu.SemaphoreType.REGULAR]
    return pl.pallas_call(
        functools.partial(layer_kernel, fsdp_size, chunks),
        out_shape=[shape((a.shape[0] * fsdp_size, a.shape[1]), low) for a in shards]
        + [shape(w.shape, low) for w in by_need]
        + [shape((seq_len, D), low)] * 2
        + [shape((8, rows), wide)],
        in_specs=[smem, vmem, vmem] + [hbm] * 5,
        out_specs=[hbm] * 8 + [vmem] * 3,
        scratch_shapes=scratch,
        compiler_params=pltpu.CompilerParams(
            collective_id=0, has_side_effects=True, vmem_limit_bytes=67043328
        ),
        name="layer_step",
    )(length, scenes, cotangent, *shards, small)


def widen_kernel(parts, *refs):
    count = len(parts)
    small = refs[6]
    outs, small_outs = refs[7:13], refs[13:17]
    stages, wides = refs[17 : 17 + count], refs[17 + count : 17 + 2 * count]
    in_sem, out_sem = refs[17 + 2 * count :]
    copies = []
    for n, (which, at) in enumerate(parts):
        copies.append(pltpu.make_async_copy(refs[which].at[at], stages[n], in_sem.at[n]))
        copies[n].start()
    for row, out in enumerate(small_outs):
        out[...] = small[row]
    backs = []
    for n, (which, at) in enumerate(parts):
        copies[n].wait()
        source = stages[n]
        if outs[which].dtype != source.dtype:
            wides[n][...] = source[...].astype(jnp.float32)
            source = wides[n]
        backs.append(pltpu.make_async_copy(source, outs[which].at[at], out_sem.at[n]))
        backs[n].start()
    for copy in backs:
        copy.wait()


def widen(sums, rows, small):
    low, wide = jnp.bfloat16, jnp.float32
    parts, stages, wides = [], [], []
    for which, array in enumerate((*sums, *rows)):
        high, span = array.shape
        step = max(16, min(high, 1 << ((BLOCK // span).bit_length() - 1)))
        for row in range(0, high, step):
            parts.append((which, pl.ds(row, step)))
            stages.append(pltpu.VMEM((step, span), low))
            wides.append(pltpu.VMEM((step, span) if which < len(sums) else (8, 128), wide))
    shape = jax.ShapeDtypeStruct
    hbm = pl.BlockSpec(memory_space=pltpu.HBM)
    vmem = pl.BlockSpec(memory_space=pltpu.VMEM)
    dma = pltpu.SemaphoreType.DMA
    return pl.pallas_call(
        functools.partial(widen_kernel, parts),
        out_shape=[shape(a.shape, wide) for a in sums]
        + [shape(a.shape, low) for a in rows]
        + [shape((small.shape[1],), wide)] * 4,
        in_specs=[hbm] * 6 + [vmem],
        out_specs=[hbm] * 6 + [vmem] * 4,
        scratch_shapes=stages + wides + [dma((len(parts),))] * 2,
        compiler_params=pltpu.CompilerParams(vmem_limit_bytes=67043328),
        name="widen",
    )(*sums, *rows, small)


BLOCK = 131072


def on_device_wide(
    scenes_in,
    scene_lengths,
    cotangent,
    qkv_weight,
    out_weight,
    up_weight,
    down_weight,
    gain_one,
    bias_one,
    gain_two,
    bias_two,
):
    params = (
        lax.all_gather(qkv_weight, "fsdp", axis=0, tiled=True),
        lax.all_gather(out_weight, "fsdp", axis=0, tiled=True),
        lax.all_gather(up_weight, "fsdp", axis=0, tiled=True),
        lax.all_gather(down_weight, "fsdp", axis=0, tiled=True),
        lax.all_gather(gain_one, "fsdp", axis=0, tiled=True),
        lax.all_gather(bias_one, "fsdp", axis=0, tiled=True),
        lax.all_gather(gain_two, "fsdp", axis=0, tiled=True),
        lax.all_gather(bias_two, "fsdp", axis=0, tiled=True),
    )
    inputs = scenes_in[0].astype(jnp.float32)
    seq_len = inputs.shape[0]
    positions = jnp.arange(seq_len, dtype=jnp.int32)
    key_valid = positions < scene_lengths[0]
    row_mask = key_valid.astype(jnp.float32)[:, None]
    saved = forward_pass(inputs, key_valid, params)
    layer_out = (saved[0] * row_mask).astype(jnp.bfloat16)[None]
    grad_out = cotangent[0].astype(jnp.float32) * row_mask
    params_back = (
        lax.all_gather(qkv_weight, "fsdp", axis=0, tiled=True),
        lax.all_gather(out_weight, "fsdp", axis=0, tiled=True),
        lax.all_gather(up_weight, "fsdp", axis=0, tiled=True),
        lax.all_gather(down_weight, "fsdp", axis=0, tiled=True),
        lax.all_gather(gain_one, "fsdp", axis=0, tiled=True),
        lax.all_gather(bias_one, "fsdp", axis=0, tiled=True),
        lax.all_gather(gain_two, "fsdp", axis=0, tiled=True),
        lax.all_gather(bias_two, "fsdp", axis=0, tiled=True),
    )
    saved_back = forward_pass(inputs, key_valid, params_back)
    grad_resid, up_grad, down_grad, gain_two_grad, bias_two_grad = mlp_back(
        grad_out, saved_back, params_back
    )
    input_grad, qkv_grad, out_grad, gain_one_grad, bias_one_grad = attn_back(
        grad_resid, saved_back, params_back
    )
    shares = (
        lax.psum_scatter(qkv_grad, "fsdp", scatter_dimension=0, tiled=True),
        lax.psum_scatter(out_grad, "fsdp", scatter_dimension=0, tiled=True),
        lax.psum_scatter(up_grad, "fsdp", scatter_dimension=0, tiled=True),
        lax.psum_scatter(down_grad, "fsdp", scatter_dimension=0, tiled=True),
        lax.psum_scatter(gain_one_grad, "fsdp", scatter_dimension=0, tiled=True),
        lax.psum_scatter(bias_one_grad, "fsdp", scatter_dimension=0, tiled=True),
        lax.psum_scatter(gain_two_grad, "fsdp", scatter_dimension=0, tiled=True),
        lax.psum_scatter(bias_two_grad, "fsdp", scatter_dimension=0, tiled=True),
    )
    summed = (
        lax.psum(shares[0].astype(jnp.bfloat16), "dp").astype(jnp.float32),
        lax.psum(shares[1].astype(jnp.bfloat16), "dp").astype(jnp.float32),
        lax.psum(shares[2].astype(jnp.bfloat16), "dp").astype(jnp.float32),
        lax.psum(shares[3].astype(jnp.bfloat16), "dp").astype(jnp.float32),
        lax.psum(shares[4].astype(jnp.bfloat16), "dp").astype(jnp.float32),
        lax.psum(shares[5].astype(jnp.bfloat16), "dp").astype(jnp.float32),
        lax.psum(shares[6].astype(jnp.bfloat16), "dp").astype(jnp.float32),
        lax.psum(shares[7].astype(jnp.bfloat16), "dp").astype(jnp.float32),
    )
    qkv_total, out_total, up_total, down_total = (summed[0], summed[1], summed[2], summed[3])
    gain_one_total, bias_one_total, gain_two_total, bias_two_total = (
        summed[4],
        summed[5],
        summed[6],
        summed[7],
    )
    input_out = input_grad.astype(jnp.bfloat16)[None]
    return (
        layer_out,
        input_out,
        qkv_total,
        out_total,
        up_total,
        down_total,
        gain_one_total,
        bias_one_total,
        gain_two_total,
        bias_two_total,
    )


def on_device(
    scenes_in,
    scene_lengths,
    cotangent,
    qkv_weight,
    out_weight,
    up_weight,
    down_weight,
    gain_one,
    bias_one,
    gain_two,
    bias_two,
):
    rows = gain_one.shape[0]
    fsdp_size = D // rows
    small = jnp.stack([gain_one, bias_one, gain_two, bias_two])
    small = jnp.pad(small, ((0, 12), (0, 0)))
    results = layer_step(
        fsdp_size,
        scene_lengths,
        scenes_in[0],
        cotangent[0],
        (qkv_weight, out_weight, up_weight, down_weight),
        small,
    )
    down_sum, up_sum, out_sum, qkv_sum, layer_out, input_grad, small_sum = results[4:]
    wide = widen((qkv_sum, out_sum, up_sum, down_sum), (layer_out, input_grad), small_sum)
    return (wide[4][None], wide[5][None], *wide[:4], *wide[6:])


def solution(mesh):
    placed = (
        P(("dp", "fsdp"), None, None),
        P(("dp", "fsdp")),
        P(("dp", "fsdp"), None, None),
        P("fsdp", None),
        P("fsdp", None),
        P("fsdp", None),
        P("fsdp", None),
        P("fsdp"),
        P("fsdp"),
        P("fsdp"),
        P("fsdp"),
    )
    body = on_device if mesh.shape["dp"] == 4 and mesh.shape["fsdp"] == 8 else on_device_wide
    return jax.shard_map(
        body,
        mesh=mesh,
        in_specs=placed,
        out_specs=(
            P(("dp", "fsdp"), None, None),
            P(("dp", "fsdp"), None, None),
            P("fsdp", None),
            P("fsdp", None),
            P("fsdp", None),
            P("fsdp", None),
            P("fsdp"),
            P("fsdp"),
            P("fsdp"),
            P("fsdp"),
        ),
        check_vma=False,
    )
```

```python
import functools
import math

import jax
import jax.numpy as jnp
from jax import lax
from jax.experimental import pallas as pl
from jax.experimental.pallas import tpu as pltpu
from jax.sharding import PartitionSpec as P

D = 1024
HEADS = 16
HEAD_DIM = 64


epsilon = 1e-05


def norm_rows(values_in):
    row_mean = jnp.mean(values_in, axis=-1, keepdims=True)
    centered = values_in - row_mean
    variance = jnp.mean(centered * centered, axis=-1, keepdims=True)
    inverse = lax.rsqrt(variance + epsilon)
    return (centered * inverse, inverse)


def norm_back(grad_normed, normed, inverse):
    first_mean = jnp.mean(grad_normed, axis=-1, keepdims=True)
    second_mean = jnp.mean(grad_normed * normed, axis=-1, keepdims=True)
    return inverse * (grad_normed - first_mean - normed * second_mean)


def inner_rows(left, right):
    return lax.dot_general(
        left, right, (((0,), (0,)), ((), ())), preferred_element_type=jnp.float32
    )


def outer_cols(left, right):
    return lax.dot_general(
        left, right, (((1,), (1,)), ((), ())), preferred_element_type=jnp.float32
    )


def forward_pass(inputs, key_valid, params):
    qkv_weight, out_weight, up_weight, down_weight, gain_one, bias_one, gain_two, bias_two = params
    seq_len = inputs.shape[0]
    normed_one, inverse_one = norm_rows(inputs)
    hidden_one = (normed_one * gain_one.astype(jnp.float32) + bias_one.astype(jnp.float32)).astype(
        jnp.bfloat16
    )
    qkv_low = jnp.dot(hidden_one, qkv_weight, preferred_element_type=jnp.float32).astype(
        jnp.bfloat16
    )
    split_view = qkv_low.reshape(seq_len, 3, HEADS, HEAD_DIM)
    queries = split_view[:, 0]
    keys_all = split_view[:, 1]
    values_all = split_view[:, 2]
    scale_factor = 1.0 / math.sqrt(HEAD_DIM)
    scores = (
        jnp.einsum("qhd,khd->hqk", queries, keys_all, preferred_element_type=jnp.float32)
        * scale_factor
    )
    masked = jnp.where(key_valid[None, None, :], scores, -1e30)
    highest = jnp.max(masked, axis=-1, keepdims=True)
    expont = jnp.exp(masked - highest)
    probs = expont / jnp.sum(expont, axis=-1, keepdims=True)
    probs_low = probs.astype(jnp.bfloat16)
    attended = jnp.einsum("hqk,khd->qhd", probs_low, values_all, preferred_element_type=jnp.float32)
    attn_low = attended.reshape(seq_len, D).astype(jnp.bfloat16)
    resid_one = inputs + jnp.dot(attn_low, out_weight, preferred_element_type=jnp.float32)
    normed_two, inverse_two = norm_rows(resid_one)
    hidden_two = (normed_two * gain_two.astype(jnp.float32) + bias_two.astype(jnp.float32)).astype(
        jnp.bfloat16
    )
    hidden_pre = jnp.dot(hidden_two, up_weight, preferred_element_type=jnp.float32)
    activated = jax.nn.gelu(hidden_pre, approximate=False).astype(jnp.bfloat16)
    result = resid_one + jnp.dot(activated, down_weight, preferred_element_type=jnp.float32)
    return (
        result,
        normed_one,
        inverse_one,
        hidden_one,
        queries,
        keys_all,
        values_all,
        probs,
        probs_low,
        attn_low,
        normed_two,
        inverse_two,
        hidden_two,
        hidden_pre,
        activated,
    )


def mlp_back(grad_out, saved, params):
    up_weight, down_weight, gain_two = (params[2], params[3], params[6])
    normed_two, inverse_two, hidden_two, hidden_pre, activated = (
        saved[10],
        saved[11],
        saved[12],
        saved[13],
        saved[14],
    )
    grad_low = grad_out.astype(jnp.bfloat16)
    down_grad = inner_rows(activated, grad_low)
    grad_act = outer_cols(grad_low, down_weight)
    cumul = 0.5 * (1.0 + lax.erf(hidden_pre * (1.0 / math.sqrt(2.0))))
    density = jnp.exp(-0.5 * hidden_pre * hidden_pre) * (1.0 / math.sqrt(2.0 * math.pi))
    grad_pre = (grad_act * (cumul + hidden_pre * density)).astype(jnp.bfloat16)
    up_grad = inner_rows(hidden_two, grad_pre)
    grad_hidden = outer_cols(grad_pre, up_weight)
    gain_two_grad = jnp.sum(grad_hidden * normed_two, axis=0)
    bias_two_grad = jnp.sum(grad_hidden, axis=0)
    grad_resid = grad_out + norm_back(
        grad_hidden * gain_two.astype(jnp.float32), normed_two, inverse_two
    )
    return (grad_resid, up_grad, down_grad, gain_two_grad, bias_two_grad)


def attn_back(grad_resid, saved, params):
    qkv_weight, out_weight, gain_one = (params[0], params[1], params[4])
    normed_one, inverse_one, hidden_one = (saved[1], saved[2], saved[3])
    queries, keys_all, values_all, probs, probs_low, attn_low = (
        saved[4],
        saved[5],
        saved[6],
        saved[7],
        saved[8],
        saved[9],
    )
    seq_len = grad_resid.shape[0]
    scale_factor = 1.0 / math.sqrt(HEAD_DIM)
    resid_low = grad_resid.astype(jnp.bfloat16)
    out_grad = inner_rows(attn_low, resid_low)
    grad_attn = (
        outer_cols(resid_low, out_weight).astype(jnp.bfloat16).reshape(seq_len, HEADS, HEAD_DIM)
    )
    grad_probs = jnp.einsum(
        "qhd,khd->hqk", grad_attn, values_all, preferred_element_type=jnp.float32
    )
    row_dot = jnp.sum(probs * grad_probs, axis=-1, keepdims=True)
    grad_scores = (probs * (grad_probs - row_dot)).astype(jnp.bfloat16)
    grad_values = jnp.einsum(
        "hqk,qhd->khd", probs_low, grad_attn, preferred_element_type=jnp.float32
    )
    grad_queries = (
        jnp.einsum("hqk,khd->qhd", grad_scores, keys_all, preferred_element_type=jnp.float32)
        * scale_factor
    )
    grad_keys = (
        jnp.einsum("hqk,qhd->khd", grad_scores, queries, preferred_element_type=jnp.float32)
        * scale_factor
    )
    grad_qkv = (
        jnp.stack([grad_queries, grad_keys, grad_values], axis=1)
        .reshape(seq_len, 3 * D)
        .astype(jnp.bfloat16)
    )
    qkv_grad = inner_rows(hidden_one, grad_qkv)
    grad_hidden = outer_cols(grad_qkv, qkv_weight)
    gain_one_grad = jnp.sum(grad_hidden * normed_one, axis=0)
    bias_one_grad = jnp.sum(grad_hidden, axis=0)
    input_grad = grad_resid + norm_back(
        grad_hidden * gain_one.astype(jnp.float32), normed_one, inverse_one
    )
    return (input_grad, qkv_grad, out_grad, gain_one_grad, bias_one_grad)


MESH_ID = pl.DeviceIdType.MESH


def aligned(index, size):
    return pl.ds(pl.multiple_of(index * size, size), size)


def greet(dp_index, fsdp_index, fsdp_size):
    barrier = pltpu.get_barrier_semaphore()
    peers = [(dp_index ^ 1, fsdp_index), (dp_index ^ 2, fsdp_index), (dp_index ^ 3, fsdp_index)]
    peers += [(dp_index, lax.rem(fsdp_index + k, fsdp_size)) for k in range(1, fsdp_size)]
    for peer in peers:
        pl.semaphore_signal(barrier, inc=1, device_id=peer, device_id_type=MESH_ID)
    pl.semaphore_wait(barrier, len(peers))


def send(src, dst, send_sem, recv_sem, device):
    return pltpu.make_async_remote_copy(
        src_ref=src,
        dst_ref=dst,
        send_sem=send_sem,
        recv_sem=recv_sem,
        device_id=device,
        device_id_type=MESH_ID,
    )


def gelu_parts(u):
    cumul = 0.5 * (1.0 + lax.erf(u * (1.0 / math.sqrt(2.0))))
    density = jnp.exp(-0.5 * u * u) * (1.0 / math.sqrt(2.0 * math.pi))
    return u * cumul, cumul + u * density


def head_scores(q_head, keys, key_valid):
    scores = outer_cols(q_head, keys) * (1.0 / math.sqrt(HEAD_DIM))
    masked = jnp.where(key_valid, scores, -1e30)
    expont = jnp.exp(masked - jnp.max(masked, axis=-1, keepdims=True))
    return expont / jnp.sum(expont, axis=-1, keepdims=True)


def transposed(target, source, fsdp_size):
    rows = target.shape[2]

    def body(n, carry):
        target[lax.rem(n, 2), lax.div(n, 2)] = jnp.transpose(source[:, aligned(n, rows)])
        return carry

    lax.fori_loop(0, fsdp_size, body, 0)


SLOTS = 2


def chunk_list(shapes):
    chunks = []
    for piece, (rows, span) in enumerate(shapes):
        part = span // 8
        high = min(rows, 128)
        width = 256 if part % 256 == 0 else 128
        for row in range(0, rows, high):
            for col in range(0, part, width):
                chunks.append((piece, row, high, part, col, width))
    return chunks


def layer_kernel(fsdp_size, chunks, *refs):
    pieces = 4
    count = len(chunks)
    column = fsdp_size // 2
    low, wide = jnp.bfloat16, jnp.float32
    length, scenes, cotangent = refs[:3]
    shards = refs[3:7]
    small = refs[7]
    fulls = refs[8:12]
    outs = refs[12:16]
    layer_out, input_grad, small_out = refs[16:19]
    rest = refs[19:]
    sum_b, one_b, two_b, zed_b, fin_b = (rest[i * count : (i + 1) * count] for i in range(5))
    rest = rest[5 * count :]
    other_b, core_b, big, small_full, hidden, hidden_t, qkv, attn, attn_t = rest[:9]
    resid, hidden_two_t, wide_low, slope, active_t, grad_low, grad_hidden, grad_resid = rest[9:17]
    small_g, small_a, small_b = rest[17:20]
    own_sem, az, bz, ax, bx, ay, by, ad, bd, ae, be, ac, bc, sv, rv = rest[20:35]
    (cs, cr, os_, or_, ts, tr, zs, zr, fs, fr, gs, gr, out_sem, ss, sr, us, ur) = rest[35:52]
    load_sem, credit = rest[52:]
    d = lax.axis_index("dp")
    f = lax.axis_index("fsdp")
    core = lax.rem(f, 2)
    place = lax.div(f, 2)
    bits = (lax.rem(d, 2), lax.div(d, 2))
    x_peer, y_peer, c_peer = (d ^ 1, f), (d ^ 2, f), (d, f ^ 1)
    peers = (x_peer, y_peer)
    seq_len = scenes.shape[0]
    ff = wide_low.shape[1]
    slots_other, slots_core = other_b.shape[0], core_b.shape[0]
    pending = []
    core_sends = {}

    def go(copy):
        copy.start()
        pending.append(copy)

    def arrived(view, send_sem, recv_sem, device):
        send(view, view, send_sem, recv_sem, device).wait_recv()

    def block(piece, place_from, quarter, half=None):
        rows = shards[piece].shape[0]
        span = shards[piece].shape[1] // 4
        row_part = aligned(place_from * 2 + core, rows)
        if half is None:
            return fulls[piece].at[row_part, aligned(quarter, span)]
        return fulls[piece].at[row_part, aligned(quarter * 2 + half, span // 2)]

    def to_partner(piece, view):
        send(view, view, ac.at[piece], bc.at[piece], c_peer).start()

    def source(k):
        return place ^ k

    def from_column(piece, k):
        at = (piece, k - 1)
        view = block(piece, source(k), d)
        arrived(view, az.at[at], bz.at[at], x_peer)
        go(send(view, view, ax.at[at], bx.at[at], x_peer))
        go(send(view, view, ay.at[at], by.at[at], y_peer))
        to_partner(piece, view)

    def from_sides(piece, k):
        at = (piece, k - 1)
        view = block(piece, source(k), d ^ 1)
        arrived(view, ax.at[at], bx.at[at], x_peer)
        part = block(piece, source(k), d ^ 1, 0)
        go(send(part, part, ad.at[at], bd.at[at], y_peer))
        to_partner(piece, view)
        view = block(piece, source(k), d ^ 2)
        arrived(view, ay.at[at], by.at[at], y_peer)
        part = block(piece, source(k), d ^ 2, 1)
        go(send(part, part, ae.at[at], be.at[at], x_peer))
        to_partner(piece, view)

    def from_corner(piece, k):
        at = (piece, k - 1)
        for half, (a, b, peer) in enumerate(((ad, bd, y_peer), (ae, be, x_peer))):
            part = block(piece, source(k), d ^ 3, half)
            arrived(part, a.at[at], b.at[at], peer)
            to_partner(piece, part)

    def from_partner(piece):
        rows = shards[piece].shape[0]
        view = fulls[piece].at[pl.ds(0, rows * column)]
        send(view, view, ac.at[piece], bc.at[piece], c_peer).wait()

    def loads(piece):
        if piece == 3:
            parts = [(fulls[3].at[pl.ds(n * D, D)], pl.ds(n * D, D)) for n in range(ff // D)]
        elif piece == 1:
            parts = [(fulls[1], pl.ds(3 * D, D))]
        else:
            parts = [
                (fulls[piece].at[:, pl.ds(n * D, D)], pl.ds(n * D, D))
                for n in range(fulls[piece].shape[1] // D)
            ]
        return [
            pltpu.make_async_copy(view, big.at[at], load_sem.at[piece, n])
            for n, (view, at) in enumerate(parts)
        ]

    def own_parts(piece, back):
        rows, span = shards[piece].shape
        first_row = sum(s.shape[0] * (s.shape[1] // D) for s in shards[:piece])
        parts = []
        for n in range(span // D):
            stage = big.at[pl.ds(first_row + n * rows, rows)]
            cols = pl.ds(n * D, D)
            whole = fulls[piece].at[aligned(f, rows), cols]
            ends = (stage, whole) if back else (shards[piece].at[:, cols], stage)
            parts.append(pltpu.make_async_copy(*ends, own_sem.at[int(back), piece, n]))
        return parts

    every = range(1, column)
    blocks = [(piece, k) for piece in range(pieces) for k in every]
    gather_order = []
    for n in range(len(blocks) + 4):
        for action, lag in ((from_column, 0), (from_sides, 1), (from_corner, 2)):
            if 0 <= n - lag < len(blocks):
                gather_order.append((action, *blocks[n - lag]))
    gathered = []

    def gather_step(limit=1):
        for _ in range(limit):
            if len(gathered) < len(gather_order):
                action, piece, k = gather_order[len(gathered)]
                gathered.append(1)
                action(piece, k)

    def gather_to(action, piece):
        last_one = gather_order.index((action, piece, column - 1))
        while len(gathered) <= last_one:
            gather_step()

    def slot_view(ref, slot, i):
        _, _, high, _, _, width = chunks[i]
        return ref.at[slot, :, pl.ds(0, column * high), pl.ds(0, width)]

    def grams(i, left_t, right):
        piece, row, high, part, col, width = chunks[i]
        slot = i % slots_other
        if i >= slots_other:
            core_sends[i - slots_other].wait_send()
        step = 2 if width == part and width == 128 else 1

        def fill(half, target):
            left = left_t[half, :, pl.ds(row, high), :].reshape(column * high, seq_len)

            def body(n, carry):
                start = pl.multiple_of(n * step * part + col, 128)
                found = jnp.dot(
                    left, right[:, pl.ds(start, step * width)], preferred_element_type=wide
                ).astype(low)
                for m in range(step):
                    target[n * step + m] = found[:, m * width : (m + 1) * width]
                return carry

            lax.fori_loop(0, 8 // step, body, 0)

        fill(1 - core, slot_view(other_b, slot, i))
        if i >= slots_core:
            pl.semaphore_wait(credit, 1)
        fill(core, sum_b[i])
        copy = send(
            slot_view(other_b, slot, i),
            slot_view(core_b, i % slots_core, i),
            cs.at[i],
            cr.at[i],
            c_peer,
        )
        copy.start()
        core_sends[i] = copy

    def add_into(target, other):
        rows = target.shape[0]
        strip = 64

        def body(n, carry):
            at = aligned(n, strip)
            target[at] = (target[at].astype(wide) + other[at].astype(wide)).astype(low)
            return carry

        lax.fori_loop(0, rows // strip, body, 0)

    def far_quarter(half, b):
        if half == 0:
            return (1 - bits[0]) + 2 * b
        return b + 2 * (1 - bits[1])

    def near_quarter(half, b):
        if half == 0:
            return bits[0] + 2 * b
        return b + 2 * bits[1]

    def pair(i):
        view = slot_view(core_b, i % slots_core, i)
        arrived(view, cs.at[i], cr.at[i], c_peer)

        def add(quarter, half):
            add_into(sum_b[i].at[quarter * 2 + half], view.at[quarter * 2 + half])

        for b in range(2):
            for half in range(2):
                add(far_quarter(half, b), half)
            for half in range(2):
                go(
                    send(
                        sum_b[i].at[far_quarter(half, b) * 2 + half],
                        one_b[i].at[half, b],
                        os_.at[i, half, b],
                        or_.at[i, half, b],
                        peers[half],
                    )
                )
        for b in range(2):
            for half in range(2):
                add(near_quarter(half, b), half)
        if i + slots_core < count:
            pl.semaphore_signal(credit, inc=1, device_id=c_peer, device_id_type=MESH_ID)

    def first(i):
        for half in range(2):
            for b in range(2):
                arrived(one_b[i].at[half, b], os_.at[i, half, b], or_.at[i, half, b], peers[half])
                add_into(sum_b[i].at[near_quarter(half, b) * 2 + half], one_b[i].at[half, b])
            other = d ^ 2 if half == 0 else d ^ 1
            go(
                send(
                    sum_b[i].at[other * 2 + half],
                    two_b[i].at[half],
                    ts.at[i, half],
                    tr.at[i, half],
                    peers[1 - half],
                )
            )

    def second(i):
        _, _, high, _, _, _ = chunks[i]
        for half in range(2):
            arrived(two_b[i].at[half], ts.at[i, half], tr.at[i, half], peers[1 - half])
            mine = sum_b[i].at[d * 2 + half]
            add_into(mine, two_b[i].at[half])
            for k in range(1, column):
                to = place ^ k
                go(
                    send(
                        mine.at[aligned(to, high)],
                        zed_b[i].at[half, k - 1],
                        zs.at[i, half, k - 1],
                        zr.at[i, half, k - 1],
                        (d, to * 2 + core),
                    )
                )

    def result(i, quarter, half):
        piece, row, high, part, col, width = chunks[i]
        start = pl.multiple_of((quarter * 2 + half) * part + col, 128)
        return outs[piece].at[pl.ds(row, high), pl.ds(start, width)]

    def last(i):
        _, _, high, _, _, _ = chunks[i]
        for half in range(2):
            for k in range(1, column):
                at = (i, half, k - 1)
                arrived(zed_b[i].at[half, k - 1], zs.at[at], zr.at[at], c_peer)
            total = sum_b[i][d * 2 + half, aligned(place, high)].astype(wide)
            for k in range(1, column):
                total = total + zed_b[i][half, k - 1].astype(wide)
            fin_b[i][half] = total.astype(low)
        for half in range(2):
            mine = result(i, d, half)
            pltpu.make_async_copy(fin_b[i].at[half], mine, out_sem.at[i, half]).start()
            for axis in range(2):
                at = (i, half, axis)
                go(send(fin_b[i].at[half], mine, fs.at[at], fr.at[at], peers[axis]))

    def spread(i):
        for half in range(2):
            for axis in range(2):
                at = (i, half, axis)
                view = result(i, d ^ (1 + axis), half)
                arrived(view, fs.at[at], fr.at[at], peers[axis])
                if half == axis:
                    go(send(view, view, gs.at[i, half], gr.at[i, half], peers[1 - axis]))

    def finish(i):
        for half in range(2):
            view = result(i, d ^ 3, half)
            arrived(view, gs.at[i, half], gr.at[i, half], peers[1 - half])
            pltpu.make_async_copy(fin_b[i].at[half], result(i, d, half), out_sem.at[i, half]).wait()

    stages = (first, second, last, spread, finish)
    order = []
    lags = (0, 2, 3, 4, 5)
    for step in range(count + lags[-1]):
        for stage, lag in zip(stages, lags):
            if 0 <= step - lag < count:
                order.append((stage, step - lag))
    done = []
    waiting = []
    paired = []

    def pair_up(keep=0):
        while len(waiting) > keep:
            i = waiting.pop(0)
            pair(i)
            paired.append(i)

    owed = [0]

    def advance(limit):
        steps, owed[0] = divmod(owed[0] + limit, 3)
        for _ in range(steps):
            if len(done) < len(order) and order[len(done)][1] in paired:
                stage, i = order[len(done)]
                done.append(1)
                stage(i)

    def pump(limit=1):
        pair_up()
        advance(limit)

    def produce(some, left_t, right, limit, keep=1):
        for i in some:
            pair_up(slots_core - 1)
            grams(i, left_t, right)
            waiting.append(i)
            pair_up(keep)
            advance(limit)

    by_piece = [[i for i in range(count) if chunks[i][0] == piece] for piece in range(pieces)]

    greet(d, f, fsdp_size)
    small_rows = small.shape[0]
    for k in range(1, fsdp_size):
        to = lax.rem(f + k, fsdp_size)
        go(send(small, small_full.at[aligned(f, small_rows)], sv.at[k - 1], rv.at[k - 1], (d, to)))
    own_small = pltpu.make_async_copy(
        small, small_full.at[aligned(f, small_rows)], own_sem.at[0, 0, pieces]
    )
    own_small.start()
    for piece in range(pieces):
        rows, span = shards[piece].shape
        for k in every:
            go(
                send(
                    shards[piece].at[:, aligned(d, span // 4)],
                    block(piece, place, d),
                    az.at[piece, k - 1],
                    bz.at[piece, k - 1],
                    (d, (place ^ k) * 2 + core),
                )
            )
        own = fulls[piece].at[aligned(f, rows)]
        send(shards[piece], own, ac.at[piece], bc.at[piece], c_peer).start()
        for copy in own_parts(piece, False):
            copy.start()
    for piece in range(pieces):
        for copy in own_parts(piece, False):
            copy.wait()
        for copy in own_parts(piece, True):
            copy.start()

    normed_one, _ = norm_rows(scenes[...].astype(wide))
    for k in range(1, fsdp_size):
        view = small_full.at[aligned(lax.rem(f - k + fsdp_size, fsdp_size), small_rows)]
        arrived(view, sv.at[k - 1], rv.at[k - 1], c_peer)
    own_small.wait()

    def vector(row):
        values = small_full[...].astype(wide)
        at = range(row, small_rows * fsdp_size, small_rows)
        return jnp.concatenate([values[n : n + 1] for n in at], axis=1)

    hidden[...] = (normed_one * vector(0) + vector(1)).astype(low)
    gather_step(2)
    transposed(hidden_t, hidden, fsdp_size)
    for piece in range(pieces):
        for copy in own_parts(piece, True):
            copy.wait()
    gather_to(from_corner, 0)
    gather_step(3)
    from_partner(0)
    for copy in loads(0):
        copy.start()
    gather_step(1)
    for copy in loads(0):
        copy.wait()

    def project(n, carry):
        cols = aligned(n, 512)
        rows = aligned(lax.div(n, D // 512), D)
        weight = big[rows, aligned(lax.rem(n, D // 512), 512)]
        qkv[:, cols] = jnp.dot(hidden[...], weight, preferred_element_type=wide).astype(low)
        return carry

    tiles = qkv.shape[1] // 512
    lax.fori_loop(0, tiles // 2, project, 0)
    gather_step(2)
    lax.fori_loop(tiles // 2, tiles, project, 0)
    gather_step(2)
    key_valid = lax.broadcasted_iota(jnp.int32, (1, seq_len), 1) < length[0]
    row_valid = lax.broadcasted_iota(jnp.int32, (seq_len, 1), 0) < length[0]
    first_half = lax.broadcasted_iota(jnp.int32, (1, 128), 1) < HEAD_DIM
    halves = (first_half.astype(wide).astype(low), 1 - first_half.astype(wide).astype(low))
    pairs = D // 128

    def attend(j, carry):
        queries, keys, values = (qkv[:, aligned(j + i * pairs, 128)] for i in range(3))
        found = []
        for half in halves:
            probs = head_scores(queries * half, keys, key_valid)
            found.append(jnp.dot(probs.astype(low), values, preferred_element_type=wide))
        attn[:, aligned(j, 128)] = jnp.where(first_half, found[0], found[1]).astype(low)
        return carry

    for j in range(0, pairs, 2):
        lax.fori_loop(j, j + 2, attend, 0)
        gather_step(2)
    transposed(attn_t, attn, fsdp_size)
    gather_to(from_corner, 1)
    gather_step(1)
    from_partner(1)
    for copy in loads(1):
        copy.start()
    for copy in loads(1):
        copy.wait()

    def second_in(n, carry):
        cols = aligned(n, 512)
        resid[:, cols] = scenes[:, cols].astype(wide) + jnp.dot(
            attn[...], big[pl.ds(3 * D, D), cols], preferred_element_type=wide
        )
        return carry

    lax.fori_loop(0, D // 512, second_in, 0)
    normed_two, _ = norm_rows(resid[...])
    hidden[...] = (normed_two * vector(2) + vector(3)).astype(low)
    transposed(hidden_two_t, hidden, fsdp_size)
    gather_to(from_corner, 2)
    gather_step(2)
    from_partner(2)
    for copy in loads(2):
        copy.start()
    span = D // 256

    def expand(n, carry):
        cols = aligned(n, 256)
        rows = aligned(lax.div(n, span), D)
        weight = big[rows, aligned(lax.rem(n, span), 256)]
        acts, grads = gelu_parts(jnp.dot(hidden[...], weight, preferred_element_type=wide))
        wide_low[:, cols] = acts.astype(low)
        slope[:, cols] = grads.astype(low)
        return carry

    for part, copy in enumerate(loads(2)):
        copy.wait()
        lax.fori_loop(part * span, (part + 1) * span, expand, 0)
        gather_step(2)
    transposed(active_t, wide_low, fsdp_size)
    grad_low[...] = jnp.where(row_valid, cotangent[...].astype(wide), 0.0).astype(low)
    early = by_piece[0][: slots_core - 1]
    produce(early, active_t, grad_low, 0, slots_core)
    gather_to(from_sides, pieces - 1)
    pair_up()
    gather_to(from_corner, pieces - 1)
    produce(by_piece[0][len(early) :][:1], active_t, grad_low, 0)
    from_partner(3)
    for copy in loads(3):
        copy.start()
    produce(by_piece[0][len(early) + 1 :], active_t, grad_low, 0)
    for part, copy in enumerate(loads(3)):
        copy.wait()
        at = pl.ds(part * D, D)
        term = jnp.dot(wide_low[:, at], big[at], preferred_element_type=wide)
        if part == 0:
            grad_hidden[...] = resid[...] + term
        else:
            grad_hidden[...] += term
        pair_up()
    layer_out[...] = jnp.where(row_valid, grad_hidden[...], 0.0).astype(low)
    pump(1)

    tile = 512

    def pre(n, carry):
        at = aligned(n, tile)
        back = outer_cols(grad_low[...], big[at])
        wide_low[:, at] = (back * slope[:, at].astype(wide)).astype(low)
        return carry

    for n in range(0, ff // tile, 2):
        lax.fori_loop(n, n + 2, pre, 0)
        pump(1)
    for copy in loads(2):
        copy.start()
    produce(by_piece[1], hidden_two_t, wide_low, 2)
    for part, copy in enumerate(loads(2)):
        copy.wait()
        back = outer_cols(wide_low[:, pl.ds(part * D, D)], big[pl.ds(part * D, D)])
        if part == 0:
            grad_hidden[...] = back
        else:
            grad_hidden[...] += back
        pump(1)
    for piece in (1, 0):
        for copy in loads(piece):
            copy.start()
    pump(1)

    def norm_step(values, grads, gain, base, row):
        normed, inverse = norm_rows(values)
        rows = D // fsdp_size
        for n, total in enumerate((grads * normed, grads)):
            sums = jnp.sum(total, axis=0, keepdims=True)
            for to in range(fsdp_size):
                small_g[to, row + n : row + n + 1, :] = sums[:, to * rows : (to + 1) * rows]
        return base + norm_back(grads * gain, normed, inverse)

    small_g[...] = jnp.zeros_like(small_g)
    base = jnp.where(row_valid, cotangent[...].astype(wide), 0.0)
    grad_resid[...] = norm_step(resid[...], grad_hidden[...], vector(2), base, 2)
    grad_low[...] = grad_resid[...].astype(low)
    pump(1)
    produce(by_piece[2], attn_t, grad_low, 2)
    for copy in loads(1):
        copy.wait()

    def attn_in(n, carry):
        rows = pl.ds(pl.multiple_of(3 * D + n * 256, 256), 256)
        attn[:, aligned(n, 256)] = outer_cols(grad_low[...], big[rows]).astype(low)
        return carry

    lax.fori_loop(0, D // 256, attn_in, 0)
    pump(1)
    factor = 1.0 / math.sqrt(HEAD_DIM)

    def attend_back(j, carry):
        queries, keys, values = (qkv[:, aligned(j + i * pairs, 128)] for i in range(3))
        grads = attn[:, aligned(j, 128)]
        found = []
        for half in halves:
            probs = head_scores(queries * half, keys, key_valid)
            grad_probs = outer_cols(grads * half, values)
            row_dot = jnp.sum(probs * grad_probs, axis=-1, keepdims=True)
            scores = (probs * (grad_probs - row_dot)).astype(low)
            found.append(
                (
                    jnp.dot(scores, keys, preferred_element_type=wide) * factor,
                    inner_rows(scores, queries) * factor,
                    inner_rows(probs.astype(low), grads),
                )
            )
        for i in range(3):
            wide_low[:, aligned(j + i * pairs, 128)] = jnp.where(
                first_half, found[0][i], found[1][i]
            ).astype(low)
        return carry

    for j in range(0, pairs, 2):
        lax.fori_loop(j, j + 2, attend_back, 0)
        pump(1)
    produce(by_piece[3], hidden_t, wide_low, 2)
    for part, copy in enumerate(loads(0)):
        copy.wait()
        total = outer_cols(wide_low[:, pl.ds(part * D, D)], big[pl.ds(part * D, D)])
        if part == 0:
            grad_hidden[...] = total
        else:
            grad_hidden[...] += total
    pump(1)
    total = norm_step(scenes[...].astype(wide), grad_hidden[...], vector(0), grad_resid[...], 0)
    input_grad[...] = total.astype(low)
    for k in range(1, fsdp_size):
        to = lax.rem(f + k, fsdp_size)
        go(send(small_g.at[to], small_a.at[k - 1], ss.at[k - 1], sr.at[k - 1], (d, to)))
    pump(2)
    total = small_g[f]
    for k in range(1, fsdp_size):
        arrived(small_a.at[k - 1], ss.at[k - 1], sr.at[k - 1], c_peer)
        total = total + small_a[k - 1]
    small_b[d] = total
    pump(2)
    for k in range(1, 4):
        go(send(small_b.at[d], small_b.at[d], us.at[k - 1], ur.at[k - 1], (d ^ k, f)))
    pump(4)
    for k in range(1, 4):
        arrived(small_b.at[d ^ k], us.at[k - 1], ur.at[k - 1], c_peer)
    small_out[...] = (small_b[0] + small_b[1]) + (small_b[2] + small_b[3])
    pump(3 * len(order))
    for copy in pending:
        copy.wait_send()
    for i in range(max(0, count - slots_other), count):
        core_sends[i].wait_send()


def layer_step(fsdp_size, length, scenes, cotangent, shards, small):
    column = fsdp_size // 2
    hops = column - 1
    seq_len = scenes.shape[0]
    ff = shards[3].shape[0] * fsdp_size
    low, wide = jnp.bfloat16, jnp.float32
    by_need = (shards[3], shards[2], shards[1], shards[0])
    chunks = chunk_list([w.shape for w in by_need])
    count = len(chunks)
    hbm = pl.BlockSpec(memory_space=pltpu.HBM)
    vmem = pl.BlockSpec(memory_space=pltpu.VMEM)
    smem = pl.BlockSpec(memory_space=pltpu.SMEM)
    dma = pltpu.SemaphoreType.DMA
    shape = jax.ShapeDtypeStruct
    scratch = []
    for kind in ("sum", "one", "two", "zed", "fin"):
        for _, _, high, _, _, width in chunks:
            buffers = {
                "sum": (8, column * high, width),
                "one": (2, 2, column * high, width),
                "two": (2, column * high, width),
                "zed": (2, hops, high, width),
                "fin": (2, high, width),
            }
            scratch.append(pltpu.VMEM(buffers[kind], low))
    tall = max(c[2] for c in chunks) * column
    broad = max(c[5] for c in chunks)
    rows = D // fsdp_size
    turned = pltpu.VMEM((2, column, rows, seq_len), low)
    scratch += [pltpu.VMEM((SLOTS, 8, tall, broad), low)] * 2
    scratch += [
        pltpu.VMEM((ff, D), low),
        pltpu.VMEM((small.shape[0] * fsdp_size, small.shape[1]), low),
        pltpu.VMEM((seq_len, D), low),
        turned,
        pltpu.VMEM((seq_len, 3 * D), low),
        pltpu.VMEM((seq_len, D), low),
        turned,
        pltpu.VMEM((seq_len, D), wide),
        turned,
        pltpu.VMEM((seq_len, ff), low),
        pltpu.VMEM((seq_len, ff), low),
        pltpu.VMEM((2, column, ff // fsdp_size, seq_len), low),
        pltpu.VMEM((seq_len, D), low),
        pltpu.VMEM((seq_len, D), wide),
        pltpu.VMEM((seq_len, D), wide),
        pltpu.VMEM((fsdp_size, 8, rows), wide),
        pltpu.VMEM((fsdp_size - 1, 8, rows), wide),
        pltpu.VMEM((4, 8, rows), wide),
    ]
    scratch += [dma((2, 4, 5))] + [dma((4, hops))] * 10 + [dma((4,))] * 2 + [dma((fsdp_size - 1,))] * 2
    scratch += [dma((count,))] * 2 + [dma((count, 2, 2))] * 2 + [dma((count, 2))] * 2
    scratch += [dma((count, 2, hops))] * 2 + [dma((count, 2, 2))] * 2 + [dma((count, 2))] * 2
    scratch += [dma((count, 2))] + [dma((fsdp_size - 1,))] * 2 + [dma((3,))] * 2
    scratch += [dma((4, 4)), pltpu.SemaphoreType.REGULAR]
    return pl.pallas_call(
        functools.partial(layer_kernel, fsdp_size, chunks),
        out_shape=[shape((a.shape[0] * fsdp_size, a.shape[1]), low) for a in shards]
        + [shape(w.shape, low) for w in by_need]
        + [shape((seq_len, D), low)] * 2
        + [shape((8, rows), wide)],
        in_specs=[smem, vmem, vmem] + [hbm] * 5,
        out_specs=[hbm] * 8 + [vmem] * 3,
        scratch_shapes=scratch,
        compiler_params=pltpu.CompilerParams(
            collective_id=0, has_side_effects=True, vmem_limit_bytes=67043328
        ),
        name="layer_step",
    )(length, scenes, cotangent, *shards, small)


def widen_kernel(parts, *refs):
    count = len(parts)
    small = refs[6]
    outs, small_outs = refs[7:13], refs[13:17]
    stages, wides = refs[17 : 17 + count], refs[17 + count : 17 + 2 * count]
    in_sem, out_sem = refs[17 + 2 * count :]
    copies = []
    for n, (which, at) in enumerate(parts):
        copies.append(pltpu.make_async_copy(refs[which].at[at], stages[n], in_sem.at[n]))
        copies[n].start()
    for row, out in enumerate(small_outs):
        out[...] = small[row]
    backs = []
    for n, (which, at) in enumerate(parts):
        copies[n].wait()
        source = stages[n]
        if outs[which].dtype != source.dtype:
            wides[n][...] = source[...].astype(jnp.float32)
            source = wides[n]
        backs.append(pltpu.make_async_copy(source, outs[which].at[at], out_sem.at[n]))
        backs[n].start()
    for copy in backs:
        copy.wait()


def widen(sums, rows, small):
    low, wide = jnp.bfloat16, jnp.float32
    parts, stages, wides = [], [], []
    for which, array in enumerate((*sums, *rows)):
        high, span = array.shape
        step = max(16, min(high, 1 << ((BLOCK // span).bit_length() - 1)))
        for row in range(0, high, step):
            parts.append((which, pl.ds(row, step)))
            stages.append(pltpu.VMEM((step, span), low))
            wides.append(pltpu.VMEM((step, span) if which < len(sums) else (8, 128), wide))
    shape = jax.ShapeDtypeStruct
    hbm = pl.BlockSpec(memory_space=pltpu.HBM)
    vmem = pl.BlockSpec(memory_space=pltpu.VMEM)
    dma = pltpu.SemaphoreType.DMA
    return pl.pallas_call(
        functools.partial(widen_kernel, parts),
        out_shape=[shape(a.shape, wide) for a in sums]
        + [shape(a.shape, low) for a in rows]
        + [shape((small.shape[1],), wide)] * 4,
        in_specs=[hbm] * 6 + [vmem],
        out_specs=[hbm] * 6 + [vmem] * 4,
        scratch_shapes=stages + wides + [dma((len(parts),))] * 2,
        compiler_params=pltpu.CompilerParams(vmem_limit_bytes=67043328),
        name="widen",
    )(*sums, *rows, small)


BLOCK = 131072


def on_device_wide(
    scenes_in,
    scene_lengths,
    cotangent,
    qkv_weight,
    out_weight,
    up_weight,
    down_weight,
    gain_one,
    bias_one,
    gain_two,
    bias_two,
):
    params = (
        lax.all_gather(qkv_weight, "fsdp", axis=0, tiled=True),
        lax.all_gather(out_weight, "fsdp", axis=0, tiled=True),
        lax.all_gather(up_weight, "fsdp", axis=0, tiled=True),
        lax.all_gather(down_weight, "fsdp", axis=0, tiled=True),
        lax.all_gather(gain_one, "fsdp", axis=0, tiled=True),
        lax.all_gather(bias_one, "fsdp", axis=0, tiled=True),
        lax.all_gather(gain_two, "fsdp", axis=0, tiled=True),
        lax.all_gather(bias_two, "fsdp", axis=0, tiled=True),
    )
    inputs = scenes_in[0].astype(jnp.float32)
    seq_len = inputs.shape[0]
    positions = jnp.arange(seq_len, dtype=jnp.int32)
    key_valid = positions < scene_lengths[0]
    row_mask = key_valid.astype(jnp.float32)[:, None]
    saved = forward_pass(inputs, key_valid, params)
    layer_out = (saved[0] * row_mask).astype(jnp.bfloat16)[None]
    grad_out = cotangent[0].astype(jnp.float32) * row_mask
    params_back = (
        lax.all_gather(qkv_weight, "fsdp", axis=0, tiled=True),
        lax.all_gather(out_weight, "fsdp", axis=0, tiled=True),
        lax.all_gather(up_weight, "fsdp", axis=0, tiled=True),
        lax.all_gather(down_weight, "fsdp", axis=0, tiled=True),
        lax.all_gather(gain_one, "fsdp", axis=0, tiled=True),
        lax.all_gather(bias_one, "fsdp", axis=0, tiled=True),
        lax.all_gather(gain_two, "fsdp", axis=0, tiled=True),
        lax.all_gather(bias_two, "fsdp", axis=0, tiled=True),
    )
    saved_back = forward_pass(inputs, key_valid, params_back)
    grad_resid, up_grad, down_grad, gain_two_grad, bias_two_grad = mlp_back(
        grad_out, saved_back, params_back
    )
    input_grad, qkv_grad, out_grad, gain_one_grad, bias_one_grad = attn_back(
        grad_resid, saved_back, params_back
    )
    shares = (
        lax.psum_scatter(qkv_grad, "fsdp", scatter_dimension=0, tiled=True),
        lax.psum_scatter(out_grad, "fsdp", scatter_dimension=0, tiled=True),
        lax.psum_scatter(up_grad, "fsdp", scatter_dimension=0, tiled=True),
        lax.psum_scatter(down_grad, "fsdp", scatter_dimension=0, tiled=True),
        lax.psum_scatter(gain_one_grad, "fsdp", scatter_dimension=0, tiled=True),
        lax.psum_scatter(bias_one_grad, "fsdp", scatter_dimension=0, tiled=True),
        lax.psum_scatter(gain_two_grad, "fsdp", scatter_dimension=0, tiled=True),
        lax.psum_scatter(bias_two_grad, "fsdp", scatter_dimension=0, tiled=True),
    )
    summed = (
        lax.psum(shares[0].astype(jnp.bfloat16), "dp").astype(jnp.float32),
        lax.psum(shares[1].astype(jnp.bfloat16), "dp").astype(jnp.float32),
        lax.psum(shares[2].astype(jnp.bfloat16), "dp").astype(jnp.float32),
        lax.psum(shares[3].astype(jnp.bfloat16), "dp").astype(jnp.float32),
        lax.psum(shares[4].astype(jnp.bfloat16), "dp").astype(jnp.float32),
        lax.psum(shares[5].astype(jnp.bfloat16), "dp").astype(jnp.float32),
        lax.psum(shares[6].astype(jnp.bfloat16), "dp").astype(jnp.float32),
        lax.psum(shares[7].astype(jnp.bfloat16), "dp").astype(jnp.float32),
    )
    qkv_total, out_total, up_total, down_total = (summed[0], summed[1], summed[2], summed[3])
    gain_one_total, bias_one_total, gain_two_total, bias_two_total = (
        summed[4],
        summed[5],
        summed[6],
        summed[7],
    )
    input_out = input_grad.astype(jnp.bfloat16)[None]
    return (
        layer_out,
        input_out,
        qkv_total,
        out_total,
        up_total,
        down_total,
        gain_one_total,
        bias_one_total,
        gain_two_total,
        bias_two_total,
    )


def on_device(
    scenes_in,
    scene_lengths,
    cotangent,
    qkv_weight,
    out_weight,
    up_weight,
    down_weight,
    gain_one,
    bias_one,
    gain_two,
    bias_two,
):
    rows = gain_one.shape[0]
    fsdp_size = D // rows
    small = jnp.stack([gain_one, bias_one, gain_two, bias_two])
    small = jnp.pad(small, ((0, 12), (0, 0)))
    results = layer_step(
        fsdp_size,
        scene_lengths,
        scenes_in[0],
        cotangent[0],
        (qkv_weight, out_weight, up_weight, down_weight),
        small,
    )
    down_sum, up_sum, out_sum, qkv_sum, layer_out, input_grad, small_sum = results[4:]
    wide = widen((qkv_sum, out_sum, up_sum, down_sum), (layer_out, input_grad), small_sum)
    return (wide[4][None], wide[5][None], *wide[:4], *wide[6:])


def solution(mesh):
    placed = (
        P(("dp", "fsdp"), None, None),
        P(("dp", "fsdp")),
        P(("dp", "fsdp"), None, None),
        P("fsdp", None),
        P("fsdp", None),
        P("fsdp", None),
        P("fsdp", None),
        P("fsdp"),
        P("fsdp"),
        P("fsdp"),
        P("fsdp"),
    )
    body = on_device if mesh.shape["dp"] == 4 and mesh.shape["fsdp"] == 8 else on_device_wide
    return jax.shard_map(
        body,
        mesh=mesh,
        in_specs=placed,
        out_specs=(
            P(("dp", "fsdp"), None, None),
            P(("dp", "fsdp"), None, None),
            P("fsdp", None),
            P("fsdp", None),
            P("fsdp", None),
            P("fsdp", None),
            P("fsdp"),
            P("fsdp"),
            P("fsdp"),
            P("fsdp"),
        ),
        check_vma=False,
    )
```
